512 devices in a mesh: gy: 16 (over x_lo, z), gx: 32 (over x_hi, y, core).
Axes of the slice: x: 4 (x_hi: 2, x_lo: 2; x = x_hi * 2 + x_lo), y: 8, z: 8, core: 2. Of those that a mesh axis runs over, the one named last changes fastest.
Arguments:
- field: bfloat16 [1024, 512, 128], P('gy', 'gx'), may hold values from -8 to 8
- cotangent: bfloat16 [512, 256, 256], P('gy', 'gx'), may hold values from -6 to 6
- gain_fine: float32 [128], replicated, may hold values from 0.1 to 1.9
- weight_fine: bfloat16 [3, 3, 128, 128], replicated, may hold values from -0.1875 to 0.1875
- projection: bfloat16 [128, 256], replicated, may hold values from -0.5 to 0.5
- gain_coarse: float32 [256], replicated, may hold values from 0.1 to 1.9
- weight_coarse: bfloat16 [3, 3, 256, 256], replicated, may hold values from -0.125 to 0.125
Outputs:
- coarse_output: bfloat16 [512, 256, 256], P('gy', 'gx')
- field_grad: bfloat16 [1024, 512, 128], P('gy', 'gx')
- fine_weight_grad: float32 [3, 3, 128, 128], replicated
- fine_gain_grad: float32 [128], replicated
- projection_grad: float32 [128, 256], replicated
- coarse_weight_grad: float32 [3, 3, 256, 256], replicated
- coarse_gain_grad: float32 [256], replicated
The draws below stay inside these ranges and needn't reach their ends.
All inputs are finite; a program needn't handle non-finite values.
Results may differ from the reference program's by a relative error of at most 0.014.
Values may be sent and summed in bfloat16 or wider, within the bound.
No kernel may reach another device: no remote copies, remote signals or barrier semaphores. Data moves between devices by JAX's collectives and lax.ppermute only.
A program may use at most 64 MiB of HBM per device.

```python
import jax
import jax.numpy as jnp
from jax import lax

C1 = 128
C2 = 256
GROUPS = 32
ROWS = 1024
COLS = 512


def draw_field(key, part):
    base_key = jax.random.fold_in(key, 11)
    noise_key, chan_key = jax.random.split(base_key, 2)
    noise = jax.random.normal(noise_key, (ROWS, COLS, C1), jnp.float32)
    row_pos = jnp.arange(ROWS, dtype=jnp.float32) / ROWS
    col_pos = jnp.arange(COLS, dtype=jnp.float32) / COLS
    ramp = jnp.exp(jnp.log(3.0) * 0.5 * (row_pos[:, None] + col_pos[None, :]))
    chan_scale = jnp.exp(jax.random.uniform(chan_key, (C1,), jnp.float32, -1.0, 1.0) * jnp.log(2.0))
    values = noise * ramp[:, :, None] * chan_scale[None, None, :] * 0.6
    return jnp.clip(values, -8.0, 8.0).astype(jnp.bfloat16)


def level_of(own_key, extent, cuts, smallest, high):
    level = 1.0
    for position, shards_of in cuts:
        draws = jax.random.uniform(jax.random.fold_in(jax.random.fold_in(own_key, 6), position), (shards_of,), jnp.float32, smallest / len(cuts), high / len(cuts))
        level = level * jnp.repeat(jnp.exp(draws), extent[position] // shards_of).reshape((-1,) + (1,) * (len(extent) - 1 - position))
    return level


def scatter_about(rng, shape, deviation, most, cuts=(), kind=jnp.bfloat16):
    values = jax.random.normal(rng, shape, jnp.float32) * deviation
    if len(cuts) > 0:
        values = level_of(rng, shape, cuts, -0.22, 0.18) * values
    return jnp.clip(values, min=-most, max=most).astype(kind)


def setup_inputs(seed: int = 0) -> dict:
    splits = jax.random.split(jax.random.key(seed), 8)
    return {
        "field": draw_field(jax.random.fold_in(splits[7], 71), 0),
        "cotangent": scatter_about(splits[1], (ROWS // 2, COLS // 2, C2), 1.0, 6.0, ((0, 16), (1, 32))),
        "gain_fine": jnp.clip(1.0 + 0.18 * jax.random.normal(splits[2], (C1,), jnp.float32), 0.1, 1.9),
        "weight_fine": scatter_about(splits[3], (3, 3, C1, C1), (9 * C1) ** -0.5, 0.1875),
        "projection": scatter_about(splits[4], (C1, C2), C1 ** -0.5, 0.5),
        "gain_coarse": jnp.clip(1.0 + 0.18 * jax.random.normal(splits[5], (C2,), jnp.float32), 0.1, 1.9),
        "weight_coarse": scatter_about(splits[6], (3, 3, C2, C2), (9 * C2) ** -0.5, 0.125),
    }


EPSILON = 1e-05

def conv_forward(padded, weight, height, width):
    channels = padded.shape[2]
    total = jnp.zeros((height * width, weight.shape[3]), jnp.float32)
    for row_tap in range(3):
        for col_tap in range(3):
            window = padded[row_tap:row_tap + height, col_tap:col_tap + width].reshape(height * width, channels)
            total = total + jnp.dot(window, weight[row_tap, col_tap], preferred_element_type=jnp.float32)
    return total.reshape(height, width, weight.shape[3])

def conv_transpose(padded, weight, height, width):
    channels = padded.shape[2]
    total = jnp.zeros((height * width, weight.shape[2]), jnp.float32)
    for row_tap in range(3):
        for col_tap in range(3):
            window = padded[2 - row_tap:2 - row_tap + height, 2 - col_tap:2 - col_tap + width].reshape(height * width, channels)
            total = total + jnp.dot(window, weight[row_tap, col_tap].T, preferred_element_type=jnp.float32)
    return total.reshape(height, width, weight.shape[2])

def conv_weight(padded, grads, height, width):
    channels = padded.shape[2]
    flat_grads = grads.reshape(height * width, grads.shape[2])
    taps = []
    for row_tap in range(3):
        for col_tap in range(3):
            window = padded[row_tap:row_tap + height, col_tap:col_tap + width].reshape(height * width, channels)
            taps.append(lax.dot_general(window, flat_grads, (((0,), (0,)), ((), ())), preferred_element_type=jnp.float32))
    return jnp.stack(taps).reshape(3, 3, channels, grads.shape[2])

def pad_zero(values):
    return jnp.pad(values, ((1, 1), (1, 1), (0, 0)))

def normalize(values):
    channels = values.shape[2]
    grouped = values.reshape(-1, GROUPS, channels // GROUPS)
    count = grouped.shape[0] * grouped.shape[2]
    average = lax.optimization_barrier(jnp.sum(grouped, axis=(0, 2))) / count
    variance = lax.optimization_barrier(jnp.sum(grouped * grouped, axis=(0, 2))) / count - average * average
    inverse = lax.rsqrt(variance + EPSILON)
    normed = (grouped - average[None, :, None]) * inverse[None, :, None]
    return (normed.reshape(values.shape), inverse)

def norm_backward(dnorm, normed, inverse):
    channels = normed.shape[2]
    dgroup = dnorm.reshape(-1, GROUPS, channels // GROUPS)
    ngroup = normed.reshape(-1, GROUPS, channels // GROUPS)
    count = dgroup.shape[0] * dgroup.shape[2]
    first = lax.optimization_barrier(jnp.sum(dgroup, axis=(0, 2))) / count
    second = lax.optimization_barrier(jnp.sum(dgroup * ngroup, axis=(0, 2))) / count
    result = inverse[None, :, None] * (dgroup - first[None, :, None] - ngroup * second[None, :, None])
    return result.reshape(normed.shape)

def silu_slope(act):
    sigma = jax.nn.sigmoid(act)
    return sigma * (1.0 + act * (1.0 - sigma))

def reference(field, cotangent, gain_fine, weight_fine, projection, gain_coarse, weight_coarse):
    height, width, chan_fine = field.shape
    chan_coarse = projection.shape[1]
    half_h, half_w = (height // 2, width // 2)
    values = field.astype(jnp.float32)
    normed_fine, inverse_fine = normalize(values)
    act_fine = normed_fine * gain_fine
    hidden_fine = jax.nn.silu(act_fine).astype(jnp.bfloat16)
    padded_fine = pad_zero(hidden_fine)
    block_fine = (values + conv_forward(padded_fine, weight_fine, height, width)).astype(jnp.bfloat16)
    pooled = lax.optimization_barrier(jnp.mean(block_fine.astype(jnp.float32).reshape(half_h, 2, half_w, 2, chan_fine), axis=(1, 3))).astype(jnp.bfloat16)
    coarse_in = jnp.dot(pooled.reshape(-1, chan_fine), projection, preferred_element_type=jnp.float32).reshape(half_h, half_w, chan_coarse).astype(jnp.bfloat16)
    coarse_vals = coarse_in.astype(jnp.float32)
    normed_coarse, inverse_coarse = normalize(coarse_vals)
    act_coarse = normed_coarse * gain_coarse
    hidden_coarse = jax.nn.silu(act_coarse).astype(jnp.bfloat16)
    padded_coarse = pad_zero(hidden_coarse)
    coarse_output = (coarse_vals + conv_forward(padded_coarse, weight_coarse, half_h, half_w)).astype(jnp.bfloat16)
    coarse_weight_grad = conv_weight(padded_coarse, cotangent, half_h, half_w)
    dact_coarse = conv_transpose(pad_zero(cotangent), weight_coarse, half_h, half_w) * silu_slope(act_coarse)
    coarse_gain_grad = lax.optimization_barrier(jnp.sum((dact_coarse * normed_coarse).reshape(-1, chan_coarse), axis=0))
    dcoarse = (cotangent.astype(jnp.float32) + norm_backward(dact_coarse * gain_coarse, normed_coarse, inverse_coarse)).astype(jnp.bfloat16)
    projection_grad = lax.dot_general(pooled.reshape(-1, chan_fine), dcoarse.reshape(-1, chan_coarse), (((0,), (0,)), ((), ())), preferred_element_type=jnp.float32)
    dpool = jnp.dot(dcoarse.reshape(-1, chan_coarse), projection.T, preferred_element_type=jnp.float32).reshape(half_h, half_w, chan_fine)
    dblock = (jnp.broadcast_to(dpool[:, None, :, None, :], (half_h, 2, half_w, 2, chan_fine)).reshape(height, width, chan_fine) * 0.25).astype(jnp.bfloat16)
    fine_weight_grad = conv_weight(padded_fine, dblock, height, width)
    dact_fine = conv_transpose(pad_zero(dblock), weight_fine, height, width) * silu_slope(act_fine)
    fine_gain_grad = lax.optimization_barrier(jnp.sum((dact_fine * normed_fine).reshape(-1, chan_fine), axis=0))
    field_grad = (dblock.astype(jnp.float32) + norm_backward(dact_fine * gain_fine, normed_fine, inverse_fine)).astype(jnp.bfloat16)
    return (coarse_output, field_grad, fine_weight_grad, fine_gain_grad, projection_grad, coarse_weight_grad, coarse_gain_grad)
```

```python
import jax
import jax.numpy as jnp
from jax import lax
from jax.sharding import Mesh
from jax.sharding import PartitionSpec as P

GROUPS = 32
GY = ("gy_0", "gy_1")
GX = ("gx_0", "gx_1", "gx_2")
GY_GX = GY + GX
NEAR = ("gx_1", "gx_2")
FAR = ("gx_0", "gy_0", "gy_1")
STAGES = (("gx_2",), ("gx_0", "gy_0"), ("gx_1", "gy_1"))
LANES = 128
EPSILON = 1e-05


def exchanged(parts, axis):
    count = lax.axis_size(axis)
    up = [(i, i + 1) for i in range(count - 1)]
    down = [(i + 1, i) for i in range(count - 1)]
    heads = jnp.concatenate([head.reshape(-1, LANES) for head, _ in parts])
    tails = jnp.concatenate([tail.reshape(-1, LANES) for _, tail in parts])
    before = lax.ppermute(tails, axis, up)
    after = lax.ppermute(heads, axis, down)
    result, at = [], 0
    for head, _ in parts:
        rows = head.size // LANES
        result.append(
            (before[at : at + rows].reshape(head.shape), after[at : at + rows].reshape(head.shape))
        )
        at += rows
    return result


def with_rims(fine, coarse, wide, narrow):
    (f0, f1), (c0, c1) = exchanged(
        ((fine[:wide], fine[-wide:]), (coarse[:narrow], coarse[-narrow:])), GY
    )
    fine = jnp.concatenate([f0, fine, f1])
    coarse = jnp.concatenate([c0, coarse, c1])
    (f0, f1), (c0, c1) = exchanged(
        ((fine[:, :wide], fine[:, -wide:]), (coarse[:, :narrow], coarse[:, -narrow:])), GX
    )
    return jnp.concatenate([f0, fine, f1], axis=1), jnp.concatenate([c0, coarse, c1], axis=1)


def total(values):
    for axes in (NEAR, FAR):
        count = lax.axis_size(axes)
        copies = jnp.broadcast_to(values[None], (count,) + values.shape)
        values = jnp.sum(lax.all_to_all(copies, axes, 0, 0, tiled=True), axis=0)
    return values


def group_totals(first, second):
    pair = jnp.concatenate(
        [
            jnp.sum(first.reshape(GROUPS, -1), axis=1),
            jnp.sum(second.reshape(GROUPS, -1), axis=1),
            jnp.zeros((LANES - 2 * GROUPS,), jnp.float32),
        ]
    )
    sums = total(pair[None])[0]
    return sums[:GROUPS], sums[GROUPS : 2 * GROUPS]


def gradient_totals(rows):
    part = rows.astype(jnp.bfloat16)
    for axes in STAGES:
        count = lax.axis_size(axes)
        pieces = lax.all_to_all(
            part.reshape(count, -1, LANES), axes, 0, 0, tiled=True
        )
        part = jnp.sum(pieces.astype(jnp.float32), axis=0).astype(jnp.bfloat16)
    for axes in STAGES[::-1]:
        count = lax.axis_size(axes)
        copies = jnp.broadcast_to(part[None], (count,) + part.shape)
        part = lax.all_to_all(copies, axes, 0, 0, tiled=True).reshape(-1, LANES)
    return part


def conv_forward(padded, weight, height, width):
    channels = padded.shape[2]
    total = jnp.zeros((height * width, weight.shape[3]), jnp.float32)
    for row_tap in range(3):
        for col_tap in range(3):
            window = padded[row_tap : row_tap + height, col_tap : col_tap + width].reshape(
                height * width, channels
            )
            total = total + jnp.dot(
                window, weight[row_tap, col_tap], preferred_element_type=jnp.float32
            )
    return total.reshape(height, width, weight.shape[3])


def conv_transpose(padded, weight, height, width):
    channels = padded.shape[2]
    total = jnp.zeros((height * width, weight.shape[2]), jnp.float32)
    for row_tap in range(3):
        for col_tap in range(3):
            window = padded[
                2 - row_tap : 2 - row_tap + height, 2 - col_tap : 2 - col_tap + width
            ].reshape(height * width, channels)
            total = total + jnp.dot(
                window, weight[row_tap, col_tap].T, preferred_element_type=jnp.float32
            )
    return total.reshape(height, width, weight.shape[2])


def conv_weight(padded, grads, height, width):
    channels = padded.shape[2]
    flat_grads = grads.reshape(height * width, grads.shape[2])
    taps = []
    for row_tap in range(3):
        for col_tap in range(3):
            window = padded[row_tap : row_tap + height, col_tap : col_tap + width].reshape(
                height * width, channels
            )
            taps.append(
                lax.dot_general(
                    window, flat_grads, (((0,), (0,)), ((), ())), preferred_element_type=jnp.float32
                )
            )
    return jnp.stack(taps).reshape(9 * channels, grads.shape[2])


def inside(height, width, rim):
    row = lax.broadcasted_iota(jnp.int32, (height + 2 * rim, width + 2 * rim, 1), 0)
    col = lax.broadcasted_iota(jnp.int32, (height + 2 * rim, width + 2 * rim, 1), 1)
    row = row - rim + lax.axis_index(GY) * height
    col = col - rim + lax.axis_index(GX) * width
    rows, cols = height * lax.axis_size(GY), width * lax.axis_size(GX)
    return (row >= 0) & (row < rows) & (col >= 0) & (col < cols)


def upsample(values):
    rows, cols, channels = values.shape
    return jnp.broadcast_to(values[:, None, :, None, :], (rows, 2, cols, 2, channels)).reshape(
        2 * rows, 2 * cols, channels
    )


def per_channel(values, channels):
    return jnp.repeat(values, channels // GROUPS)


def silu_slope(act):
    sigma = jax.nn.sigmoid(act)
    return sigma * (1.0 + act * (1.0 - sigma))


def moments(first, second, count, channels):
    average = first / count
    inverse = lax.rsqrt(second / count - average * average + EPSILON)
    return per_channel(average, channels), per_channel(inverse, channels)


def on_device(field, cotangent, gain_fine, weight_fine, projection, gain_coarse, weight_coarse):
    height, width, chan_fine = field.shape
    chan_coarse = projection.shape[1]
    half_h, half_w = (height // 2, width // 2)
    cells_all = height * width * lax.axis_size(GY_GX)
    fine_count = cells_all * (chan_fine // GROUPS)
    coarse_count = cells_all // 4 * (chan_coarse // GROUPS)

    values = field.astype(jnp.float32)
    first, second = group_totals(
        jnp.sum(values, axis=(0, 1)), jnp.sum(values * values, axis=(0, 1))
    )
    wide_field, wide_grad = with_rims(field, cotangent, 3, 2)

    mean_fine, inverse_fine = moments(first, second, fine_count, chan_fine)
    wide_values = wide_field.astype(jnp.float32)
    wide_act = (wide_values - mean_fine) * inverse_fine * gain_fine
    hidden_fine = jnp.where(inside(height, width, 3), jax.nn.silu(wide_act), 0.0).astype(
        jnp.bfloat16
    )
    block_fine = (
        wide_values[1:-1, 1:-1] + conv_forward(hidden_fine, weight_fine, height + 4, width + 4)
    ).astype(jnp.bfloat16)
    pooled = jnp.mean(
        block_fine.astype(jnp.float32).reshape(half_h + 2, 2, half_w + 2, 2, chan_fine),
        axis=(1, 3),
    ).astype(jnp.bfloat16)
    coarse_in = (
        jnp.dot(pooled.reshape(-1, chan_fine), projection, preferred_element_type=jnp.float32)
        .reshape(half_h + 2, half_w + 2, chan_coarse)
        .astype(jnp.bfloat16)
    )
    wide_coarse = coarse_in.astype(jnp.float32)
    coarse_vals = wide_coarse[1:-1, 1:-1]
    first, second = group_totals(
        jnp.sum(coarse_vals, axis=(0, 1)), jnp.sum(coarse_vals * coarse_vals, axis=(0, 1))
    )

    mean_coarse, inverse_coarse = moments(first, second, coarse_count, chan_coarse)
    in_coarse = inside(half_h, half_w, 1)
    normed_coarse = (wide_coarse - mean_coarse) * inverse_coarse
    act_coarse = normed_coarse * gain_coarse
    hidden_coarse = jnp.where(in_coarse, jax.nn.silu(act_coarse), 0.0).astype(jnp.bfloat16)
    coarse_output = (
        coarse_vals + conv_forward(hidden_coarse, weight_coarse, half_h, half_w)
    ).astype(jnp.bfloat16)
    dact_coarse = conv_transpose(
        wide_grad, weight_coarse, half_h + 2, half_w + 2
    ) * silu_slope(act_coarse)
    dnorm = dact_coarse * gain_coarse
    own = (slice(1, -1), slice(1, -1))
    coarse_gain_grad = jnp.sum(dact_coarse[own] * normed_coarse[own], axis=(0, 1))
    first, second = group_totals(
        jnp.sum(dnorm[own], axis=(0, 1)), coarse_gain_grad * gain_coarse
    )
    coarse_weight_grad = conv_weight(hidden_coarse, cotangent, half_h, half_w)
    dcoarse = wide_grad[1:-1, 1:-1].astype(jnp.float32) + inverse_coarse * (
        dnorm
        - per_channel(first / coarse_count, chan_coarse)
        - normed_coarse * per_channel(second / coarse_count, chan_coarse)
    )
    dcoarse = jnp.where(in_coarse, dcoarse, 0.0).astype(jnp.bfloat16)
    projection_grad = lax.dot_general(
        pooled[own].reshape(-1, chan_fine),
        dcoarse[own].reshape(-1, chan_coarse),
        (((0,), (0,)), ((), ())),
        preferred_element_type=jnp.float32,
    )
    small_dblock = (
        jnp.dot(
            dcoarse.reshape(-1, chan_coarse), projection.T, preferred_element_type=jnp.float32
        ).reshape(half_h + 2, half_w + 2, chan_fine)
        * 0.25
    ).astype(jnp.bfloat16)
    wide_dblock = upsample(small_dblock)[1:-1, 1:-1]
    dblock = wide_dblock[1:-1, 1:-1]

    hidden_own = hidden_fine[2:-2, 2:-2]
    fine_weight_grad = conv_weight(hidden_own, dblock, height, width)
    normed_fine = (values - mean_fine) * inverse_fine
    act_fine = normed_fine * gain_fine
    dact_fine = conv_transpose(wide_dblock, weight_fine, height, width) * silu_slope(act_fine)
    dnorm = dact_fine * gain_fine
    fine_gain_grad = jnp.sum(dact_fine * normed_fine, axis=(0, 1))
    first = jnp.sum(jnp.sum(dnorm, axis=(0, 1)).reshape(GROUPS, -1), axis=1)
    second = jnp.sum((fine_gain_grad * gain_fine).reshape(GROUPS, -1), axis=1)
    small = jnp.concatenate(
        [
            fine_gain_grad,
            coarse_gain_grad,
            first,
            second,
            jnp.zeros((LANES - 2 * GROUPS,), jnp.float32),
        ]
    )
    sums = total(small.reshape(-1, LANES)).reshape(-1)
    fine_gain_grad, coarse_gain_grad, first, second = jnp.split(
        sums[: chan_fine + chan_coarse + 2 * GROUPS],
        [chan_fine, chan_fine + chan_coarse, chan_fine + chan_coarse + GROUPS],
    )
    field_grad = (
        dblock.astype(jnp.float32)
        + inverse_fine
        * (
            dnorm
            - per_channel(first / fine_count, chan_fine)
            - normed_fine * per_channel(second / fine_count, chan_fine)
        )
    ).astype(jnp.bfloat16)

    tall = 9 * chan_coarse
    rows = [
        coarse_weight_grad[:, :LANES],
        coarse_weight_grad[:, LANES:],
        fine_weight_grad,
        projection_grad[:, :LANES],
        projection_grad[:, LANES:],
    ]
    used = sum(r.shape[0] for r in rows)
    devices = lax.axis_size(GY_GX)
    spare = -used % (4 * devices)
    grads = gradient_totals(
        jnp.concatenate(
            [r.astype(jnp.bfloat16) for r in rows] + [jnp.zeros((spare, LANES), jnp.bfloat16)]
        )
    ).astype(jnp.float32)
    at, pieces = 0, []
    for r in rows:
        pieces.append(grads[at : at + r.shape[0]])
        at += r.shape[0]
    return (
        coarse_output,
        field_grad,
        pieces[2].reshape(weight_fine.shape),
        fine_gain_grad,
        jnp.concatenate(pieces[3:], axis=1),
        jnp.concatenate(pieces[:2], axis=1).reshape(weight_coarse.shape),
        coarse_gain_grad,
    )


def solution(mesh):
    finer = Mesh(mesh.devices.reshape(2, 8, 2, 8, 2), GY_GX)
    in_specs = (P(GY, GX, None), P(GY, GX, None), P(), P(), P(), P(), P())
    out_specs = (P(GY, GX, None), P(GY, GX, None), P(), P(), P(), P(), P())
    return jax.shard_map(
        on_device, mesh=finer, in_specs=in_specs, out_specs=out_specs, check_vma=False
    )
```

```python
import functools

import jax
import jax.numpy as jnp
from jax import lax
from jax.experimental import pallas as pl
from jax.experimental.pallas import tpu as pltpu
from jax.sharding import Mesh
from jax.sharding import PartitionSpec as P

GROUPS = 32
GY = ("gy_0", "gy_1")
GX = ("gx_0", "gx_1", "gx_2")
GY_GX = GY + GX
NEAR = ("gx_1", "gx_2")
FAR = ("gx_0", "gy_0", "gy_1")
STAGES = (("gx_2",), ("gx_0", "gy_0"), ("gx_1", "gy_1"))
LANES = 128
EPSILON = 1e-05

PITCH = 32
FINE_RIM = 3
COARSE_RIM = 2


def exchanged(parts, axis):
    count = lax.axis_size(axis)
    up = [(i, i + 1) for i in range(count - 1)]
    down = [(i + 1, i) for i in range(count - 1)]
    heads = jnp.concatenate([head.reshape(-1, LANES) for head, _ in parts])
    tails = jnp.concatenate([tail.reshape(-1, LANES) for _, tail in parts])
    before = lax.ppermute(tails, axis, up)
    after = lax.ppermute(heads, axis, down)
    result, at = [], 0
    for head, _ in parts:
        rows = head.size // LANES
        result.append(
            (before[at : at + rows].reshape(head.shape), after[at : at + rows].reshape(head.shape))
        )
        at += rows
    return result


def ring(own, left, right, pitch):
    rows, cols, channels = own.shape
    gap = pitch - cols - left.shape[1] - right.shape[1]
    return jnp.concatenate([own, right, jnp.zeros((rows, gap, channels), own.dtype), left], axis=1)


def with_rims(fine, coarse, wide, narrow):
    (f0, f1), (c0, c1) = exchanged(
        ((fine[:wide], fine[-wide:]), (coarse[:narrow], coarse[-narrow:])), GY
    )
    fine = jnp.concatenate([f0, fine, f1])
    coarse = jnp.concatenate([c0, coarse, c1])
    (f0, f1), (c0, c1) = exchanged(
        ((fine[:, :wide], fine[:, -wide:]), (coarse[:, :narrow], coarse[:, -narrow:])), GX
    )
    return ring(fine, f0, f1, PITCH), ring(coarse, c0, c1, PITCH // 2)


def call(body, outs, *args, scratch=()):
    spaces = [
        pl.BlockSpec(memory_space=pltpu.SMEM if a.dtype == jnp.int32 else pltpu.VMEM) for a in args
    ]
    return pl.pallas_call(
        body,
        out_shape=[jax.ShapeDtypeStruct(shape, dtype) for shape, dtype in outs],
        in_specs=spaces,
        out_specs=[pl.BlockSpec(memory_space=pltpu.VMEM) for _ in outs],
        scratch_shapes=[pltpu.VMEM(shape, dtype) for shape, dtype in scratch],
    )(*args)


def group_sum(values, size):
    lanes = values.shape[1]
    lane = lax.broadcasted_iota(jnp.int32, values.shape, 1)
    step = 1
    while step < size:
        after = pltpu.roll(values, lanes - step, 1)
        before = pltpu.roll(values, step, 1)
        values = values + jnp.where((lane & step) == 0, after, before)
        step *= 2
    return values


def wide(row):
    return jnp.broadcast_to(row, (8, row.shape[1]))


def moments(first, second, count, size):
    average = group_sum(wide(first), size) / count
    square = group_sum(wide(second), size) / count
    return average, lax.rsqrt(square - average * average + EPSILON)


def sigmoid(act):
    return 1.0 / (1.0 + jnp.exp(-act))


def in_grid(shape, first_row, first_col, rim, rows, cols):
    row = lax.broadcasted_iota(jnp.int32, shape, 0) + first_row
    place = lax.broadcasted_iota(jnp.int32, shape, 1)
    col = jnp.where(place < shape[1] - rim, place, place - shape[1]) + first_col
    return (row >= 0) & (row < rows) & (col >= 0) & (col < cols)


def over_cells(values):
    lanes = values.shape[-1]
    return jnp.sum(jnp.sum(values.reshape(-1, 8, lanes), axis=0), axis=0, keepdims=True)


def spread(copies, rows):
    for k, row in enumerate(rows):
        copies[:, k, :] = jnp.broadcast_to(row, (copies.shape[0], LANES))


def field_sums(field, copies):
    first = jnp.zeros((8, LANES), jnp.float32)
    second = jnp.zeros((8, LANES), jnp.float32)
    for at in range(0, field.shape[0], 8):
        v = field[at : at + 8].astype(jnp.float32).reshape(-1, 8, LANES)
        first = first + jnp.sum(v, axis=0)
        second = second + jnp.sum(v * v, axis=0)
    spread(
        copies, [jnp.sum(first, axis=0, keepdims=True), jnp.sum(second, axis=0, keepdims=True)]
    )


def relay(received, copies):
    sums = jnp.sum(received[...], axis=0)
    for k in range(copies.shape[1]):
        copies[:, k, :] = jnp.broadcast_to(sums[k : k + 1], (copies.shape[0], LANES))


def fine_forward(count, rows, cols, place, x, sums, gain, weight, projection,
                 hidden, pooled, coarse, copies, stats, block):
    tot = jnp.sum(sums[...], axis=0)
    average, inverse = moments(tot[0:1], tot[1:2], count, LANES // GROUPS)
    stats[0] = average
    stats[1] = inverse
    average, scale = average[0:1], inverse[0:1] * gain[...]
    lines = x.shape[0]
    step = 10
    for at in range(0, lines, step):
        v = x[at : at + step].astype(jnp.float32)
        act = (v - average) * scale
        h = act * sigmoid(act)
        keep = in_grid(
            h.shape, at - FINE_RIM + place[0], place[1], FINE_RIM, rows, cols
        )
        h = jnp.where(keep, h, 0.0)
        hidden[at : at + step, :, 0:LANES] = pltpu.roll(h, 1, 1).astype(jnp.bfloat16)
        hidden[at : at + step, :, LANES : 2 * LANES] = h.astype(jnp.bfloat16)
        hidden[at : at + step, :, 2 * LANES :] = pltpu.roll(h, PITCH - 1, 1).astype(jnp.bfloat16)
    step = (lines - 2) // 4
    for at in range(0, lines - 2, step):
        acc = x[at + 1 : at + 1 + step].astype(jnp.float32).reshape(step * PITCH, LANES)
        conv = jnp.zeros_like(acc)
        for tap in range(3):
            conv = conv + jnp.dot(
                hidden[at + tap : at + tap + step].reshape(step * PITCH, 3 * LANES),
                weight[tap],
                preferred_element_type=jnp.float32,
            )
        block[at * PITCH : (at + step) * PITCH] = (
            (acc + conv).astype(jnp.bfloat16).astype(jnp.float32)
        )
    half = PITCH // 2
    step = (lines - 2) // 4
    first = jnp.zeros((1, coarse.shape[1]), jnp.float32)
    second = jnp.zeros((1, coarse.shape[1]), jnp.float32)
    for at in range(0, (lines - 2) // 2, step):
        size = 2 * step * half
        pair = block[pl.ds(2 * at * PITCH, size, stride=2), :] + block[
            pl.ds(2 * at * PITCH + 1, size, stride=2), :
        ]
        mean = 0.25 * jnp.sum(pair.reshape(step, 2, half, LANES), axis=1)
        mean = mean.reshape(step * half, LANES).astype(jnp.bfloat16)
        pooled[at * half : (at + step) * half] = mean
        cells = jnp.dot(mean, projection[...], preferred_element_type=jnp.float32).astype(
            jnp.bfloat16
        )
        coarse[at * half : (at + step) * half] = cells
        own = cells.astype(jnp.float32).reshape(step, half, -1)[:, : half // 2]
        low = 1 if at == 0 else 0
        high = step - 1 if at + step == (lines - 2) // 2 else step
        own = own[low:high]
        first = first + over_cells(own)
        second = second + over_cells(own * own)
    spread(copies, [first[:, :LANES], first[:, LANES:], second[:, :LANES], second[:, LANES:]])


def coarse_transpose(grad, weight, out, shifted):
    half = PITCH // 2
    lines = grad.shape[0]
    step = lines // 4
    for at in range(0, lines, step):
        g = grad[at : at + step].astype(jnp.float32)
        shifted[0, at : at + step] = pltpu.roll(g, half - 1, 1).astype(jnp.bfloat16)
        shifted[1, at : at + step] = grad[at : at + step]
        shifted[2, at : at + step] = pltpu.roll(g, 1, 1).astype(jnp.bfloat16)
    step = (lines - 2) // 2
    for at in range(0, lines - 2, step):
        acc = jnp.zeros((step * half, weight.shape[2]), jnp.float32)
        for row_tap in range(3):
            for col_tap in range(3):
                begin = at + 2 - row_tap
                acc = acc + lax.dot_general(
                    shifted[col_tap, begin : begin + step].reshape(step * half, -1),
                    weight[row_tap, col_tap],
                    (((1,), (1,)), ((), ())),
                    preferred_element_type=jnp.float32,
                )
        out[at * half : (at + step) * half] = acc


def coarse_middle(count, rows, cols, place, sums, coarse, pre, gain,
                  hidden, dnorm, copies, stats):
    tot = jnp.sum(sums[...], axis=0)
    average, inverse = moments(
        jnp.concatenate([tot[0:1], tot[1:2]], axis=1),
        jnp.concatenate([tot[2:3], tot[3:4]], axis=1),
        count,
        2 * LANES // GROUPS,
    )
    stats[0] = average
    stats[1] = inverse
    average, inverse = average[0:1], inverse[0:1]
    half = PITCH // 2
    lines = coarse.shape[0] // half
    channels = coarse.shape[1]
    step = lines // 2
    first = jnp.zeros((1, channels), jnp.float32)
    second = jnp.zeros((1, channels), jnp.float32)
    for at in range(0, lines, step):
        span = slice(at * half, (at + step) * half)
        normed = (coarse[span].astype(jnp.float32) - average) * inverse
        act = normed * gain[...]
        sigma = sigmoid(act)
        h = (act * sigma).reshape(step, half, channels)
        h = jnp.where(
            in_grid(h.shape, at - 1 + place[2], place[3], COARSE_RIM, rows, cols), h, 0.0
        )
        hidden[at : at + step, :, 0:channels] = pltpu.roll(h, 1, 1).astype(jnp.bfloat16)
        hidden[at : at + step, :, channels : 2 * channels] = h.astype(jnp.bfloat16)
        hidden[at : at + step, :, 2 * channels :] = pltpu.roll(h, half - 1, 1).astype(jnp.bfloat16)
        dact = pre[span] * (sigma * (1.0 + act * (1.0 - sigma)))
        dn = dact * gain[...]
        dnorm[span] = dn
        low = 1 if at == 0 else 0
        high = step - 1 if at + step == lines else step
        own = slice(low, high), slice(0, half // 2)
        first = first + over_cells(dn.reshape(step, half, channels)[own])
        second = second + over_cells((dact * normed).reshape(step, half, channels)[own])
    spread(copies, [first[:, :LANES], first[:, LANES:], second[:, :LANES], second[:, LANES:]])


def coarse_rest(hidden, coarse, grad, weight, out, rows_out):
    half = PITCH // 2
    height = out.shape[0]
    channels = out.shape[2]
    step = height // 2
    for at in range(0, height, step):
        acc = coarse[(at + 1) * half : (at + 1 + step) * half].astype(jnp.float32)
        conv = jnp.zeros_like(acc)
        for tap in range(3):
            conv = conv + jnp.dot(
                hidden[at + tap : at + tap + step].reshape(step * half, 3 * channels),
                weight[tap],
                preferred_element_type=jnp.float32,
            )
        out[at : at + step] = (acc + conv).reshape(step, half, channels)[:, : half // 2].astype(
            jnp.bfloat16
        )
    g = grad[2 : 2 + height].astype(jnp.float32)
    own = lax.broadcasted_iota(jnp.int32, g.shape, 1) < half // 2
    g = jnp.where(own, g, 0.0).astype(jnp.bfloat16).reshape(height * half, channels)
    tall = 9 * channels
    for tap in range(3):
        k = lax.dot_general(
            hidden[tap : tap + height].reshape(height * half, 3 * channels),
            g,
            (((0,), (0,)), ((), ())),
            preferred_element_type=jnp.float32,
        ).astype(jnp.bfloat16)
        at = tap * 3 * channels
        rows_out[at : at + 3 * channels] = k[:, :LANES]
        rows_out[tall + at : tall + at + 3 * channels] = k[:, LANES:]


def fine_backward(coarse_count, rows, cols, place, sums, coarse, pooled, grad, dnorm, stats_c,
                  gain_c, projection, weight_t, x, hidden, stats_f, gain_f, rows_in,
                  rows_out, gain_c_grad, partial, up, shifted, taps):
    rows_out[0 : rows_in.shape[0]] = rows_in[...]
    tot = jnp.sum(sums[...], axis=0)
    first = jnp.concatenate([tot[0:1], tot[1:2]], axis=1)
    second = jnp.concatenate([tot[2:3], tot[3:4]], axis=1)
    gain_c_grad[...] = second
    size = 2 * LANES // GROUPS
    a_sum = group_sum(wide(first), size)[0:1] / coarse_count
    b_sum = group_sum(wide(second * gain_c[...]), size)[0:1] / coarse_count
    average, inverse = stats_c[0, 0:1], stats_c[1, 0:1]
    half = PITCH // 2
    lines = coarse.shape[0] // half
    channels = coarse.shape[1]
    height = 2 * (lines - 2)
    step = lines // 2
    proj_grad = jnp.zeros((LANES, channels), jnp.float32)
    for at in range(0, lines, step):
        span = slice(at * half, (at + step) * half)
        normed = (coarse[span].astype(jnp.float32) - average) * inverse
        g = grad[at + 1 : at + 1 + step].astype(jnp.float32).reshape(step * half, channels)
        d = g + inverse * (dnorm[span] - a_sum - normed * b_sum)
        d = d.reshape(step, half, channels)
        d = jnp.where(
            in_grid(d.shape, at - 1 + place[2], place[3], COARSE_RIM, rows, cols), d, 0.0
        )
        line = lax.broadcasted_iota(jnp.int32, d.shape, 0) + at
        spot = lax.broadcasted_iota(jnp.int32, d.shape, 1)
        own = (line >= 1) & (line < lines - 1) & (spot < half // 2)
        own = jnp.where(own, d, 0.0).astype(jnp.bfloat16).reshape(step * half, channels)
        d = d.astype(jnp.bfloat16).reshape(step * half, channels)
        proj_grad = proj_grad + lax.dot_general(
            pooled[span], own, (((0,), (0,)), ((), ())), preferred_element_type=jnp.float32
        )
        small = lax.dot_general(
            d, projection[...], (((1,), (1,)), ((), ())), preferred_element_type=jnp.float32
        )
        small = (small * 0.25).astype(jnp.bfloat16).astype(jnp.float32)
        up[pl.ds(at * PITCH, step * half, stride=2), :] = small
        up[pl.ds(at * PITCH + 1, step * half, stride=2), :] = small
    for at in range(0, lines, step):
        u = up[at * PITCH : (at + step) * PITCH].reshape(step, PITCH, LANES)
        shifted[at : at + step, :, 0:LANES] = pltpu.roll(u, PITCH - 1, 1).astype(jnp.bfloat16)
        shifted[at : at + step, :, LANES : 2 * LANES] = u.astype(jnp.bfloat16)
        shifted[at : at + step, :, 2 * LANES :] = pltpu.roll(u, 1, 1).astype(jnp.bfloat16)
    width = PITCH // 2
    for tap in range(3):
        for at in range(0, lines, step):
            y = jnp.dot(
                shifted[at : at + step, 0:width, :].reshape(step * width, 3 * LANES),
                weight_t[tap],
                preferred_element_type=jnp.float32,
            )
            taps[tap, at : at + step] = y.reshape(step, width, LANES)
    average, inverse = stats_f[0, 0:1], stats_f[1, 0:1]
    first = jnp.zeros((1, LANES), jnp.float32)
    second = jnp.zeros((1, LANES), jnp.float32)
    step = 8
    for at in range(0, lines - 2, step):
        even = taps[0, at + 1 : at + 1 + step] + taps[1, at + 1 : at + 1 + step] + taps[
            2, at : at + step
        ]
        odd = taps[0, at + 2 : at + 2 + step] + taps[1, at + 1 : at + 1 + step] + taps[
            2, at + 1 : at + 1 + step
        ]
        both = jnp.stack([even, odd], axis=1).reshape(2 * step, width, LANES)
        begin = FINE_RIM + 2 * at
        v = x[begin : begin + 2 * step, 0:width, :].astype(jnp.float32)
        normed = (v - average) * inverse
        act = normed * gain_f[...]
        sigma = sigmoid(act)
        dact = both * (sigma * (1.0 + act * (1.0 - sigma)))
        dn = dact * gain_f[...]
        first = first + over_cells(dn)
        second = second + over_cells(dact * normed)
        u = up[(at + 1) * PITCH : (at + 1 + step) * PITCH].reshape(step, PITCH, LANES)[:, 0:width]
        u = jnp.broadcast_to(u[:, None], (step, 2, width, LANES)).reshape(2 * step, width, LANES)
        partial[2 * at : 2 * at + 2 * step] = u + inverse * dn
    d = up[PITCH : (lines - 1) * PITCH].reshape(lines - 2, PITCH, LANES)[:, 0:width]
    d = jnp.broadcast_to(
        d.astype(jnp.bfloat16)[:, None], (lines - 2, 2, width, LANES)
    ).reshape(height * width, LANES)
    at = 18 * channels
    for tap in range(3):
        begin = FINE_RIM - 1 + tap
        k = lax.dot_general(
            hidden[begin : begin + height, 0:width, :].reshape(height * width, 3 * LANES),
            d,
            (((0,), (0,)), ((), ())),
            preferred_element_type=jnp.float32,
        )
        rows_out[at : at + 3 * LANES] = k.astype(jnp.bfloat16)
        at += 3 * LANES
    proj_grad = proj_grad.astype(jnp.bfloat16)
    rows_out[at : at + LANES] = proj_grad[:, :LANES]
    rows_out[at + LANES : at + 2 * LANES] = proj_grad[:, LANES:]
    at += 2 * LANES
    spare = rows_out.shape[0] - at
    small = jnp.concatenate([first, second], axis=0)
    high = small.astype(jnp.bfloat16).astype(jnp.float32)
    middle = (small - high).astype(jnp.bfloat16).astype(jnp.float32)
    low = small - high - middle
    tail = jnp.concatenate([high, middle, low, jnp.zeros_like(low)], axis=0)
    rows_out[at:] = jnp.concatenate(
        [jnp.zeros((spare - 8, LANES), jnp.float32), tail], axis=0
    ).astype(jnp.bfloat16)


def finish(fine_count, rows, partial, x, stats, gain,
           field_grad, weight_f, gain_f, proj, weight_c):
    count = rows.shape[0]
    small = rows[count - 8 :].astype(jnp.float32)
    small = small[0:2] + small[2:4] + small[4:6]
    first, second = small[0:1], small[1:2]
    gain_f[...] = second
    size = LANES // GROUPS
    a_sum = group_sum(wide(first), size)[0:1] / fine_count
    b_sum = group_sum(wide(second * gain[...]), size)[0:1] / fine_count
    average, inverse = stats[0, 0:1], stats[1, 0:1]
    height, width, _ = partial.shape
    step = 16
    for at in range(0, height, step):
        v = x[FINE_RIM + at : FINE_RIM + at + step, 0:width, :].astype(jnp.float32)
        normed = (v - average) * inverse
        field_grad[at : at + step] = (
            partial[at : at + step] - inverse * (a_sum + normed * b_sum)
        ).astype(jnp.bfloat16)
    tall = weight_c.shape[0]
    weight_c[:, :LANES] = rows[0:tall].astype(jnp.float32)
    weight_c[:, LANES:] = rows[tall : 2 * tall].astype(jnp.float32)
    at = 2 * tall
    weight_f[...] = rows[at : at + weight_f.shape[0]].astype(jnp.float32)
    at += weight_f.shape[0]
    proj[:, :LANES] = rows[at : at + LANES].astype(jnp.float32)
    proj[:, LANES:] = rows[at + LANES : at + 2 * LANES].astype(jnp.float32)


def gathered(copies):
    far = lax.axis_size(FAR)
    received = lax.all_to_all(copies, NEAR, 0, 0, tiled=True)
    (copies,) = call(relay, [((far,) + copies.shape[1:], jnp.float32)], received)
    return lax.all_to_all(copies, FAR, 0, 0, tiled=True)


def planes(values):
    high = lax.reduce_precision(values, 8, 7)
    middle = lax.reduce_precision(values - high, 8, 7)
    low = values - high - middle
    return jnp.concatenate([high, middle, low, jnp.zeros((2, LANES), jnp.float32)]).astype(
        jnp.bfloat16
    )


def from_planes(rows):
    rows = rows.astype(jnp.float32)
    return rows[0:2] + rows[2:4] + rows[4:6]


def gradient_totals(part):
    holder = True
    for axes in STAGES:
        count = lax.axis_size(axes)
        pieces = lax.all_to_all(part.reshape(count, -1, LANES), axes, 0, 0, tiled=True)
        sums = jnp.sum(pieces.astype(jnp.float32), axis=0)
        holder = holder & (lax.axis_index(axes) == count - 1)
        tail = jnp.where(holder, planes(from_planes(sums[-8:])), sums[-8:].astype(jnp.bfloat16))
        part = lax.dynamic_update_slice(
            sums.astype(jnp.bfloat16), tail, (sums.shape[0] - 8, 0)
        )
    for axes in STAGES[::-1]:
        count = lax.axis_size(axes)
        copies = jnp.broadcast_to(part[None], (count,) + part.shape)
        part = lax.all_to_all(copies, axes, 0, 0, tiled=True).reshape(-1, LANES)
    return part


def on_device(field, cotangent, gain_fine, weight_fine, projection, gain_coarse, weight_coarse):
    height, width, chan_fine = field.shape
    chan_coarse = projection.shape[1]
    half_h, half_w = (height // 2, width // 2)
    cells_all = height * width * lax.axis_size(GY_GX)
    fine_count = cells_all * (chan_fine // GROUPS)
    coarse_count = cells_all // 4 * (chan_coarse // GROUPS)
    rows, cols = height * lax.axis_size(GY), width * lax.axis_size(GX)
    f32, bf16 = jnp.float32, jnp.bfloat16
    near = lax.axis_size(NEAR)
    row, col = lax.axis_index(GY), lax.axis_index(GX)
    place = jnp.stack([row * height, col * width, row * half_h, col * half_w]).astype(jnp.int32)
    gain_f, gain_c = gain_fine.reshape(1, -1), gain_coarse.reshape(1, -1)
    weight_t = weight_fine.transpose(0, 1, 3, 2).reshape(3, 3 * chan_fine, chan_fine)

    (copies,) = call(field_sums, [((near, 2, LANES), f32)], field)
    sums = gathered(copies)
    x, grad = with_rims(field, cotangent, FINE_RIM, COARSE_RIM)
    lines = half_h + 2
    cells = lines * PITCH // 2
    (pre,) = call(
        coarse_transpose,
        [((cells, chan_coarse), f32)],
        grad,
        weight_coarse,
        scratch=[((3,) + grad.shape, bf16)],
    )
    hidden_f, pooled, coarse, copies, stats_f = call(
        functools.partial(fine_forward, fine_count, rows, cols),
        [
            (x.shape[:2] + (3 * chan_fine,), bf16),
            ((cells, chan_fine), bf16),
            ((cells, chan_coarse), bf16),
            ((near, 4, LANES), f32),
            ((2, 8, chan_fine), f32),
        ],
        place,
        x,
        sums,
        gain_f,
        weight_fine.reshape(3, 3 * chan_fine, chan_fine),
        projection,
        scratch=[((2 * lines * PITCH + 8, chan_fine), f32)],
    )
    sums = gathered(copies)
    hidden_c, dnorm, copies, stats_c = call(
        functools.partial(coarse_middle, coarse_count, rows // 2, cols // 2),
        [
            ((lines, PITCH // 2, 3 * chan_coarse), bf16),
            ((cells, chan_coarse), f32),
            ((near, 4, LANES), f32),
            ((2, 8, chan_coarse), f32),
        ],
        place,
        sums,
        coarse,
        pre,
        gain_c,
    )
    sums = gathered(copies)
    used = 18 * chan_coarse + 9 * chan_fine + chan_coarse
    used += -(used + 8) % (4 * lax.axis_size(GY_GX)) + 8
    coarse_output, parts = call(
        coarse_rest,
        [((half_h, half_w, chan_coarse), bf16), ((18 * chan_coarse, LANES), bf16)],
        hidden_c,
        coarse,
        grad,
        weight_coarse.reshape(3, 3 * chan_coarse, chan_coarse),
    )
    parts, coarse_gain_grad, partial = call(
        functools.partial(fine_backward, coarse_count, rows // 2, cols // 2),
        [
            ((used, LANES), bf16),
            ((1, chan_coarse), f32),
            ((height, width, chan_fine), f32),
        ],
        place,
        sums,
        coarse,
        pooled,
        grad,
        dnorm,
        stats_c,
        gain_c,
        projection,
        weight_t,
        x,
        hidden_f,
        stats_f,
        gain_f,
        parts,
        scratch=[
            ((lines * PITCH + 8, chan_fine), f32),
            ((lines, PITCH, 3 * chan_fine), bf16),
            ((3, lines, PITCH // 2, chan_fine), f32),
        ],
    )
    totals = gradient_totals(parts)
    field_grad, fine_weight_grad, fine_gain_grad, projection_grad, coarse_weight_grad = call(
        functools.partial(finish, fine_count),
        [
            ((height, width, chan_fine), bf16),
            ((9 * chan_fine, chan_fine), f32),
            ((1, chan_fine), f32),
            ((chan_fine, chan_coarse), f32),
            ((9 * chan_coarse, chan_coarse), f32),
        ],
        totals,
        partial,
        x,
        stats_f,
        gain_f,
    )
    return (
        coarse_output,
        field_grad,
        fine_weight_grad.reshape(weight_fine.shape),
        fine_gain_grad.reshape(-1),
        projection_grad,
        coarse_weight_grad.reshape(weight_coarse.shape),
        coarse_gain_grad.reshape(-1),
    )


def solution(mesh):
    finer = Mesh(mesh.devices.reshape(2, 8, 2, 8, 2), GY_GX)
    in_specs = (P(GY, GX, None), P(GY, GX, None), P(), P(), P(), P(), P())
    out_specs = (P(GY, GX, None), P(GY, GX, None), P(), P(), P(), P(), P())
    return jax.shard_map(
        on_device, mesh=finer, in_specs=in_specs, out_specs=out_specs, check_vma=False
    )
```

```python
import functools

import jax
import jax.numpy as jnp
from jax import lax
from jax.experimental import pallas as pl
from jax.experimental.pallas import tpu as pltpu
from jax.sharding import Mesh
from jax.sharding import PartitionSpec as P


GROUPS = 32
GY = ("gy_0", "gy_1")
GX = ("gx_0", "gx_1", "gx_2")
GY_GX = GY + GX
NEAR = ("gx_1", "gx_2")
FAR = ("gx_0", "gy_0", "gy_1")
STAGES = (("gx_2",), ("gx_0", "gy_0"), ("gx_1", "gy_1"))
LANES = 128
EPSILON = 1e-05

HBM = pltpu.HBM
PITCH = 32
FINE_RIM = 3
COARSE_RIM = 2


def swap(heads, tails, axis):
    ends = lax.axis_size(axis) - 1
    before = lax.ppermute(tails, axis, [(i, i + 1) for i in range(ends)])
    after = lax.ppermute(heads, axis, [(i + 1, i) for i in range(ends)])
    return before, after


def joined(fine, coarse):
    cells = coarse.reshape(-1, coarse.shape[2])
    return jnp.concatenate(
        [fine.reshape(-1, LANES)] + [cells[:, k : k + LANES] for k in range(0, cells.shape[1], LANES)]
    )


def parted(rims, fine, coarse):
    size = fine[0] * fine[1]
    cells = coarse[0] * coarse[1]
    halves = [rims[size + k * cells : size + (k + 1) * cells] for k in range(coarse[2] // LANES)]
    return rims[:size].reshape(fine), jnp.concatenate(halves, axis=1).reshape(coarse)


def ring(own, left, right, pitch):
    rows, cols, channels = own.shape
    gap = pitch - cols - left.shape[1] - right.shape[1]
    return jnp.concatenate([own, right, jnp.zeros((rows, gap, channels), own.dtype), left], axis=1)


def with_rims(fine, coarse, heads, tails):
    shapes = (FINE_RIM,) + fine.shape[1:], (COARSE_RIM,) + coarse.shape[1:]
    (f0, c0), (f1, c1) = (parted(r, *shapes) for r in swap(heads, tails, GY))
    fine = jnp.concatenate([f0, fine, f1])
    coarse = jnp.concatenate([c0, coarse, c1])
    shapes = (
        (fine.shape[0], FINE_RIM, fine.shape[2]),
        (coarse.shape[0], COARSE_RIM, coarse.shape[2]),
    )
    heads = joined(fine[:, :FINE_RIM], coarse[:, :COARSE_RIM])
    tails = joined(fine[:, -FINE_RIM:], coarse[:, -COARSE_RIM:])
    rims = swap(heads, tails, GX)
    (f0, c0), (f1, c1) = (parted(r, *shapes) for r in rims)
    return ring(fine, f0, f1, PITCH), ring(coarse, c0, c1, PITCH // 2)


def call(body, outs, *args, scratch=(), plain=()):
    spaces = [
        pl.BlockSpec(memory_space=pltpu.SMEM if a.dtype == jnp.int32 else pltpu.VMEM) for a in args
    ]
    args = [
        a
        if a.dtype == jnp.int32
        else pltpu.with_memory_space_constraint(a, pltpu.HBM if k in plain else pltpu.VMEM)
        for k, a in enumerate(args)
    ]
    return pl.pallas_call(
        body,
        out_shape=[
            (pltpu.VMEM if len(o) == 2 else o[2] or jax.ShapeDtypeStruct)(o[0], o[1])
            for o in outs
        ],
        in_specs=spaces,
        out_specs=[pl.BlockSpec(memory_space=pltpu.VMEM) for _ in outs],
        scratch_shapes=[pltpu.VMEM(shape, dtype) for shape, dtype in scratch],
        compiler_params=pltpu.CompilerParams(vmem_limit_bytes=24 << 20),
    )(*args)


def group_sum(values, size):
    lanes = values.shape[1]
    lane = lax.broadcasted_iota(jnp.int32, values.shape, 1)
    step = 1
    while step < size:
        after = pltpu.roll(values, lanes - step, 1)
        before = pltpu.roll(values, step, 1)
        values = values + jnp.where((lane & step) == 0, after, before)
        step *= 2
    return values


def wide(row):
    return jnp.broadcast_to(row, (8, row.shape[1]))


def moments(first, second, count, size):
    average = group_sum(wide(first), size) / count
    square = group_sum(wide(second), size) / count
    return average, lax.rsqrt(square - average * average + EPSILON)


def sigmoid(act):
    return 1.0 / (1.0 + jnp.exp(-act))


def in_grid(shape, first_row, first_col, rim, rows, cols):
    row = lax.broadcasted_iota(jnp.int32, shape, 0) + first_row
    place = lax.broadcasted_iota(jnp.int32, shape, 1)
    col = jnp.where(place < shape[1] - rim, place, place - shape[1]) + first_col
    return (row >= 0) & (row < rows) & (col >= 0) & (col < cols)


def over_cells(values):
    lanes = values.shape[-1]
    return jnp.sum(jnp.sum(values.reshape(-1, 8, lanes), axis=0), axis=0, keepdims=True)


def spread(copies, rows):
    for k, row in enumerate(rows):
        copies[:, k, :] = jnp.broadcast_to(row, (copies.shape[0], LANES))


def slab(rims, at, values):
    cells = values.reshape(-1, values.shape[-1])
    for lane in range(0, cells.shape[1], LANES):
        rims[at : at + cells.shape[0]] = cells[:, lane : lane + LANES]
        at += cells.shape[0]
    return at


def field_sums(field, grad, copies, heads, tails):
    slab(heads, slab(heads, 0, field[:FINE_RIM]), grad[:COARSE_RIM])
    slab(tails, slab(tails, 0, field[field.shape[0] - FINE_RIM :]), grad[grad.shape[0] - COARSE_RIM :])
    first = jnp.zeros((8, LANES), jnp.float32)
    second = jnp.zeros((8, LANES), jnp.float32)
    for at in range(0, field.shape[0], 8):
        v = field[at : at + 8].astype(jnp.float32).reshape(-1, 8, LANES)
        first = first + jnp.sum(v, axis=0)
        second = second + jnp.sum(v * v, axis=0)
    spread(
        copies, [jnp.sum(first, axis=0, keepdims=True), jnp.sum(second, axis=0, keepdims=True)]
    )


def relay(received, copies):
    sums = jnp.sum(received[...], axis=0)
    for k in range(copies.shape[1]):
        copies[:, k, :] = jnp.broadcast_to(sums[k : k + 1], (copies.shape[0], LANES))


def fine_forward(count, rows, cols, place, x, sums, gain, weight, projection,
                 center, pooled, coarse, copies, stats, hidden, block):
    tot = jnp.sum(sums[...], axis=0)
    average, inverse = moments(tot[0:1], tot[1:2], count, LANES // GROUPS)
    stats[0] = average
    stats[1] = inverse
    average, scale = average[0:1], inverse[0:1] * gain[...]
    lines = x.shape[0]
    step = 10
    for at in range(0, lines, step):
        v = x[at : at + step].astype(jnp.float32)
        act = (v - average) * scale
        h = act * sigmoid(act)
        keep = in_grid(
            h.shape, at - FINE_RIM + place[0], place[1], FINE_RIM, rows, cols
        )
        h = jnp.where(keep, h, 0.0)
        hidden[at : at + step, :, 0:LANES] = pltpu.roll(h, 1, 1).astype(jnp.bfloat16)
        hidden[at : at + step, :, LANES : 2 * LANES] = h.astype(jnp.bfloat16)
        center[at : at + step] = h.astype(jnp.bfloat16)
        hidden[at : at + step, :, 2 * LANES :] = pltpu.roll(h, PITCH - 1, 1).astype(jnp.bfloat16)
    step = (lines - 2) // 4
    for at in range(0, lines - 2, step):
        acc = x[at + 1 : at + 1 + step].astype(jnp.float32).reshape(step * PITCH, LANES)
        conv = jnp.zeros_like(acc)
        for tap in range(3):
            conv = conv + jnp.dot(
                hidden[at + tap : at + tap + step].reshape(step * PITCH, 3 * LANES),
                weight[tap],
                preferred_element_type=jnp.float32,
            )
        block[at * PITCH : (at + step) * PITCH] = (
            (acc + conv).astype(jnp.bfloat16).astype(jnp.float32)
        )
    half = PITCH // 2
    step = (lines - 2) // 4
    first = jnp.zeros((1, coarse.shape[1]), jnp.float32)
    second = jnp.zeros((1, coarse.shape[1]), jnp.float32)
    for at in range(0, (lines - 2) // 2, step):
        size = 2 * step * half
        pair = block[pl.ds(2 * at * PITCH, size, stride=2), :] + block[
            pl.ds(2 * at * PITCH + 1, size, stride=2), :
        ]
        mean = 0.25 * jnp.sum(pair.reshape(step, 2, half, LANES), axis=1)
        mean = mean.reshape(step * half, LANES).astype(jnp.bfloat16)
        pooled[at * half : (at + step) * half] = mean
        cells = jnp.dot(mean, projection[...], preferred_element_type=jnp.float32).astype(
            jnp.bfloat16
        )
        coarse[at * half : (at + step) * half] = cells
        own = cells.astype(jnp.float32).reshape(step, half, -1)[:, : half // 2]
        low = 1 if at == 0 else 0
        high = step - 1 if at + step == (lines - 2) // 2 else step
        own = own[low:high]
        first = first + over_cells(own)
        second = second + over_cells(own * own)
    spread(copies, [first[:, :LANES], first[:, LANES:], second[:, :LANES], second[:, LANES:]])


def coarse_transpose(grad, weight, fine_weight, out, fine_out, shifted):
    for tap in range(9):
        block = fine_weight[tap].astype(jnp.float32).T.astype(jnp.bfloat16)
        fine_out[tap // 3, tap % 3 * LANES : (tap % 3 + 1) * LANES] = block
    half = PITCH // 2
    lines = grad.shape[0]
    step = lines // 4
    for at in range(0, lines, step):
        g = grad[at : at + step].astype(jnp.float32)
        shifted[0, at : at + step] = pltpu.roll(g, half - 1, 1).astype(jnp.bfloat16)
        shifted[1, at : at + step] = grad[at : at + step]
        shifted[2, at : at + step] = pltpu.roll(g, 1, 1).astype(jnp.bfloat16)
    step = (lines - 2) // 2
    for at in range(0, lines - 2, step):
        acc = jnp.zeros((step * half, weight.shape[2]), jnp.float32)
        for row_tap in range(3):
            for col_tap in range(3):
                begin = at + 2 - row_tap
                acc = acc + lax.dot_general(
                    shifted[col_tap, begin : begin + step].reshape(step * half, -1),
                    weight[row_tap, col_tap],
                    (((1,), (1,)), ((), ())),
                    preferred_element_type=jnp.float32,
                )
        out[at * half : (at + step) * half] = acc


def coarse_middle(count, rows, cols, place, sums, coarse, pre, gain,
                  hidden, dnorm, copies, stats):
    tot = jnp.sum(sums[...], axis=0)
    average, inverse = moments(
        jnp.concatenate([tot[0:1], tot[1:2]], axis=1),
        jnp.concatenate([tot[2:3], tot[3:4]], axis=1),
        count,
        2 * LANES // GROUPS,
    )
    stats[0] = average
    stats[1] = inverse
    average, inverse = average[0:1], inverse[0:1]
    half = PITCH // 2
    lines = coarse.shape[0] // half
    channels = coarse.shape[1]
    step = lines // 2
    first = jnp.zeros((1, channels), jnp.float32)
    second = jnp.zeros((1, channels), jnp.float32)
    for at in range(0, lines, step):
        span = slice(at * half, (at + step) * half)
        normed = (coarse[span].astype(jnp.float32) - average) * inverse
        act = normed * gain[...]
        sigma = sigmoid(act)
        h = (act * sigma).reshape(step, half, channels)
        h = jnp.where(
            in_grid(h.shape, at - 1 + place[2], place[3], COARSE_RIM, rows, cols), h, 0.0
        )
        hidden[at : at + step] = h.astype(jnp.bfloat16)
        dact = pre[span] * (sigma * (1.0 + act * (1.0 - sigma)))
        dn = dact * gain[...]
        dnorm[span] = dn
        low = 1 if at == 0 else 0
        high = step - 1 if at + step == lines else step
        own = slice(low, high), slice(0, half // 2)
        first = first + over_cells(dn.reshape(step, half, channels)[own])
        second = second + over_cells((dact * normed).reshape(step, half, channels)[own])
    spread(copies, [first[:, :LANES], first[:, LANES:], second[:, :LANES], second[:, LANES:]])


def coarse_rest(center, coarse, grad, weight, out, rows_out, hidden):
    half = PITCH // 2
    height = out.shape[0]
    channels = out.shape[2]
    step = center.shape[0] // 2
    for at in range(0, center.shape[0], step):
        h = center[at : at + step].astype(jnp.float32)
        hidden[at : at + step, :, 0:channels] = pltpu.roll(h, 1, 1).astype(jnp.bfloat16)
        hidden[at : at + step, :, channels : 2 * channels] = center[at : at + step]
        hidden[at : at + step, :, 2 * channels :] = pltpu.roll(h, half - 1, 1).astype(jnp.bfloat16)
    step = height // 2
    for at in range(0, height, step):
        acc = coarse[(at + 1) * half : (at + 1 + step) * half].astype(jnp.float32)
        conv = jnp.zeros_like(acc)
        for tap in range(3):
            conv = conv + jnp.dot(
                hidden[at + tap : at + tap + step].reshape(step * half, 3 * channels),
                weight[tap],
                preferred_element_type=jnp.float32,
            )
        out[at : at + step] = (acc + conv).reshape(step, half, channels)[:, : half // 2].astype(
            jnp.bfloat16
        )
    g = grad[2 : 2 + height].astype(jnp.float32)
    own = lax.broadcasted_iota(jnp.int32, g.shape, 1) < half // 2
    g = jnp.where(own, g, 0.0).astype(jnp.bfloat16).reshape(height * half, channels)
    tall = 9 * channels
    for tap in range(3):
        k = lax.dot_general(
            hidden[tap : tap + height].reshape(height * half, 3 * channels),
            g,
            (((0,), (0,)), ((), ())),
            preferred_element_type=jnp.float32,
        ).astype(jnp.bfloat16)
        at = tap * 3 * channels
        rows_out[at : at + 3 * channels] = k[:, :LANES]
        rows_out[tall + at : tall + at + 3 * channels] = k[:, LANES:]


def fine_backward(coarse_count, rows, cols, place, sums, coarse, pooled, grad, dnorm, stats_c,
                  gain_c, projection, weight_t, x, hidden, stats_f, gain_f, rows_in,
                  rows_out, gain_c_grad, partial, up, shifted, taps):
    rows_out[0 : rows_in.shape[0]] = rows_in[...]
    tot = jnp.sum(sums[...], axis=0)
    first = jnp.concatenate([tot[0:1], tot[1:2]], axis=1)
    second = jnp.concatenate([tot[2:3], tot[3:4]], axis=1)
    gain_c_grad[...] = second
    size = 2 * LANES // GROUPS
    a_sum = group_sum(wide(first), size)[0:1] / coarse_count
    b_sum = group_sum(wide(second * gain_c[...]), size)[0:1] / coarse_count
    average, inverse = stats_c[0, 0:1], stats_c[1, 0:1]
    half = PITCH // 2
    lines = coarse.shape[0] // half
    channels = coarse.shape[1]
    height = 2 * (lines - 2)
    step = lines // 2
    proj_grad = jnp.zeros((LANES, channels), jnp.float32)
    for at in range(0, lines, step):
        span = slice(at * half, (at + step) * half)
        normed = (coarse[span].astype(jnp.float32) - average) * inverse
        g = grad[at + 1 : at + 1 + step].astype(jnp.float32).reshape(step * half, channels)
        d = g + inverse * (dnorm[span] - a_sum - normed * b_sum)
        d = d.reshape(step, half, channels)
        d = jnp.where(
            in_grid(d.shape, at - 1 + place[2], place[3], COARSE_RIM, rows, cols), d, 0.0
        )
        line = lax.broadcasted_iota(jnp.int32, d.shape, 0) + at
        spot = lax.broadcasted_iota(jnp.int32, d.shape, 1)
        own = (line >= 1) & (line < lines - 1) & (spot < half // 2)
        own = jnp.where(own, d, 0.0).astype(jnp.bfloat16).reshape(step * half, channels)
        d = d.astype(jnp.bfloat16).reshape(step * half, channels)
        proj_grad = proj_grad + lax.dot_general(
            pooled[span], own, (((0,), (0,)), ((), ())), preferred_element_type=jnp.float32
        )
        small = lax.dot_general(
            d, projection[...], (((1,), (1,)), ((), ())), preferred_element_type=jnp.float32
        )
        small = (small * 0.25).astype(jnp.bfloat16).astype(jnp.float32)
        up[pl.ds(at * PITCH, step * half, stride=2), :] = small
        up[pl.ds(at * PITCH + 1, step * half, stride=2), :] = small
    for at in range(0, lines, step):
        u = up[at * PITCH : (at + step) * PITCH].reshape(step, PITCH, LANES)
        shifted[at : at + step, :, 0:LANES] = pltpu.roll(u, PITCH - 1, 1).astype(jnp.bfloat16)
        shifted[at : at + step, :, LANES : 2 * LANES] = u.astype(jnp.bfloat16)
        shifted[at : at + step, :, 2 * LANES :] = pltpu.roll(u, 1, 1).astype(jnp.bfloat16)
    width = PITCH // 2
    for tap in range(3):
        for at in range(0, lines, step):
            y = jnp.dot(
                shifted[at : at + step, 0:width, :].reshape(step * width, 3 * LANES),
                weight_t[tap],
                preferred_element_type=jnp.float32,
            )
            taps[tap, at : at + step] = y.reshape(step, width, LANES)
    average, inverse = stats_f[0, 0:1], stats_f[1, 0:1]
    first = jnp.zeros((1, LANES), jnp.float32)
    second = jnp.zeros((1, LANES), jnp.float32)
    step = 8
    for at in range(0, lines - 2, step):
        even = taps[0, at + 1 : at + 1 + step] + taps[1, at + 1 : at + 1 + step] + taps[
            2, at : at + step
        ]
        odd = taps[0, at + 2 : at + 2 + step] + taps[1, at + 1 : at + 1 + step] + taps[
            2, at + 1 : at + 1 + step
        ]
        both = jnp.stack([even, odd], axis=1).reshape(2 * step, width, LANES)
        begin = FINE_RIM + 2 * at
        v = x[begin : begin + 2 * step, 0:width, :].astype(jnp.float32)
        normed = (v - average) * inverse
        act = normed * gain_f[...]
        sigma = sigmoid(act)
        dact = both * (sigma * (1.0 + act * (1.0 - sigma)))
        dn = dact * gain_f[...]
        first = first + over_cells(dn)
        second = second + over_cells(dact * normed)
        u = up[(at + 1) * PITCH : (at + 1 + step) * PITCH].reshape(step, PITCH, LANES)[:, 0:width]
        u = jnp.broadcast_to(u[:, None], (step, 2, width, LANES)).reshape(2 * step, width, LANES)
        partial[2 * at : 2 * at + 2 * step] = u + inverse * dn
    for at in range(1, lines - 1, step):
        u = up[at * PITCH : (at + step) * PITCH].reshape(step, PITCH, LANES)
        own = lax.broadcasted_iota(jnp.int32, u.shape, 1) < width
        u = jnp.where(own, u, 0.0)
        shifted[at : at + step, :, 0:LANES] = pltpu.roll(u, PITCH - 1, 1).astype(jnp.bfloat16)
        shifted[at : at + step, :, LANES : 2 * LANES] = u.astype(jnp.bfloat16)
        shifted[at : at + step, :, 2 * LANES :] = pltpu.roll(u, 1, 1).astype(jnp.bfloat16)
    d = shifted[1 : lines - 1]
    d = jnp.broadcast_to(d[:, None], (lines - 2, 2) + d.shape[1:])
    d = d.reshape(height * PITCH, 3 * LANES)
    at = 18 * channels
    for tap in range(3):
        begin = FINE_RIM - 1 + tap
        k = lax.dot_general(
            hidden[begin : begin + height].reshape(height * PITCH, LANES),
            d,
            (((0,), (0,)), ((), ())),
            preferred_element_type=jnp.float32,
        ).astype(jnp.bfloat16)
        for col_tap in range(3):
            rows_out[at : at + LANES] = k[:, col_tap * LANES : (col_tap + 1) * LANES]
            at += LANES
    proj_grad = proj_grad.astype(jnp.bfloat16)
    rows_out[at : at + LANES] = proj_grad[:, :LANES]
    rows_out[at + LANES : at + 2 * LANES] = proj_grad[:, LANES:]
    at += 2 * LANES
    spare = rows_out.shape[0] - at
    small = jnp.concatenate([first, second], axis=0)
    rows_out[at:] = jnp.concatenate(
        [jnp.zeros((spare - 8, LANES), jnp.float32), split(small)], axis=0
    ).astype(jnp.bfloat16)


def finish(fine_count, rows, partial, x, stats, gain,
           field_grad, weight_f, gain_f, proj, weight_c):
    count = rows.shape[0]
    small = rows[count - 8 :].astype(jnp.float32)
    small = small[0:2] + small[2:4] + small[4:6]
    first, second = small[0:1], small[1:2]
    gain_f[...] = second
    size = LANES // GROUPS
    a_sum = group_sum(wide(first), size)[0:1] / fine_count
    b_sum = group_sum(wide(second * gain[...]), size)[0:1] / fine_count
    average, inverse = stats[0, 0:1], stats[1, 0:1]
    height, width, _ = partial.shape
    step = 16
    for at in range(0, height, step):
        v = x[FINE_RIM + at : FINE_RIM + at + step, 0:width, :].astype(jnp.float32)
        normed = (v - average) * inverse
        field_grad[at : at + step] = (
            partial[at : at + step] - inverse * (a_sum + normed * b_sum)
        ).astype(jnp.bfloat16)
    tall = weight_c.shape[0]
    weight_c[:, :LANES] = rows[0:tall].astype(jnp.float32)
    weight_c[:, LANES:] = rows[tall : 2 * tall].astype(jnp.float32)
    at = 2 * tall
    weight_f[...] = rows[at : at + weight_f.shape[0]].astype(jnp.float32)
    at += weight_f.shape[0]
    proj[:, :LANES] = rows[at : at + LANES].astype(jnp.float32)
    proj[:, LANES:] = rows[at + LANES : at + 2 * LANES].astype(jnp.float32)


def gathered(copies):
    far = lax.axis_size(FAR)
    received = lax.all_to_all(copies, NEAR, 0, 0, tiled=True)
    (copies,) = call(relay, [((far,) + copies.shape[1:], jnp.float32, None)], received)
    return lax.all_to_all(copies, FAR, 0, 0, tiled=True)


def split(small):
    high = small.astype(jnp.bfloat16).astype(jnp.float32)
    middle = (small - high).astype(jnp.bfloat16).astype(jnp.float32)
    low = small - high - middle
    return jnp.concatenate([high, middle, low, jnp.zeros_like(low)], axis=0)


def add_up(stage, place, pieces, out, *scratch):
    rows = pieces.shape[1]
    step = 256 if rows % 256 == 0 else rows
    pitch = out.shape[-2]
    for at in range(0, rows, step):
        sums = pieces[0, at : at + step].astype(jnp.float32)
        for k in range(1, pieces.shape[0]):
            sums = sums + pieces[k, at : at + step].astype(jnp.float32)
        if at + step == rows:
            last = sums[step - 8 :]
            tail = split(last[0:2] + last[2:4] + last[4:6])
            tail = jnp.where(place[4 + stage] == 1, tail, last)
            sums = jnp.concatenate([sums[: step - 8], tail], axis=0)
        if scratch:
            scratch[0][at : at + step] = sums
        else:
            out[at : at + step] = sums.astype(jnp.bfloat16)
    if scratch:
        for k in range(out.shape[0]):
            out[k] = scratch[0][k * pitch : (k + 1) * pitch].astype(jnp.bfloat16)


def planes(values):
    high = lax.reduce_precision(values, 8, 7)
    middle = lax.reduce_precision(values - high, 8, 7)
    low = values - high - middle
    return jnp.concatenate([high, middle, low, jnp.zeros((2, LANES), jnp.float32)]).astype(
        jnp.bfloat16
    )


def gradient_totals(part, place):
    for stage, axes in enumerate(STAGES):
        count = lax.axis_size(axes)
        pieces = lax.all_to_all(part.reshape(count, -1, LANES), axes, 0, 0, tiled=True)
        rows = pieces.shape[1]
        kernel = functools.partial(add_up, stage)
        if stage == 0:
            (part,) = call(kernel, [((rows, LANES), jnp.bfloat16, None)], place, pieces)
        elif stage == 1:
            pitch = rows // lax.axis_size(STAGES[2])
            (part,) = call(
                kernel,
                [((rows // pitch, pitch, LANES), jnp.bfloat16, None)],
                place,
                pieces,
                scratch=[((rows, LANES), jnp.float32)],
            )
        else:
            sums = jnp.sum(pieces.astype(jnp.float32), axis=0)
            last = sums[-8:]
            tail = planes(last[0:2] + last[2:4] + last[4:6])
            tail = jnp.where(place[4 + stage] == 1, tail, last.astype(jnp.bfloat16))
            part = jnp.concatenate([sums[:-8].astype(jnp.bfloat16), tail])
    for axes in STAGES[::-1]:
        count = lax.axis_size(axes)
        copies = jnp.broadcast_to(part[None], (count,) + part.shape)
        part = lax.all_to_all(copies, axes, 0, 0, tiled=True).reshape(-1, LANES)
    return part


def on_device(field, cotangent, gain_fine, weight_fine, projection, gain_coarse, weight_coarse):
    height, width, chan_fine = field.shape
    chan_coarse = projection.shape[1]
    half_h, half_w = (height // 2, width // 2)
    cells_all = height * width * lax.axis_size(GY_GX)
    fine_count = cells_all * (chan_fine // GROUPS)
    coarse_count = cells_all // 4 * (chan_coarse // GROUPS)
    rows, cols = height * lax.axis_size(GY), width * lax.axis_size(GX)
    f32, bf16 = jnp.float32, jnp.bfloat16
    near = lax.axis_size(NEAR)
    row, col = lax.axis_index(GY), lax.axis_index(GX)
    holds, held = [], jnp.int32(1)
    for axes in STAGES:
        held = held * (lax.axis_index(axes) == lax.axis_size(axes) - 1)
        holds.append(held)
    place = jnp.stack([row * height, col * width, row * half_h, col * half_w] + holds)
    place = place.astype(jnp.int32)
    gain_f, gain_c = gain_fine.reshape(1, -1), gain_coarse.reshape(1, -1)

    slabs = FINE_RIM * width + COARSE_RIM * half_w * chan_coarse // LANES
    copies, heads, tails = call(
        field_sums,
        [((near, 2, LANES), f32, None), ((slabs, LANES), bf16, None), ((slabs, LANES), bf16, None)],
        field,
        cotangent,
        plain=(0, 1),
    )
    sums = gathered(copies)
    x, grad = with_rims(field, cotangent, heads, tails)
    lines = half_h + 2
    cells = lines * PITCH // 2
    pre, weight_t = call(
        coarse_transpose,
        [((cells, chan_coarse), f32), ((3, 3 * chan_fine, chan_fine), bf16, HBM)],
        grad,
        weight_coarse,
        weight_fine.reshape(9, chan_fine, chan_fine),
        plain=(1, 2),
        scratch=[((3,) + grad.shape, bf16)],
    )
    hidden_f, pooled, coarse, copies, stats_f = call(
        functools.partial(fine_forward, fine_count, rows, cols),
        [
            (x.shape, bf16, HBM),
            ((cells, chan_fine), bf16, HBM),
            ((cells, chan_coarse), bf16),
            ((near, 4, LANES), f32, None),
            ((2, 8, chan_fine), f32),
        ],
        place,
        x,
        sums,
        gain_f,
        weight_fine.reshape(3, 3 * chan_fine, chan_fine),
        projection,
        scratch=[
            (x.shape[:2] + (3 * chan_fine,), bf16),
            ((2 * lines * PITCH + 8, chan_fine), f32),
        ],
    )
    sums = gathered(copies)
    hidden_c, dnorm, copies, stats_c = call(
        functools.partial(coarse_middle, coarse_count, rows // 2, cols // 2),
        [
            ((lines, PITCH // 2, chan_coarse), bf16, HBM),
            ((cells, chan_coarse), f32, HBM),
            ((near, 4, LANES), f32, None),
            ((2, 8, chan_coarse), f32),
        ],
        place,
        sums,
        coarse,
        pre,
        gain_c,
    )
    sums = gathered(copies)
    used = 18 * chan_coarse + 9 * chan_fine + chan_coarse
    used += -(used + 8) % (4 * lax.axis_size(GY_GX)) + 8
    coarse_output, parts = call(
        coarse_rest,
        [((half_h, half_w, chan_coarse), bf16, None), ((18 * chan_coarse, LANES), bf16)],
        hidden_c,
        coarse,
        grad,
        weight_coarse.reshape(3, 3 * chan_coarse, chan_coarse),
        scratch=[((lines, PITCH // 2, 3 * chan_coarse), bf16)],
        plain=(0, 3),
    )
    parts, coarse_gain_grad, partial = call(
        functools.partial(fine_backward, coarse_count, rows // 2, cols // 2),
        [
            ((used, LANES), bf16, None),
            ((1, chan_coarse), f32, None),
            ((height, width, chan_fine), f32),
        ],
        place,
        sums,
        coarse,
        pooled,
        grad,
        dnorm,
        stats_c,
        gain_c,
        projection,
        weight_t,
        x,
        hidden_f,
        stats_f,
        gain_f,
        parts,
        scratch=[
            ((lines * PITCH + 8, chan_fine), f32),
            ((lines, PITCH, 3 * chan_fine), bf16),
            ((3, lines, PITCH // 2, chan_fine), f32),
        ],
        plain=(3, 5, 8, 9, 11),
    )
    totals = gradient_totals(parts, place)
    field_grad, fine_weight_grad, fine_gain_grad, projection_grad, coarse_weight_grad = call(
        functools.partial(finish, fine_count),
        [
            ((height, width, chan_fine), bf16, None),
            ((9 * chan_fine, chan_fine), f32, None),
            ((1, chan_fine), f32, None),
            ((chan_fine, chan_coarse), f32, None),
            ((9 * chan_coarse, chan_coarse), f32, None),
        ],
        totals,
        partial,
        x,
        stats_f,
        gain_f,
    )
    return (
        coarse_output,
        field_grad,
        fine_weight_grad.reshape(weight_fine.shape),
        fine_gain_grad.reshape(-1),
        projection_grad,
        coarse_weight_grad.reshape(weight_coarse.shape),
        coarse_gain_grad.reshape(-1),
    )


def solution(mesh):
    finer = Mesh(mesh.devices.reshape(2, 8, 2, 8, 2), GY_GX)
    in_specs = (P(GY, GX, None), P(GY, GX, None), P(), P(), P(), P(), P())
    out_specs = (P(GY, GX, None), P(GY, GX, None), P(), P(), P(), P(), P())

    return jax.shard_map(
        on_device, mesh=finer, in_specs=in_specs, out_specs=out_specs, check_vma=False
    )
```

```python
import functools

import jax
import jax.numpy as jnp
from jax import lax
from jax.experimental import pallas as pl
from jax.experimental.pallas import tpu as pltpu
from jax.sharding import Mesh
from jax.sharding import PartitionSpec as P


GROUPS = 32
GY = ("gy_0", "gy_1")
GX = ("gx_0", "gx_1", "gx_2")
GY_GX = GY + GX
NEAR = ("gx_1", "gx_2")
FAR = ("gx_0", "gy_0", "gy_1")
STAGES = (("gx_2",), ("gx_0", "gy_0"), ("gx_1", "gy_1"))
LANES = 128
EPSILON = 1e-05

HBM = pltpu.HBM
PITCH = 32
FINE_RIM = 3
COARSE_RIM = 2


def swap(heads, tails, axis):
    ends = lax.axis_size(axis) - 1
    before = lax.ppermute(tails, axis, [(i, i + 1) for i in range(ends)])
    after = lax.ppermute(heads, axis, [(i + 1, i) for i in range(ends)])
    return before, after


def joined(fine, coarse):
    cells = coarse.reshape(-1, coarse.shape[2])
    return jnp.concatenate(
        [fine.reshape(-1, LANES)] + [cells[:, k : k + LANES] for k in range(0, cells.shape[1], LANES)]
    )


def parted(rims, fine, coarse):
    size = fine[0] * fine[1]
    cells = coarse[0] * coarse[1]
    halves = [rims[size + k * cells : size + (k + 1) * cells] for k in range(coarse[2] // LANES)]
    return rims[:size].reshape(fine), jnp.concatenate(halves, axis=1).reshape(coarse)


def ring(own, left, right, pitch):
    rows, cols, channels = own.shape
    gap = pitch - cols - left.shape[1] - right.shape[1]
    return jnp.concatenate([own, right, jnp.zeros((rows, gap, channels), own.dtype), left], axis=1)


def with_rims(fine, coarse, heads, tails):
    shapes = (FINE_RIM,) + fine.shape[1:], (COARSE_RIM,) + coarse.shape[1:]
    rims = swap(heads, tails, GY)
    (f0, c0), (f1, c1) = (parted(r, *shapes) for r in rims)
    fine = jnp.concatenate([f0, fine, f1])
    coarse = jnp.concatenate([c0, coarse, c1])
    shapes = (
        (fine.shape[0], FINE_RIM, fine.shape[2]),
        (coarse.shape[0], COARSE_RIM, coarse.shape[2]),
    )
    heads = joined(fine[:, :FINE_RIM], coarse[:, :COARSE_RIM])
    tails = joined(fine[:, -FINE_RIM:], coarse[:, -COARSE_RIM:])
    rims = swap(heads, tails, GX)
    f0, f1 = (parted(r, *shapes)[0] for r in rims)
    return ring(fine, f0, f1, PITCH), (coarse, rims, shapes)


def coarse_ring(coarse, rims, shapes):
    c0, c1 = (parted(r, *shapes)[1] for r in rims)
    return ring(coarse, c0, c1, PITCH // 2)


def call(body, outs, *args, scratch=(), plain=()):
    spaces = [
        pl.BlockSpec(memory_space=pltpu.SMEM if a.dtype == jnp.int32 else pltpu.VMEM) for a in args
    ]
    args = [
        a
        if a.dtype == jnp.int32
        else pltpu.with_memory_space_constraint(a, pltpu.HBM if k in plain else pltpu.VMEM)
        for k, a in enumerate(args)
    ]
    return pl.pallas_call(
        body,
        out_shape=[
            (pltpu.VMEM if len(o) == 2 else o[2] or jax.ShapeDtypeStruct)(o[0], o[1])
            for o in outs
        ],
        in_specs=spaces,
        out_specs=[pl.BlockSpec(memory_space=pltpu.VMEM) for _ in outs],
        scratch_shapes=[pltpu.VMEM(shape, dtype) for shape, dtype in scratch],
        compiler_params=pltpu.CompilerParams(vmem_limit_bytes=24 << 20),
    )(*args)


def group_sum(values, size):
    lanes = values.shape[1]
    lane = lax.broadcasted_iota(jnp.int32, values.shape, 1)
    step = 1
    while step < size:
        after = pltpu.roll(values, lanes - step, 1)
        before = pltpu.roll(values, step, 1)
        values = values + jnp.where((lane & step) == 0, after, before)
        step *= 2
    return values


def wide(row):
    return jnp.broadcast_to(row, (8, row.shape[1]))


def moments(first, second, count, size):
    average = group_sum(wide(first), size) / count
    square = group_sum(wide(second), size) / count
    return average, lax.rsqrt(square - average * average + EPSILON)


def sigmoid(act):
    return 1.0 / (1.0 + jnp.exp(-act))


def in_grid(shape, first_row, first_col, rim, rows, cols):
    row = lax.broadcasted_iota(jnp.int32, shape, 0) + first_row
    place = lax.broadcasted_iota(jnp.int32, shape, 1)
    col = jnp.where(place < shape[1] - rim, place, place - shape[1]) + first_col
    return (row >= 0) & (row < rows) & (col >= 0) & (col < cols)


def over_cells(values):
    lanes = values.shape[-1]
    return jnp.sum(jnp.sum(values.reshape(-1, 8, lanes), axis=0), axis=0, keepdims=True)


def spread(copies, rows):
    for k, row in enumerate(rows):
        copies[:, k, :] = jnp.broadcast_to(row, (copies.shape[0], LANES))


def slab(rims, at, values):
    cells = values.reshape(-1, values.shape[-1])
    for lane in range(0, cells.shape[1], LANES):
        rims[at : at + cells.shape[0]] = cells[:, lane : lane + LANES]
        at += cells.shape[0]
    return at


def field_sums(field, grad, copies, heads, tails):
    slab(heads, slab(heads, 0, field[:FINE_RIM]), grad[:COARSE_RIM])
    slab(tails, slab(tails, 0, field[field.shape[0] - FINE_RIM :]), grad[grad.shape[0] - COARSE_RIM :])
    first = jnp.zeros((8, LANES), jnp.float32)
    second = jnp.zeros((8, LANES), jnp.float32)
    for at in range(0, field.shape[0], 8):
        v = field[at : at + 8].astype(jnp.float32).reshape(-1, 8, LANES)
        first = first + jnp.sum(v, axis=0)
        second = second + jnp.sum(v * v, axis=0)
    spread(
        copies, [jnp.sum(first, axis=0, keepdims=True), jnp.sum(second, axis=0, keepdims=True)]
    )


def relay(received, copies):
    sums = jnp.sum(received[...], axis=0)
    for k in range(copies.shape[1]):
        copies[:, k, :] = jnp.broadcast_to(sums[k : k + 1], (copies.shape[0], LANES))


def fine_forward(count, rows, cols, place, x, sums, gain, weight, projection,
                 center, pooled, coarse, copies, stats, hidden, block):
    tot = jnp.sum(sums[...], axis=0)
    average, inverse = moments(tot[0:1], tot[1:2], count, LANES // GROUPS)
    stats[0] = average
    stats[1] = inverse
    average, scale = average[0:1], inverse[0:1] * gain[...]
    lines = x.shape[0]
    step = 10
    for at in range(0, lines, step):
        v = x[at : at + step].astype(jnp.float32)
        act = (v - average) * scale
        h = act * sigmoid(act)
        keep = in_grid(
            h.shape, at - FINE_RIM + place[0], place[1], FINE_RIM, rows, cols
        )
        h = jnp.where(keep, h, 0.0)
        hidden[at : at + step, :, 0:LANES] = pltpu.roll(h, 1, 1).astype(jnp.bfloat16)
        hidden[at : at + step, :, LANES : 2 * LANES] = h.astype(jnp.bfloat16)
        center[at : at + step] = h.astype(jnp.bfloat16)
        hidden[at : at + step, :, 2 * LANES :] = pltpu.roll(h, PITCH - 1, 1).astype(jnp.bfloat16)
    step = (lines - 2) // 4
    for at in range(0, lines - 2, step):
        acc = x[at + 1 : at + 1 + step].astype(jnp.float32).reshape(step * PITCH, LANES)
        conv = jnp.zeros_like(acc)
        for tap in range(3):
            conv = conv + jnp.dot(
                hidden[at + tap : at + tap + step].reshape(step * PITCH, 3 * LANES),
                weight[tap],
                preferred_element_type=jnp.float32,
            )
        block[at * PITCH : (at + step) * PITCH] = (
            (acc + conv).astype(jnp.bfloat16).astype(jnp.float32)
        )
    half = PITCH // 2
    step = (lines - 2) // 4
    first = jnp.zeros((1, coarse.shape[1]), jnp.float32)
    second = jnp.zeros((1, coarse.shape[1]), jnp.float32)
    for at in range(0, (lines - 2) // 2, step):
        size = 2 * step * half
        pair = block[pl.ds(2 * at * PITCH, size, stride=2), :] + block[
            pl.ds(2 * at * PITCH + 1, size, stride=2), :
        ]
        mean = 0.25 * jnp.sum(pair.reshape(step, 2, half, LANES), axis=1)
        mean = mean.reshape(step * half, LANES).astype(jnp.bfloat16)
        pooled[at * half : (at + step) * half] = mean
        cells = jnp.dot(mean, projection[...], preferred_element_type=jnp.float32).astype(
            jnp.bfloat16
        )
        coarse[at * half : (at + step) * half] = cells
        own = cells.astype(jnp.float32).reshape(step, half, -1)[:, : half // 2]
        low = 1 if at == 0 else 0
        high = step - 1 if at + step == (lines - 2) // 2 else step
        own = own[low:high]
        first = first + over_cells(own)
        second = second + over_cells(own * own)
    spread(copies, [first[:, :LANES], first[:, LANES:], second[:, :LANES], second[:, LANES:]])


def coarse_transpose(grad, weight, fine_weight, out, fine_out, shifted):
    for tap in range(9):
        block = fine_weight[tap].astype(jnp.float32).T.astype(jnp.bfloat16)
        fine_out[tap // 3, tap % 3 * LANES : (tap % 3 + 1) * LANES] = block
    half = PITCH // 2
    lines = grad.shape[0]
    step = lines // 4
    for at in range(0, lines, step):
        g = grad[at : at + step].astype(jnp.float32)
        shifted[0, at : at + step] = pltpu.roll(g, half - 1, 1).astype(jnp.bfloat16)
        shifted[1, at : at + step] = grad[at : at + step]
        shifted[2, at : at + step] = pltpu.roll(g, 1, 1).astype(jnp.bfloat16)
    step = (lines - 2) // 2
    for at in range(0, lines - 2, step):
        acc = jnp.zeros((step * half, weight.shape[2]), jnp.float32)
        for row_tap in range(3):
            for col_tap in range(3):
                begin = at + 2 - row_tap
                acc = acc + lax.dot_general(
                    shifted[col_tap, begin : begin + step].reshape(step * half, -1),
                    weight[row_tap, col_tap],
                    (((1,), (1,)), ((), ())),
                    preferred_element_type=jnp.float32,
                )
        out[at * half : (at + step) * half] = acc


def coarse_middle(count, rows, cols, place, sums, coarse, pre, gain,
                  hidden, dnorm, copies, stats):
    tot = jnp.sum(sums[...], axis=0)
    average, inverse = moments(
        jnp.concatenate([tot[0:1], tot[1:2]], axis=1),
        jnp.concatenate([tot[2:3], tot[3:4]], axis=1),
        count,
        2 * LANES // GROUPS,
    )
    stats[0] = average
    stats[1] = inverse
    average, inverse = average[0:1], inverse[0:1]
    half = PITCH // 2
    lines = coarse.shape[0] // half
    channels = coarse.shape[1]
    step = lines // 2
    first = jnp.zeros((1, channels), jnp.float32)
    second = jnp.zeros((1, channels), jnp.float32)
    for at in range(0, lines, step):
        span = slice(at * half, (at + step) * half)
        normed = (coarse[span].astype(jnp.float32) - average) * inverse
        act = normed * gain[...]
        sigma = sigmoid(act)
        h = (act * sigma).reshape(step, half, channels)
        h = jnp.where(
            in_grid(h.shape, at - 1 + place[2], place[3], COARSE_RIM, rows, cols), h, 0.0
        )
        hidden[at : at + step] = h.astype(jnp.bfloat16)
        dact = pre[span] * (sigma * (1.0 + act * (1.0 - sigma)))
        dn = dact * gain[...]
        dnorm[span] = dn
        low = 1 if at == 0 else 0
        high = step - 1 if at + step == lines else step
        own = slice(low, high), slice(0, half // 2)
        first = first + over_cells(dn.reshape(step, half, channels)[own])
        second = second + over_cells((dact * normed).reshape(step, half, channels)[own])
    spread(copies, [first[:, :LANES], first[:, LANES:], second[:, :LANES], second[:, LANES:]])


def coarse_rest(center, coarse, grad, weight, out, rows_out, hidden):
    half = PITCH // 2
    height = out.shape[0]
    channels = out.shape[2]
    step = center.shape[0] // 2
    for at in range(0, center.shape[0], step):
        h = center[at : at + step].astype(jnp.float32)
        hidden[at : at + step, :, 0:channels] = pltpu.roll(h, 1, 1).astype(jnp.bfloat16)
        hidden[at : at + step, :, channels : 2 * channels] = center[at : at + step]
        hidden[at : at + step, :, 2 * channels :] = pltpu.roll(h, half - 1, 1).astype(jnp.bfloat16)
    step = height // 2
    for at in range(0, height, step):
        acc = coarse[(at + 1) * half : (at + 1 + step) * half].astype(jnp.float32)
        conv = jnp.zeros_like(acc)
        for tap in range(3):
            conv = conv + jnp.dot(
                hidden[at + tap : at + tap + step].reshape(step * half, 3 * channels),
                weight[tap],
                preferred_element_type=jnp.float32,
            )
        out[at : at + step] = (acc + conv).reshape(step, half, channels)[:, : half // 2].astype(
            jnp.bfloat16
        )
    g = grad[2 : 2 + height].astype(jnp.float32)
    own = lax.broadcasted_iota(jnp.int32, g.shape, 1) < half // 2
    g = jnp.where(own, g, 0.0).astype(jnp.bfloat16).reshape(height * half, channels)
    tall = 9 * channels
    for tap in range(3):
        k = lax.dot_general(
            hidden[tap : tap + height].reshape(height * half, 3 * channels),
            g,
            (((0,), (0,)), ((), ())),
            preferred_element_type=jnp.float32,
        ).astype(jnp.bfloat16)
        at = tap * 3 * channels
        rows_out[at : at + 3 * channels] = k[:, :LANES]
        rows_out[tall + at : tall + at + 3 * channels] = k[:, LANES:]


def fine_backward(coarse_count, rows, cols, place, sums, coarse, pooled, grad, dnorm, stats_c,
                  gain_c, projection, weight_t, x, hidden, stats_f, gain_f, rows_in,
                  rows_out, gain_c_grad, partial, up, shifted, taps):
    rows_out[0 : rows_in.shape[0]] = rows_in[...]
    tot = jnp.sum(sums[...], axis=0)
    first = jnp.concatenate([tot[0:1], tot[1:2]], axis=1)
    second = jnp.concatenate([tot[2:3], tot[3:4]], axis=1)
    gain_c_grad[...] = second
    size = 2 * LANES // GROUPS
    a_sum = group_sum(wide(first), size)[0:1] / coarse_count
    b_sum = group_sum(wide(second * gain_c[...]), size)[0:1] / coarse_count
    average, inverse = stats_c[0, 0:1], stats_c[1, 0:1]
    half = PITCH // 2
    lines = coarse.shape[0] // half
    channels = coarse.shape[1]
    height = 2 * (lines - 2)
    step = lines // 2
    proj_grad = jnp.zeros((LANES, channels), jnp.float32)
    for at in range(0, lines, step):
        span = slice(at * half, (at + step) * half)
        normed = (coarse[span].astype(jnp.float32) - average) * inverse
        g = grad[at + 1 : at + 1 + step].astype(jnp.float32).reshape(step * half, channels)
        d = g + inverse * (dnorm[span] - a_sum - normed * b_sum)
        d = d.reshape(step, half, channels)
        d = jnp.where(
            in_grid(d.shape, at - 1 + place[2], place[3], COARSE_RIM, rows, cols), d, 0.0
        )
        line = lax.broadcasted_iota(jnp.int32, d.shape, 0) + at
        spot = lax.broadcasted_iota(jnp.int32, d.shape, 1)
        own = (line >= 1) & (line < lines - 1) & (spot < half // 2)
        own = jnp.where(own, d, 0.0).astype(jnp.bfloat16).reshape(step * half, channels)
        d = d.astype(jnp.bfloat16).reshape(step * half, channels)
        proj_grad = proj_grad + lax.dot_general(
            pooled[span], own, (((0,), (0,)), ((), ())), preferred_element_type=jnp.float32
        )
        small = lax.dot_general(
            d, projection[...], (((1,), (1,)), ((), ())), preferred_element_type=jnp.float32
        )
        small = (small * 0.25).astype(jnp.bfloat16).astype(jnp.float32)
        up[pl.ds(at * PITCH, step * half, stride=2), :] = small
        up[pl.ds(at * PITCH + 1, step * half, stride=2), :] = small
    for at in range(0, lines, step):
        u = up[at * PITCH : (at + step) * PITCH].reshape(step, PITCH, LANES)
        shifted[at : at + step, :, 0:LANES] = pltpu.roll(u, PITCH - 1, 1).astype(jnp.bfloat16)
        shifted[at : at + step, :, LANES : 2 * LANES] = u.astype(jnp.bfloat16)
        shifted[at : at + step, :, 2 * LANES :] = pltpu.roll(u, 1, 1).astype(jnp.bfloat16)
    width = PITCH // 2
    for tap in range(3):
        for at in range(0, lines, step):
            y = jnp.dot(
                shifted[at : at + step, 0:width, :].reshape(step * width, 3 * LANES),
                weight_t[tap],
                preferred_element_type=jnp.float32,
            )
            taps[tap, at : at + step] = y.reshape(step, width, LANES)
    average, inverse = stats_f[0, 0:1], stats_f[1, 0:1]
    first = jnp.zeros((1, LANES), jnp.float32)
    second = jnp.zeros((1, LANES), jnp.float32)
    step = 8
    for at in range(0, lines - 2, step):
        even = taps[0, at + 1 : at + 1 + step] + taps[1, at + 1 : at + 1 + step] + taps[
            2, at : at + step
        ]
        odd = taps[0, at + 2 : at + 2 + step] + taps[1, at + 1 : at + 1 + step] + taps[
            2, at + 1 : at + 1 + step
        ]
        both = jnp.stack([even, odd], axis=1).reshape(2 * step, width, LANES)
        begin = FINE_RIM + 2 * at
        v = x[begin : begin + 2 * step, 0:width, :].astype(jnp.float32)
        normed = (v - average) * inverse
        act = normed * gain_f[...]
        sigma = sigmoid(act)
        dact = both * (sigma * (1.0 + act * (1.0 - sigma)))
        dn = dact * gain_f[...]
        first = first + over_cells(dn)
        second = second + over_cells(dact * normed)
        u = up[(at + 1) * PITCH : (at + 1 + step) * PITCH].reshape(step, PITCH, LANES)[:, 0:width]
        u = jnp.broadcast_to(u[:, None], (step, 2, width, LANES)).reshape(2 * step, width, LANES)
        partial[2 * at : 2 * at + 2 * step] = u + inverse * dn
    for at in range(1, lines - 1, step):
        u = up[at * PITCH : (at + step) * PITCH].reshape(step, PITCH, LANES)
        own = lax.broadcasted_iota(jnp.int32, u.shape, 1) < width
        u = jnp.where(own, u, 0.0)
        shifted[at : at + step, :, 0:LANES] = pltpu.roll(u, PITCH - 1, 1).astype(jnp.bfloat16)
        shifted[at : at + step, :, LANES : 2 * LANES] = u.astype(jnp.bfloat16)
        shifted[at : at + step, :, 2 * LANES :] = pltpu.roll(u, 1, 1).astype(jnp.bfloat16)
    d = shifted[1 : lines - 1]
    d = jnp.broadcast_to(d[:, None], (lines - 2, 2) + d.shape[1:])
    d = d.reshape(height * PITCH, 3 * LANES)
    at = 18 * channels
    for tap in range(3):
        begin = FINE_RIM - 1 + tap
        k = lax.dot_general(
            hidden[begin : begin + height].reshape(height * PITCH, LANES),
            d,
            (((0,), (0,)), ((), ())),
            preferred_element_type=jnp.float32,
        ).astype(jnp.bfloat16)
        for col_tap in range(3):
            rows_out[at : at + LANES] = k[:, col_tap * LANES : (col_tap + 1) * LANES]
            at += LANES
    proj_grad = proj_grad.astype(jnp.bfloat16)
    rows_out[at : at + LANES] = proj_grad[:, :LANES]
    rows_out[at + LANES : at + 2 * LANES] = proj_grad[:, LANES:]
    at += 2 * LANES
    spare = rows_out.shape[0] - at
    small = jnp.concatenate([first, second], axis=0)
    rows_out[at:] = jnp.concatenate(
        [jnp.zeros((spare - 8, LANES), jnp.float32), split(small)], axis=0
    ).astype(jnp.bfloat16)


def finish(fine_count, rows, partial, x, stats, gain,
           field_grad, weight_f, gain_f, proj, weight_c):
    count = rows.shape[0]
    small = rows[count - 8 :].astype(jnp.float32)
    small = small[0:2] + small[2:4] + small[4:6]
    first, second = small[0:1], small[1:2]
    gain_f[...] = second
    size = LANES // GROUPS
    a_sum = group_sum(wide(first), size)[0:1] / fine_count
    b_sum = group_sum(wide(second * gain[...]), size)[0:1] / fine_count
    average, inverse = stats[0, 0:1], stats[1, 0:1]
    height, width, _ = partial.shape
    step = 16
    for at in range(0, height, step):
        v = x[FINE_RIM + at : FINE_RIM + at + step, 0:width, :].astype(jnp.float32)
        normed = (v - average) * inverse
        field_grad[at : at + step] = (
            partial[at : at + step] - inverse * (a_sum + normed * b_sum)
        ).astype(jnp.bfloat16)
    tall = weight_c.shape[0]
    weight_c[:, :LANES] = rows[0:tall].astype(jnp.float32)
    weight_c[:, LANES:] = rows[tall : 2 * tall].astype(jnp.float32)
    at = 2 * tall
    weight_f[...] = rows[at : at + weight_f.shape[0]].astype(jnp.float32)
    at += weight_f.shape[0]
    proj[:, :LANES] = rows[at : at + LANES].astype(jnp.float32)
    proj[:, LANES:] = rows[at + LANES : at + 2 * LANES].astype(jnp.float32)


def gathered(copies, late=None):
    far = lax.axis_size(FAR)
    received = lax.all_to_all(copies, NEAR, 0, 0, tiled=True)
    (copies,) = call(relay, [((far,) + copies.shape[1:], jnp.float32, None)], received)
    if late is not None:
        copies, late = lax.optimization_barrier((copies, late))
    sums = lax.all_to_all(copies, FAR, 0, 0, tiled=True)
    return sums if late is None else (sums, late)


def split(small):
    high = small.astype(jnp.bfloat16).astype(jnp.float32)
    middle = (small - high).astype(jnp.bfloat16).astype(jnp.float32)
    low = small - high - middle
    return jnp.concatenate([high, middle, low, jnp.zeros_like(low)], axis=0)


def add_up(stage, place, pieces, out, *scratch):
    rows = pieces.shape[1]
    step = 256 if rows % 256 == 0 else rows
    pitch = out.shape[-2]
    for at in range(0, rows, step):
        sums = pieces[0, at : at + step].astype(jnp.float32)
        for k in range(1, pieces.shape[0]):
            sums = sums + pieces[k, at : at + step].astype(jnp.float32)
        if at + step == rows:
            last = sums[step - 8 :]
            tail = split(last[0:2] + last[2:4] + last[4:6])
            tail = jnp.where(place[4 + stage] == 1, tail, last)
            sums = jnp.concatenate([sums[: step - 8], tail], axis=0)
        if scratch:
            scratch[0][at : at + step] = sums
        elif len(out.shape) == 3:
            for k in range(out.shape[0]):
                out[k] = sums.astype(jnp.bfloat16)
        else:
            out[at : at + step] = sums.astype(jnp.bfloat16)
    if scratch:
        for k in range(out.shape[0]):
            out[k] = scratch[0][k * pitch : (k + 1) * pitch].astype(jnp.bfloat16)


def gradient_totals(part, place):
    for stage, axes in enumerate(STAGES):
        count = lax.axis_size(axes)
        pieces = lax.all_to_all(part.reshape(count, -1, LANES), axes, 0, 0, tiled=True)
        rows = pieces.shape[1]
        kernel = functools.partial(add_up, stage)
        if stage == 0:
            (part,) = call(kernel, [((rows, LANES), jnp.bfloat16, None)], place, pieces)
        elif stage == 1:
            pitch = rows // lax.axis_size(STAGES[2])
            (part,) = call(
                kernel,
                [((rows // pitch, pitch, LANES), jnp.bfloat16, None)],
                place,
                pieces,
                scratch=[((rows, LANES), jnp.float32)],
            )
        else:
            (part,) = call(kernel, [((count, rows, LANES), jnp.bfloat16, None)], place, pieces)
    part = lax.all_to_all(part, STAGES[2], 0, 0, tiled=True).reshape(-1, LANES)
    for axes in STAGES[1::-1]:
        count = lax.axis_size(axes)
        copies = jnp.broadcast_to(part[None], (count,) + part.shape)
        part = lax.all_to_all(copies, axes, 0, 0, tiled=True).reshape(-1, LANES)
    return part


def on_device(field, cotangent, gain_fine, weight_fine, projection, gain_coarse, weight_coarse):
    height, width, chan_fine = field.shape
    chan_coarse = projection.shape[1]
    half_h, half_w = (height // 2, width // 2)
    cells_all = height * width * lax.axis_size(GY_GX)
    fine_count = cells_all * (chan_fine // GROUPS)
    coarse_count = cells_all // 4 * (chan_coarse // GROUPS)
    rows, cols = height * lax.axis_size(GY), width * lax.axis_size(GX)
    f32, bf16 = jnp.float32, jnp.bfloat16
    near = lax.axis_size(NEAR)
    row, col = lax.axis_index(GY), lax.axis_index(GX)
    holds, held = [], jnp.int32(1)
    for axes in STAGES:
        held = held * (lax.axis_index(axes) == lax.axis_size(axes) - 1)
        holds.append(held)
    place = jnp.stack([row * height, col * width, row * half_h, col * half_w] + holds)
    place = place.astype(jnp.int32)
    gain_f, gain_c = gain_fine.reshape(1, -1), gain_coarse.reshape(1, -1)

    slabs = FINE_RIM * width + COARSE_RIM * half_w * chan_coarse // LANES
    copies, heads, tails = call(
        field_sums,
        [((near, 2, LANES), f32, None), ((slabs, LANES), bf16, None), ((slabs, LANES), bf16, None)],
        field,
        cotangent,
        plain=(0, 1),
    )
    sums = gathered(copies)
    x, (tall, rims, shapes) = with_rims(field, cotangent, heads, tails)
    lines = half_h + 2
    cells = lines * PITCH // 2
    hidden_f, pooled, coarse, copies, stats_f = call(
        functools.partial(fine_forward, fine_count, rows, cols),
        [
            (x.shape, bf16, HBM),
            ((cells, chan_fine), bf16, HBM),
            ((cells, chan_coarse), bf16),
            ((near, 4, LANES), f32, None),
            ((2, 8, chan_fine), f32),
        ],
        place,
        x,
        sums,
        gain_f,
        weight_fine.reshape(3, 3 * chan_fine, chan_fine),
        projection,
        scratch=[
            (x.shape[:2] + (3 * chan_fine,), bf16),
            ((2 * lines * PITCH + 8, chan_fine), f32),
        ],
    )
    sums, (tall, rims) = gathered(copies, (tall, rims))
    grad = coarse_ring(tall, rims, shapes)
    pre, weight_t = call(
        coarse_transpose,
        [((cells, chan_coarse), f32), ((3, 3 * chan_fine, chan_fine), bf16, HBM)],
        grad,
        weight_coarse,
        weight_fine.reshape(9, chan_fine, chan_fine),
        plain=(1, 2),
        scratch=[((3,) + grad.shape, bf16)],
    )
    hidden_c, dnorm, copies, stats_c = call(
        functools.partial(coarse_middle, coarse_count, rows // 2, cols // 2),
        [
            ((lines, PITCH // 2, chan_coarse), bf16, HBM),
            ((cells, chan_coarse), f32, HBM),
            ((near, 4, LANES), f32, None),
            ((2, 8, chan_coarse), f32),
        ],
        place,
        sums,
        coarse,
        pre,
        gain_c,
    )
    sums = gathered(copies)
    used = 18 * chan_coarse + 9 * chan_fine + chan_coarse
    used += -(used + 8) % (4 * lax.axis_size(GY_GX)) + 8
    coarse_output, parts = call(
        coarse_rest,
        [((half_h, half_w, chan_coarse), bf16, None), ((18 * chan_coarse, LANES), bf16)],
        hidden_c,
        coarse,
        grad,
        weight_coarse.reshape(3, 3 * chan_coarse, chan_coarse),
        scratch=[((lines, PITCH // 2, 3 * chan_coarse), bf16)],
        plain=(0, 3),
    )
    parts, coarse_gain_grad, partial = call(
        functools.partial(fine_backward, coarse_count, rows // 2, cols // 2),
        [
            ((used, LANES), bf16, None),
            ((1, chan_coarse), f32, None),
            ((height, width, chan_fine), f32),
        ],
        place,
        sums,
        coarse,
        pooled,
        grad,
        dnorm,
        stats_c,
        gain_c,
        projection,
        weight_t,
        x,
        hidden_f,
        stats_f,
        gain_f,
        parts,
        scratch=[
            ((lines * PITCH + 8, chan_fine), f32),
            ((lines, PITCH, 3 * chan_fine), bf16),
            ((3, lines, PITCH // 2, chan_fine), f32),
        ],
        plain=(3, 5, 8, 9, 11),
    )
    totals = gradient_totals(parts, place)
    field_grad, fine_weight_grad, fine_gain_grad, projection_grad, coarse_weight_grad = call(
        functools.partial(finish, fine_count),
        [
            ((height, width, chan_fine), bf16, None),
            ((9 * chan_fine, chan_fine), f32, None),
            ((1, chan_fine), f32, None),
            ((chan_fine, chan_coarse), f32, None),
            ((9 * chan_coarse, chan_coarse), f32, None),
        ],
        totals,
        partial,
        x,
        stats_f,
        gain_f,
    )
    return (
        coarse_output,
        field_grad,
        fine_weight_grad.reshape(weight_fine.shape),
        fine_gain_grad.reshape(-1),
        projection_grad,
        coarse_weight_grad.reshape(weight_coarse.shape),
        coarse_gain_grad.reshape(-1),
    )


def solution(mesh):
    finer = Mesh(mesh.devices.reshape(2, 8, 2, 8, 2), GY_GX)
    in_specs = (P(GY, GX, None), P(GY, GX, None), P(), P(), P(), P(), P())
    out_specs = (P(GY, GX, None), P(GY, GX, None), P(), P(), P(), P(), P())

    return jax.shard_map(
        on_device, mesh=finer, in_specs=in_specs, out_specs=out_specs, check_vma=False
    )
```

```python
import functools

import jax
import jax.numpy as jnp
from jax import lax
from jax.experimental import pallas as pl
from jax.experimental.pallas import tpu as pltpu
from jax.sharding import Mesh
from jax.sharding import PartitionSpec as P


GROUPS = 32
GY = ("gy_0", "gy_1")
GX = ("gx_0", "gx_1", "gx_2")
GY_GX = GY + GX
NEAR = ("gx_1", "gx_2")
FAR = ("gx_0", "gy_0", "gy_1")
STAGES = (("gx_2",), ("gx_0", "gy_0"), ("gx_1", "gy_1"))
LANES = 128
EPSILON = 1e-05

HBM = pltpu.HBM
PITCH = 32
FINE_RIM = 3
COARSE_RIM = 2


def is_even(axis):
    return lax.axis_index(axis) % 2 == 0


def swap(inner, outer, axis):
    count = lax.axis_size(axis)
    mate = lax.ppermute(inner, axis, [(i, i ^ 1) for i in range(count)])
    pairs = [(i, i + 1) for i in range(1, count - 1, 2)]
    other = lax.ppermute(outer, axis, pairs + [(j, i) for i, j in pairs])
    even = is_even(axis)
    return jnp.where(even, other, mate), jnp.where(even, mate, other)


def joined(fine, coarse):
    cells = coarse.reshape(-1, coarse.shape[2])
    return jnp.concatenate(
        [fine.reshape(-1, LANES)] + [cells[:, k : k + LANES] for k in range(0, cells.shape[1], LANES)]
    )


def parted(rims, fine, coarse):
    size = fine[0] * fine[1]
    cells = coarse[0] * coarse[1]
    halves = [rims[size + k * cells : size + (k + 1) * cells] for k in range(coarse[2] // LANES)]
    return rims[:size].reshape(fine), jnp.concatenate(halves, axis=1).reshape(coarse)


def ring(own, left, right, pitch):
    rows, cols, channels = own.shape
    gap = pitch - cols - left.shape[1] - right.shape[1]
    return jnp.concatenate([own, right, jnp.zeros((rows, gap, channels), own.dtype), left], axis=1)


def with_rims(fine, coarse, inner, outer):
    shapes = (FINE_RIM,) + fine.shape[1:], (COARSE_RIM,) + coarse.shape[1:]
    rims = swap(inner, outer, GY)
    (f0, c0), (f1, c1) = (parted(r, *shapes) for r in rims)
    fine = jnp.concatenate([f0, fine, f1])
    coarse = jnp.concatenate([c0, coarse, c1])
    shapes = (
        (fine.shape[0], FINE_RIM, fine.shape[2]),
        (coarse.shape[0], COARSE_RIM, coarse.shape[2]),
    )
    heads = joined(fine[:, :FINE_RIM], coarse[:, :COARSE_RIM])
    tails = joined(fine[:, -FINE_RIM:], coarse[:, -COARSE_RIM:])
    even = is_even(GX)
    inner, outer = jnp.where(even, tails, heads), jnp.where(even, heads, tails)
    rims = swap(inner, outer, GX)
    f0, f1 = (parted(r, *shapes)[0] for r in rims)
    return ring(fine, f0, f1, PITCH), (coarse, rims, shapes)


def coarse_ring(coarse, rims, shapes):
    c0, c1 = (parted(r, *shapes)[1] for r in rims)
    return ring(coarse, c0, c1, PITCH // 2)


def call(body, outs, *args, scratch=(), plain=()):
    spaces = [
        pl.BlockSpec(memory_space=pltpu.SMEM if a.dtype == jnp.int32 else pltpu.VMEM) for a in args
    ]
    args = [
        a
        if a.dtype == jnp.int32
        else pltpu.with_memory_space_constraint(a, pltpu.HBM if k in plain else pltpu.VMEM)
        for k, a in enumerate(args)
    ]
    return pl.pallas_call(
        body,
        out_shape=[
            (pltpu.VMEM if len(o) == 2 else o[2] or jax.ShapeDtypeStruct)(o[0], o[1])
            for o in outs
        ],
        in_specs=spaces,
        out_specs=[pl.BlockSpec(memory_space=pltpu.VMEM) for _ in outs],
        scratch_shapes=[pltpu.VMEM(shape, dtype) for shape, dtype in scratch],
        compiler_params=pltpu.CompilerParams(vmem_limit_bytes=24 << 20),
    )(*args)


def group_sum(values, size):
    lanes = values.shape[1]
    lane = lax.broadcasted_iota(jnp.int32, values.shape, 1)
    step = 1
    while step < size:
        after = pltpu.roll(values, lanes - step, 1)
        before = pltpu.roll(values, step, 1)
        values = values + jnp.where((lane & step) == 0, after, before)
        step *= 2
    return values


def wide(row):
    return jnp.broadcast_to(row, (8, row.shape[1]))


def moments(first, second, count, size):
    average = group_sum(wide(first), size) / count
    square = group_sum(wide(second), size) / count
    return average, lax.rsqrt(square - average * average + EPSILON)


def sigmoid(act):
    return 1.0 / (1.0 + jnp.exp(-act))


def in_grid(shape, first_row, first_col, rim, rows, cols):
    row = lax.broadcasted_iota(jnp.int32, shape, 0) + first_row
    place = lax.broadcasted_iota(jnp.int32, shape, 1)
    col = jnp.where(place < shape[1] - rim, place, place - shape[1]) + first_col
    return (row >= 0) & (row < rows) & (col >= 0) & (col < cols)


def over_cells(values):
    lanes = values.shape[-1]
    return jnp.sum(jnp.sum(values.reshape(-1, 8, lanes), axis=0), axis=0, keepdims=True)


def spread(copies, rows):
    for k, row in enumerate(rows):
        copies[:, k, :] = jnp.broadcast_to(row, (copies.shape[0], LANES))


def slab(rims, at, values):
    cells = values.reshape(-1, values.shape[-1])
    for lane in range(0, cells.shape[1], LANES):
        rims[at : at + cells.shape[0]] = cells[:, lane : lane + LANES]
        at += cells.shape[0]
    return at


def field_sums(field, grad, copies, inner, outer):
    even = is_even(GY)
    low, high = field.shape[0] - FINE_RIM, grad.shape[0] - COARSE_RIM

    def write(heads, tails):
        slab(heads, slab(heads, 0, field[:FINE_RIM]), grad[:COARSE_RIM])
        slab(tails, slab(tails, 0, field[low:]), grad[high:])

    pl.when(even)(lambda: write(outer, inner))
    pl.when(jnp.logical_not(even))(lambda: write(inner, outer))
    first = jnp.zeros((8, LANES), jnp.float32)
    second = jnp.zeros((8, LANES), jnp.float32)
    for at in range(0, field.shape[0], 8):
        v = field[at : at + 8].astype(jnp.float32).reshape(-1, 8, LANES)
        first = first + jnp.sum(v, axis=0)
        second = second + jnp.sum(v * v, axis=0)
    spread(
        copies, [jnp.sum(first, axis=0, keepdims=True), jnp.sum(second, axis=0, keepdims=True)]
    )


def relay(received, copies):
    sums = jnp.sum(received[...], axis=0)
    for k in range(copies.shape[1]):
        copies[:, k, :] = jnp.broadcast_to(sums[k : k + 1], (copies.shape[0], LANES))


def fine_forward(count, rows, cols, place, x, sums, gain, weight, projection,
                 center, pooled, coarse, copies, stats, hidden, block):
    tot = jnp.sum(sums[...], axis=0)
    average, inverse = moments(tot[0:1], tot[1:2], count, LANES // GROUPS)
    stats[0] = average
    stats[1] = inverse
    average, scale = average[0:1], inverse[0:1] * gain[...]
    lines = x.shape[0]
    step = 10
    for at in range(0, lines, step):
        v = x[at : at + step].astype(jnp.float32)
        act = (v - average) * scale
        h = act * sigmoid(act)
        keep = in_grid(
            h.shape, at - FINE_RIM + place[0], place[1], FINE_RIM, rows, cols
        )
        h = jnp.where(keep, h, 0.0)
        hidden[at : at + step, :, 0:LANES] = pltpu.roll(h, 1, 1).astype(jnp.bfloat16)
        hidden[at : at + step, :, LANES : 2 * LANES] = h.astype(jnp.bfloat16)
        center[at : at + step] = h.astype(jnp.bfloat16)
        hidden[at : at + step, :, 2 * LANES :] = pltpu.roll(h, PITCH - 1, 1).astype(jnp.bfloat16)
    step = (lines - 2) // 4
    for at in range(0, lines - 2, step):
        acc = x[at + 1 : at + 1 + step].astype(jnp.float32).reshape(step * PITCH, LANES)
        conv = jnp.zeros_like(acc)
        for tap in range(3):
            conv = conv + jnp.dot(
                hidden[at + tap : at + tap + step].reshape(step * PITCH, 3 * LANES),
                weight[tap],
                preferred_element_type=jnp.float32,
            )
        block[at * PITCH : (at + step) * PITCH] = (
            (acc + conv).astype(jnp.bfloat16).astype(jnp.float32)
        )
    half = PITCH // 2
    step = (lines - 2) // 4
    first = jnp.zeros((1, coarse.shape[1]), jnp.float32)
    second = jnp.zeros((1, coarse.shape[1]), jnp.float32)
    for at in range(0, (lines - 2) // 2, step):
        size = 2 * step * half
        pair = block[pl.ds(2 * at * PITCH, size, stride=2), :] + block[
            pl.ds(2 * at * PITCH + 1, size, stride=2), :
        ]
        mean = 0.25 * jnp.sum(pair.reshape(step, 2, half, LANES), axis=1)
        mean = mean.reshape(step * half, LANES).astype(jnp.bfloat16)
        pooled[at * half : (at + step) * half] = mean
        cells = jnp.dot(mean, projection[...], preferred_element_type=jnp.float32).astype(
            jnp.bfloat16
        )
        coarse[at * half : (at + step) * half] = cells
        own = cells.astype(jnp.float32).reshape(step, half, -1)[:, : half // 2]
        low = 1 if at == 0 else 0
        high = step - 1 if at + step == (lines - 2) // 2 else step
        own = own[low:high]
        first = first + over_cells(own)
        second = second + over_cells(own * own)
    spread(copies, [first[:, :LANES], first[:, LANES:], second[:, :LANES], second[:, LANES:]])


def coarse_transpose(grad, weight, fine_weight, out, fine_out, shifted):
    for tap in range(9):
        block = fine_weight[tap].astype(jnp.float32).T.astype(jnp.bfloat16)
        fine_out[tap // 3, tap % 3 * LANES : (tap % 3 + 1) * LANES] = block
    half = PITCH // 2
    lines = grad.shape[0]
    step = lines // 4
    for at in range(0, lines, step):
        g = grad[at : at + step].astype(jnp.float32)
        shifted[0, at : at + step] = pltpu.roll(g, half - 1, 1).astype(jnp.bfloat16)
        shifted[1, at : at + step] = grad[at : at + step]
        shifted[2, at : at + step] = pltpu.roll(g, 1, 1).astype(jnp.bfloat16)
    step = (lines - 2) // 2
    for at in range(0, lines - 2, step):
        acc = jnp.zeros((step * half, weight.shape[2]), jnp.float32)
        for row_tap in range(3):
            for col_tap in range(3):
                begin = at + 2 - row_tap
                acc = acc + lax.dot_general(
                    shifted[col_tap, begin : begin + step].reshape(step * half, -1),
                    weight[row_tap, col_tap],
                    (((1,), (1,)), ((), ())),
                    preferred_element_type=jnp.float32,
                )
        out[at * half : (at + step) * half] = acc


def coarse_middle(count, rows, cols, place, sums, coarse, pre, gain,
                  hidden, dnorm, copies, stats):
    tot = jnp.sum(sums[...], axis=0)
    average, inverse = moments(
        jnp.concatenate([tot[0:1], tot[1:2]], axis=1),
        jnp.concatenate([tot[2:3], tot[3:4]], axis=1),
        count,
        2 * LANES // GROUPS,
    )
    stats[0] = average
    stats[1] = inverse
    average, inverse = average[0:1], inverse[0:1]
    half = PITCH // 2
    lines = coarse.shape[0] // half
    channels = coarse.shape[1]
    step = lines // 2
    first = jnp.zeros((1, channels), jnp.float32)
    second = jnp.zeros((1, channels), jnp.float32)
    for at in range(0, lines, step):
        span = slice(at * half, (at + step) * half)
        normed = (coarse[span].astype(jnp.float32) - average) * inverse
        act = normed * gain[...]
        sigma = sigmoid(act)
        h = (act * sigma).reshape(step, half, channels)
        h = jnp.where(
            in_grid(h.shape, at - 1 + place[2], place[3], COARSE_RIM, rows, cols), h, 0.0
        )
        hidden[at : at + step] = h.astype(jnp.bfloat16)
        dact = pre[span] * (sigma * (1.0 + act * (1.0 - sigma)))
        dn = dact * gain[...]
        dnorm[span] = dn
        low = 1 if at == 0 else 0
        high = step - 1 if at + step == lines else step
        own = slice(low, high), slice(0, half // 2)
        first = first + over_cells(dn.reshape(step, half, channels)[own])
        second = second + over_cells((dact * normed).reshape(step, half, channels)[own])
    spread(copies, [first[:, :LANES], first[:, LANES:], second[:, :LANES], second[:, LANES:]])


def coarse_rest(center, coarse, grad, weight, out, rows_out, hidden):
    half = PITCH // 2
    height = out.shape[0]
    channels = out.shape[2]
    step = center.shape[0] // 2
    for at in range(0, center.shape[0], step):
        h = center[at : at + step].astype(jnp.float32)
        hidden[at : at + step, :, 0:channels] = pltpu.roll(h, 1, 1).astype(jnp.bfloat16)
        hidden[at : at + step, :, channels : 2 * channels] = center[at : at + step]
        hidden[at : at + step, :, 2 * channels :] = pltpu.roll(h, half - 1, 1).astype(jnp.bfloat16)
    step = height // 2
    for at in range(0, height, step):
        acc = coarse[(at + 1) * half : (at + 1 + step) * half].astype(jnp.float32)
        conv = jnp.zeros_like(acc)
        for tap in range(3):
            conv = conv + jnp.dot(
                hidden[at + tap : at + tap + step].reshape(step * half, 3 * channels),
                weight[tap],
                preferred_element_type=jnp.float32,
            )
        out[at : at + step] = (acc + conv).reshape(step, half, channels)[:, : half // 2].astype(
            jnp.bfloat16
        )
    g = grad[2 : 2 + height].astype(jnp.float32)
    own = lax.broadcasted_iota(jnp.int32, g.shape, 1) < half // 2
    g = jnp.where(own, g, 0.0).astype(jnp.bfloat16).reshape(height * half, channels)
    tall = 9 * channels
    for tap in range(3):
        k = lax.dot_general(
            hidden[tap : tap + height].reshape(height * half, 3 * channels),
            g,
            (((0,), (0,)), ((), ())),
            preferred_element_type=jnp.float32,
        ).astype(jnp.bfloat16)
        at = tap * 3 * channels
        rows_out[at : at + 3 * channels] = k[:, :LANES]
        rows_out[tall + at : tall + at + 3 * channels] = k[:, LANES:]


def fine_backward(coarse_count, rows, cols, place, sums, coarse, pooled, grad, dnorm, stats_c,
                  gain_c, projection, weight_t, x, hidden, stats_f, gain_f, rows_in,
                  rows_out, gain_c_grad, partial, up, shifted, taps):
    rows_out[0 : rows_in.shape[0]] = rows_in[...]
    tot = jnp.sum(sums[...], axis=0)
    first = jnp.concatenate([tot[0:1], tot[1:2]], axis=1)
    second = jnp.concatenate([tot[2:3], tot[3:4]], axis=1)
    gain_c_grad[...] = second
    size = 2 * LANES // GROUPS
    a_sum = group_sum(wide(first), size)[0:1] / coarse_count
    b_sum = group_sum(wide(second * gain_c[...]), size)[0:1] / coarse_count
    average, inverse = stats_c[0, 0:1], stats_c[1, 0:1]
    half = PITCH // 2
    lines = coarse.shape[0] // half
    channels = coarse.shape[1]
    height = 2 * (lines - 2)
    step = lines // 2
    proj_grad = jnp.zeros((LANES, channels), jnp.float32)
    for at in range(0, lines, step):
        span = slice(at * half, (at + step) * half)
        normed = (coarse[span].astype(jnp.float32) - average) * inverse
        g = grad[at + 1 : at + 1 + step].astype(jnp.float32).reshape(step * half, channels)
        d = g + inverse * (dnorm[span] - a_sum - normed * b_sum)
        d = d.reshape(step, half, channels)
        d = jnp.where(
            in_grid(d.shape, at - 1 + place[2], place[3], COARSE_RIM, rows, cols), d, 0.0
        )
        line = lax.broadcasted_iota(jnp.int32, d.shape, 0) + at
        spot = lax.broadcasted_iota(jnp.int32, d.shape, 1)
        own = (line >= 1) & (line < lines - 1) & (spot < half // 2)
        own = jnp.where(own, d, 0.0).astype(jnp.bfloat16).reshape(step * half, channels)
        d = d.astype(jnp.bfloat16).reshape(step * half, channels)
        proj_grad = proj_grad + lax.dot_general(
            pooled[span], own, (((0,), (0,)), ((), ())), preferred_element_type=jnp.float32
        )
        small = lax.dot_general(
            d, projection[...], (((1,), (1,)), ((), ())), preferred_element_type=jnp.float32
        )
        small = (small * 0.25).astype(jnp.bfloat16).astype(jnp.float32)
        up[pl.ds(at * PITCH, step * half, stride=2), :] = small
        up[pl.ds(at * PITCH + 1, step * half, stride=2), :] = small
    for at in range(0, lines, step):
        u = up[at * PITCH : (at + step) * PITCH].reshape(step, PITCH, LANES)
        shifted[at : at + step, :, 0:LANES] = pltpu.roll(u, PITCH - 1, 1).astype(jnp.bfloat16)
        shifted[at : at + step, :, LANES : 2 * LANES] = u.astype(jnp.bfloat16)
        shifted[at : at + step, :, 2 * LANES :] = pltpu.roll(u, 1, 1).astype(jnp.bfloat16)
    width = PITCH // 2
    for tap in range(3):
        for at in range(0, lines, step):
            y = jnp.dot(
                shifted[at : at + step, 0:width, :].reshape(step * width, 3 * LANES),
                weight_t[tap],
                preferred_element_type=jnp.float32,
            )
            taps[tap, at : at + step] = y.reshape(step, width, LANES)
    average, inverse = stats_f[0, 0:1], stats_f[1, 0:1]
    first = jnp.zeros((1, LANES), jnp.float32)
    second = jnp.zeros((1, LANES), jnp.float32)
    step = 8
    for at in range(0, lines - 2, step):
        even = taps[0, at + 1 : at + 1 + step] + taps[1, at + 1 : at + 1 + step] + taps[
            2, at : at + step
        ]
        odd = taps[0, at + 2 : at + 2 + step] + taps[1, at + 1 : at + 1 + step] + taps[
            2, at + 1 : at + 1 + step
        ]
        both = jnp.stack([even, odd], axis=1).reshape(2 * step, width, LANES)
        begin = FINE_RIM + 2 * at
        v = x[begin : begin + 2 * step, 0:width, :].astype(jnp.float32)
        normed = (v - average) * inverse
        act = normed * gain_f[...]
        sigma = sigmoid(act)
        dact = both * (sigma * (1.0 + act * (1.0 - sigma)))
        dn = dact * gain_f[...]
        first = first + over_cells(dn)
        second = second + over_cells(dact * normed)
        u = up[(at + 1) * PITCH : (at + 1 + step) * PITCH].reshape(step, PITCH, LANES)[:, 0:width]
        u = jnp.broadcast_to(u[:, None], (step, 2, width, LANES)).reshape(2 * step, width, LANES)
        partial[2 * at : 2 * at + 2 * step] = u + inverse * dn
    for at in range(1, lines - 1, step):
        u = up[at * PITCH : (at + step) * PITCH].reshape(step, PITCH, LANES)
        own = lax.broadcasted_iota(jnp.int32, u.shape, 1) < width
        u = jnp.where(own, u, 0.0)
        shifted[at : at + step, :, 0:LANES] = pltpu.roll(u, PITCH - 1, 1).astype(jnp.bfloat16)
        shifted[at : at + step, :, LANES : 2 * LANES] = u.astype(jnp.bfloat16)
        shifted[at : at + step, :, 2 * LANES :] = pltpu.roll(u, 1, 1).astype(jnp.bfloat16)
    d = shifted[1 : lines - 1]
    d = jnp.broadcast_to(d[:, None], (lines - 2, 2) + d.shape[1:])
    d = d.reshape(height * PITCH, 3 * LANES)
    at = 18 * channels
    for tap in range(3):
        begin = FINE_RIM - 1 + tap
        k = lax.dot_general(
            hidden[begin : begin + height].reshape(height * PITCH, LANES),
            d,
            (((0,), (0,)), ((), ())),
            preferred_element_type=jnp.float32,
        ).astype(jnp.bfloat16)
        for col_tap in range(3):
            rows_out[at : at + LANES] = k[:, col_tap * LANES : (col_tap + 1) * LANES]
            at += LANES
    proj_grad = proj_grad.astype(jnp.bfloat16)
    rows_out[at : at + LANES] = proj_grad[:, :LANES]
    rows_out[at + LANES : at + 2 * LANES] = proj_grad[:, LANES:]
    at += 2 * LANES
    spare = rows_out.shape[0] - at
    small = jnp.concatenate([first, second], axis=0)
    rows_out[at:] = jnp.concatenate(
        [jnp.zeros((spare - 8, LANES), jnp.float32), split(small)], axis=0
    ).astype(jnp.bfloat16)


def finish(fine_count, rows, partial, x, stats, gain,
           field_grad, weight_f, gain_f, proj, weight_c):
    count = rows.shape[0]
    small = rows[count - 8 :].astype(jnp.float32)
    small = small[0:2] + small[2:4] + small[4:6]
    first, second = small[0:1], small[1:2]
    gain_f[...] = second
    size = LANES // GROUPS
    a_sum = group_sum(wide(first), size)[0:1] / fine_count
    b_sum = group_sum(wide(second * gain[...]), size)[0:1] / fine_count
    average, inverse = stats[0, 0:1], stats[1, 0:1]
    height, width, _ = partial.shape
    step = 16
    for at in range(0, height, step):
        v = x[FINE_RIM + at : FINE_RIM + at + step, 0:width, :].astype(jnp.float32)
        normed = (v - average) * inverse
        field_grad[at : at + step] = (
            partial[at : at + step] - inverse * (a_sum + normed * b_sum)
        ).astype(jnp.bfloat16)
    tall = weight_c.shape[0]
    weight_c[:, :LANES] = rows[0:tall].astype(jnp.float32)
    weight_c[:, LANES:] = rows[tall : 2 * tall].astype(jnp.float32)
    at = 2 * tall
    weight_f[...] = rows[at : at + weight_f.shape[0]].astype(jnp.float32)
    at += weight_f.shape[0]
    proj[:, :LANES] = rows[at : at + LANES].astype(jnp.float32)
    proj[:, LANES:] = rows[at + LANES : at + 2 * LANES].astype(jnp.float32)


def gathered(copies, late=None):
    far = lax.axis_size(FAR)
    received = lax.all_to_all(copies, NEAR, 0, 0, tiled=True)
    (copies,) = call(relay, [((far,) + copies.shape[1:], jnp.float32, None)], received)
    if late is not None:
        copies, late = lax.optimization_barrier((copies, late))
    sums = lax.all_to_all(copies, FAR, 0, 0, tiled=True)
    return sums if late is None else (sums, late)


def split(small):
    high = small.astype(jnp.bfloat16).astype(jnp.float32)
    middle = (small - high).astype(jnp.bfloat16).astype(jnp.float32)
    low = small - high - middle
    return jnp.concatenate([high, middle, low, jnp.zeros_like(low)], axis=0)


def add_up(stage, place, pieces, out, *scratch):
    rows = pieces.shape[1]
    step = 256 if rows % 256 == 0 else rows
    pitch = out.shape[-2]
    for at in range(0, rows, step):
        sums = pieces[0, at : at + step].astype(jnp.float32)
        for k in range(1, pieces.shape[0]):
            sums = sums + pieces[k, at : at + step].astype(jnp.float32)
        if at + step == rows:
            last = sums[step - 8 :]
            tail = split(last[0:2] + last[2:4] + last[4:6])
            tail = jnp.where(place[4 + stage] == 1, tail, last)
            sums = jnp.concatenate([sums[: step - 8], tail], axis=0)
        if scratch:
            scratch[0][at : at + step] = sums
        elif len(out.shape) == 3:
            for k in range(out.shape[0]):
                out[k] = sums.astype(jnp.bfloat16)
        else:
            out[at : at + step] = sums.astype(jnp.bfloat16)
    if scratch:
        for k in range(out.shape[0]):
            out[k] = scratch[0][k * pitch : (k + 1) * pitch].astype(jnp.bfloat16)


def gradient_totals(part, place):
    for stage, axes in enumerate(STAGES):
        count = lax.axis_size(axes)
        pieces = lax.all_to_all(part.reshape(count, -1, LANES), axes, 0, 0, tiled=True)
        rows = pieces.shape[1]
        kernel = functools.partial(add_up, stage)
        if stage == 0:
            (part,) = call(kernel, [((rows, LANES), jnp.bfloat16, None)], place, pieces)
        elif stage == 1:
            pitch = rows // lax.axis_size(STAGES[2])
            (part,) = call(
                kernel,
                [((rows // pitch, pitch, LANES), jnp.bfloat16, None)],
                place,
                pieces,
                scratch=[((rows, LANES), jnp.float32)],
            )
        else:
            (part,) = call(kernel, [((count, rows, LANES), jnp.bfloat16, None)], place, pieces)
    part = lax.all_to_all(part, STAGES[2], 0, 0, tiled=True).reshape(-1, LANES)
    for axes in STAGES[1::-1]:
        count = lax.axis_size(axes)
        copies = jnp.broadcast_to(part[None], (count,) + part.shape)
        part = lax.all_to_all(copies, axes, 0, 0, tiled=True).reshape(-1, LANES)
    return part


def on_device(field, cotangent, gain_fine, weight_fine, projection, gain_coarse, weight_coarse):
    height, width, chan_fine = field.shape
    chan_coarse = projection.shape[1]
    half_h, half_w = (height // 2, width // 2)
    cells_all = height * width * lax.axis_size(GY_GX)
    fine_count = cells_all * (chan_fine // GROUPS)
    coarse_count = cells_all // 4 * (chan_coarse // GROUPS)
    rows, cols = height * lax.axis_size(GY), width * lax.axis_size(GX)
    f32, bf16 = jnp.float32, jnp.bfloat16
    near = lax.axis_size(NEAR)
    row, col = lax.axis_index(GY), lax.axis_index(GX)
    holds, held = [], jnp.int32(1)
    for axes in STAGES:
        held = held * (lax.axis_index(axes) == lax.axis_size(axes) - 1)
        holds.append(held)
    place = jnp.stack([row * height, col * width, row * half_h, col * half_w] + holds)
    place = place.astype(jnp.int32)
    gain_f, gain_c = gain_fine.reshape(1, -1), gain_coarse.reshape(1, -1)

    slabs = FINE_RIM * width + COARSE_RIM * half_w * chan_coarse // LANES
    copies, inner, outer = call(
        field_sums,
        [((near, 2, LANES), f32, None), ((slabs, LANES), bf16, None), ((slabs, LANES), bf16, None)],
        field,
        cotangent,
        plain=(0, 1),
    )
    sums = gathered(copies)
    x, (tall, rims, shapes) = with_rims(field, cotangent, inner, outer)
    lines = half_h + 2
    cells = lines * PITCH // 2
    hidden_f, pooled, coarse, copies, stats_f = call(
        functools.partial(fine_forward, fine_count, rows, cols),
        [
            (x.shape, bf16, HBM),
            ((cells, chan_fine), bf16, HBM),
            ((cells, chan_coarse), bf16),
            ((near, 4, LANES), f32, None),
            ((2, 8, chan_fine), f32),
        ],
        place,
        x,
        sums,
        gain_f,
        weight_fine.reshape(3, 3 * chan_fine, chan_fine),
        projection,
        scratch=[
            (x.shape[:2] + (3 * chan_fine,), bf16),
            ((2 * lines * PITCH + 8, chan_fine), f32),
        ],
    )
    sums, (tall, rims) = gathered(copies, (tall, rims))
    grad = coarse_ring(tall, rims, shapes)
    pre, weight_t = call(
        coarse_transpose,
        [((cells, chan_coarse), f32), ((3, 3 * chan_fine, chan_fine), bf16, HBM)],
        grad,
        weight_coarse,
        weight_fine.reshape(9, chan_fine, chan_fine),
        plain=(1, 2),
        scratch=[((3,) + grad.shape, bf16)],
    )
    hidden_c, dnorm, copies, stats_c = call(
        functools.partial(coarse_middle, coarse_count, rows // 2, cols // 2),
        [
            ((lines, PITCH // 2, chan_coarse), bf16, HBM),
            ((cells, chan_coarse), f32, HBM),
            ((near, 4, LANES), f32, None),
            ((2, 8, chan_coarse), f32),
        ],
        place,
        sums,
        coarse,
        pre,
        gain_c,
    )
    sums = gathered(copies)
    used = 18 * chan_coarse + 9 * chan_fine + chan_coarse
    used += -(used + 8) % (4 * lax.axis_size(GY_GX)) + 8
    coarse_output, parts = call(
        coarse_rest,
        [((half_h, half_w, chan_coarse), bf16, None), ((18 * chan_coarse, LANES), bf16)],
        hidden_c,
        coarse,
        grad,
        weight_coarse.reshape(3, 3 * chan_coarse, chan_coarse),
        scratch=[((lines, PITCH // 2, 3 * chan_coarse), bf16)],
        plain=(0, 3),
    )
    parts, coarse_gain_grad, partial = call(
        functools.partial(fine_backward, coarse_count, rows // 2, cols // 2),
        [
            ((used, LANES), bf16, None),
            ((1, chan_coarse), f32, None),
            ((height, width, chan_fine), f32),
        ],
        place,
        sums,
        coarse,
        pooled,
        grad,
        dnorm,
        stats_c,
        gain_c,
        projection,
        weight_t,
        x,
        hidden_f,
        stats_f,
        gain_f,
        parts,
        scratch=[
            ((lines * PITCH + 8, chan_fine), f32),
            ((lines, PITCH, 3 * chan_fine), bf16),
            ((3, lines, PITCH // 2, chan_fine), f32),
        ],
        plain=(3, 5, 8, 9, 11),
    )
    totals = gradient_totals(parts, place)
    field_grad, fine_weight_grad, fine_gain_grad, projection_grad, coarse_weight_grad = call(
        functools.partial(finish, fine_count),
        [
            ((height, width, chan_fine), bf16, None),
            ((9 * chan_fine, chan_fine), f32, None),
            ((1, chan_fine), f32, None),
            ((chan_fine, chan_coarse), f32, None),
            ((9 * chan_coarse, chan_coarse), f32, None),
        ],
        totals,
        partial,
        x,
        stats_f,
        gain_f,
    )
    return (
        coarse_output,
        field_grad,
        fine_weight_grad.reshape(weight_fine.shape),
        fine_gain_grad.reshape(-1),
        projection_grad,
        coarse_weight_grad.reshape(weight_coarse.shape),
        coarse_gain_grad.reshape(-1),
    )


def solution(mesh):
    finer = Mesh(mesh.devices.reshape(2, 8, 2, 8, 2), GY_GX)
    in_specs = (P(GY, GX, None), P(GY, GX, None), P(), P(), P(), P(), P())
    out_specs = (P(GY, GX, None), P(GY, GX, None), P(), P(), P(), P(), P())

    return jax.shard_map(
        on_device, mesh=finer, in_specs=in_specs, out_specs=out_specs, check_vma=False
    )
```

```python
import functools

import jax
import jax.numpy as jnp
from jax import lax
from jax.experimental import pallas as pl
from jax.experimental.pallas import tpu as pltpu
from jax.sharding import Mesh
from jax.sharding import PartitionSpec as P


GROUPS = 32
GY = ("gy_0", "gy_1")
CORE = "gx_3"
GX = ("gx_0", "gx_1", "gx_2", CORE)
GY_GX = GY + GX
NEAR = ("gx_1", "gx_2", CORE)
FAR = ("gx_0", "gy_0", "gy_1")
STAGES = ((CORE,), ("gx_0", "gy_0", "gx_2"), ("gx_1", "gy_1"))
LANES = 128
EPSILON = 1e-05

HBM = pltpu.HBM
PITCH = 32
FINE_RIM = 3
COARSE_RIM = 2


def is_even(axis):
    return lax.axis_index(axis) % 2 == 0


def swap(inner, outer, axis):
    count = lax.axis_size(axis)
    mate = lax.ppermute(inner, axis, [(i, i ^ 1) for i in range(count)])
    pairs = [(i, i + 1) for i in range(1, count - 1, 2)]
    other = lax.ppermute(outer, axis, pairs + [(j, i) for i, j in pairs])
    even = is_even(axis)
    return jnp.where(even, other, mate), jnp.where(even, mate, other)


def joined(fine, coarse):
    cells = coarse.reshape(-1, coarse.shape[2])
    return jnp.concatenate(
        [fine.reshape(-1, LANES)] + [cells[:, k : k + LANES] for k in range(0, cells.shape[1], LANES)]
    )


def parted(rims, fine, coarse):
    size = fine[0] * fine[1]
    cells = coarse[0] * coarse[1]
    halves = [rims[size + k * cells : size + (k + 1) * cells] for k in range(coarse[2] // LANES)]
    return rims[:size].reshape(fine), jnp.concatenate(halves, axis=1).reshape(coarse)


def ring(own, left, right, pitch):
    rows, cols, channels = own.shape
    gap = pitch - cols - left.shape[1] - right.shape[1]
    return jnp.concatenate([own, right, jnp.zeros((rows, gap, channels), own.dtype), left], axis=1)


def with_rims(fine, coarse, inner, outer):
    shapes = (FINE_RIM,) + fine.shape[1:], (COARSE_RIM,) + coarse.shape[1:]
    rims = swap(inner, outer, GY)
    (f0, c0), (f1, c1) = (parted(r, *shapes) for r in rims)
    fine = jnp.concatenate([f0, fine, f1])
    coarse = jnp.concatenate([c0, coarse, c1])
    shapes = (
        (fine.shape[0], FINE_RIM, fine.shape[2]),
        (coarse.shape[0], COARSE_RIM, coarse.shape[2]),
    )
    heads = joined(fine[:, :FINE_RIM], coarse[:, :COARSE_RIM])
    tails = joined(fine[:, -FINE_RIM:], coarse[:, -COARSE_RIM:])
    even = is_even(GX)
    inner, outer = jnp.where(even, tails, heads), jnp.where(even, heads, tails)
    rims = swap(inner, outer, GX)
    f0, f1 = (parted(r, *shapes)[0] for r in rims)
    return ring(fine, f0, f1, PITCH), (coarse, rims, shapes)


def coarse_ring(coarse, rims, shapes):
    c0, c1 = (parted(r, *shapes)[1] for r in rims)
    return ring(coarse, c0, c1, PITCH // 2)


def call(body, outs, *args, scratch=(), plain=()):
    spaces = [
        pl.BlockSpec(memory_space=pltpu.SMEM if a.dtype == jnp.int32 else pltpu.VMEM) for a in args
    ]
    args = [
        a
        if a.dtype == jnp.int32
        else pltpu.with_memory_space_constraint(a, pltpu.HBM if k in plain else pltpu.VMEM)
        for k, a in enumerate(args)
    ]
    return pl.pallas_call(
        body,
        out_shape=[
            (pltpu.VMEM if len(o) == 2 else o[2] or jax.ShapeDtypeStruct)(o[0], o[1])
            for o in outs
        ],
        in_specs=spaces,
        out_specs=[pl.BlockSpec(memory_space=pltpu.VMEM) for _ in outs],
        scratch_shapes=[pltpu.VMEM(shape, dtype) for shape, dtype in scratch],
        compiler_params=pltpu.CompilerParams(vmem_limit_bytes=24 << 20),
    )(*args)


def group_sum(values, size):
    lanes = values.shape[1]
    lane = lax.broadcasted_iota(jnp.int32, values.shape, 1)
    step = 1
    while step < size:
        after = pltpu.roll(values, lanes - step, 1)
        before = pltpu.roll(values, step, 1)
        values = values + jnp.where((lane & step) == 0, after, before)
        step *= 2
    return values


def wide(row):
    return jnp.broadcast_to(row, (8, row.shape[1]))


def moments(first, second, count, size):
    average = group_sum(wide(first), size) / count
    square = group_sum(wide(second), size) / count
    return average, lax.rsqrt(square - average * average + EPSILON)


def sigmoid(act):
    return 1.0 / (1.0 + jnp.exp(-act))


def in_grid(shape, first_row, first_col, rim, rows, cols):
    row = lax.broadcasted_iota(jnp.int32, shape, 0) + first_row
    place = lax.broadcasted_iota(jnp.int32, shape, 1)
    col = jnp.where(place < shape[1] - rim, place, place - shape[1]) + first_col
    return (row >= 0) & (row < rows) & (col >= 0) & (col < cols)


def over_cells(values):
    lanes = values.shape[-1]
    return jnp.sum(jnp.sum(values.reshape(-1, 8, lanes), axis=0), axis=0, keepdims=True)


def spread(copies, rows):
    for k, row in enumerate(rows):
        copies[:, k, :] = jnp.broadcast_to(row, (copies.shape[0], LANES))


def slab(rims, at, values):
    cells = values.reshape(-1, values.shape[-1])
    for lane in range(0, cells.shape[1], LANES):
        rims[at : at + cells.shape[0]] = cells[:, lane : lane + LANES]
        at += cells.shape[0]
    return at


def field_sums(field, grad, copies, inner, outer):
    even = is_even(GY)
    low, high = field.shape[0] - FINE_RIM, grad.shape[0] - COARSE_RIM

    def write(heads, tails):
        slab(heads, slab(heads, 0, field[:FINE_RIM]), grad[:COARSE_RIM])
        slab(tails, slab(tails, 0, field[low:]), grad[high:])

    pl.when(even)(lambda: write(outer, inner))
    pl.when(jnp.logical_not(even))(lambda: write(inner, outer))
    first = jnp.zeros((8, LANES), jnp.float32)
    second = jnp.zeros((8, LANES), jnp.float32)
    for at in range(0, field.shape[0], 8):
        v = field[at : at + 8].astype(jnp.float32).reshape(-1, 8, LANES)
        first = first + jnp.sum(v, axis=0)
        second = second + jnp.sum(v * v, axis=0)
    spread(
        copies, [jnp.sum(first, axis=0, keepdims=True), jnp.sum(second, axis=0, keepdims=True)]
    )


def relay(received, copies):
    sums = jnp.sum(received[...], axis=0)
    for k in range(copies.shape[1]):
        copies[:, k, :] = jnp.broadcast_to(sums[k : k + 1], (copies.shape[0], LANES))


def fine_forward(count, rows, cols, place, x, sums, gain, weight, projection,
                 center, pooled, coarse, copies, stats, hidden, block):
    tot = jnp.sum(sums[...], axis=0)
    average, inverse = moments(tot[0:1], tot[1:2], count, LANES // GROUPS)
    stats[0] = average
    stats[1] = inverse
    average, scale = average[0:1], inverse[0:1] * gain[...]
    lines = x.shape[0]
    step = 10
    for at in range(0, lines, step):
        v = x[at : at + step].astype(jnp.float32)
        act = (v - average) * scale
        h = act * sigmoid(act)
        keep = in_grid(
            h.shape, at - FINE_RIM + place[0], place[1], FINE_RIM, rows, cols
        )
        h = jnp.where(keep, h, 0.0)
        hidden[at : at + step, :, 0:LANES] = pltpu.roll(h, 1, 1).astype(jnp.bfloat16)
        hidden[at : at + step, :, LANES : 2 * LANES] = h.astype(jnp.bfloat16)
        center[at : at + step] = h.astype(jnp.bfloat16)
        hidden[at : at + step, :, 2 * LANES :] = pltpu.roll(h, PITCH - 1, 1).astype(jnp.bfloat16)
    step = (lines - 2) // 4
    for at in range(0, lines - 2, step):
        acc = x[at + 1 : at + 1 + step].astype(jnp.float32).reshape(step * PITCH, LANES)
        conv = jnp.zeros_like(acc)
        for tap in range(3):
            conv = conv + jnp.dot(
                hidden[at + tap : at + tap + step].reshape(step * PITCH, 3 * LANES),
                weight[tap],
                preferred_element_type=jnp.float32,
            )
        block[at * PITCH : (at + step) * PITCH] = (
            (acc + conv).astype(jnp.bfloat16).astype(jnp.float32)
        )
    half = PITCH // 2
    step = (lines - 2) // 4
    first = jnp.zeros((1, coarse.shape[1]), jnp.float32)
    second = jnp.zeros((1, coarse.shape[1]), jnp.float32)
    for at in range(0, (lines - 2) // 2, step):
        size = 2 * step * half
        pair = block[pl.ds(2 * at * PITCH, size, stride=2), :] + block[
            pl.ds(2 * at * PITCH + 1, size, stride=2), :
        ]
        mean = 0.25 * jnp.sum(pair.reshape(step, 2, half, LANES), axis=1)
        mean = mean.reshape(step * half, LANES).astype(jnp.bfloat16)
        pooled[at * half : (at + step) * half] = mean
        cells = jnp.dot(mean, projection[...], preferred_element_type=jnp.float32).astype(
            jnp.bfloat16
        )
        coarse[at * half : (at + step) * half] = cells
        own = cells.astype(jnp.float32).reshape(step, half, -1)[:, : half // 2]
        low = 1 if at == 0 else 0
        high = step - 1 if at + step == (lines - 2) // 2 else step
        own = own[low:high]
        first = first + over_cells(own)
        second = second + over_cells(own * own)
    spread(copies, [first[:, :LANES], first[:, LANES:], second[:, :LANES], second[:, LANES:]])


def coarse_transpose(grad, weight, fine_weight, out, fine_out, shifted):
    for tap in range(9):
        block = fine_weight[tap].astype(jnp.float32).T.astype(jnp.bfloat16)
        fine_out[tap // 3, tap % 3 * LANES : (tap % 3 + 1) * LANES] = block
    half = PITCH // 2
    lines = grad.shape[0]
    step = lines // 4
    for at in range(0, lines, step):
        g = grad[at : at + step].astype(jnp.float32)
        shifted[0, at : at + step] = pltpu.roll(g, half - 1, 1).astype(jnp.bfloat16)
        shifted[1, at : at + step] = grad[at : at + step]
        shifted[2, at : at + step] = pltpu.roll(g, 1, 1).astype(jnp.bfloat16)
    step = (lines - 2) // 2
    for at in range(0, lines - 2, step):
        acc = jnp.zeros((step * half, weight.shape[2]), jnp.float32)
        for row_tap in range(3):
            for col_tap in range(3):
                begin = at + 2 - row_tap
                acc = acc + lax.dot_general(
                    shifted[col_tap, begin : begin + step].reshape(step * half, -1),
                    weight[row_tap, col_tap],
                    (((1,), (1,)), ((), ())),
                    preferred_element_type=jnp.float32,
                )
        out[at * half : (at + step) * half] = acc


def coarse_middle(count, rows, cols, place, sums, coarse, pre, gain,
                  hidden, dnorm, copies, stats):
    tot = jnp.sum(sums[...], axis=0)
    average, inverse = moments(
        jnp.concatenate([tot[0:1], tot[1:2]], axis=1),
        jnp.concatenate([tot[2:3], tot[3:4]], axis=1),
        count,
        2 * LANES // GROUPS,
    )
    stats[0] = average
    stats[1] = inverse
    average, inverse = average[0:1], inverse[0:1]
    half = PITCH // 2
    lines = coarse.shape[0] // half
    channels = coarse.shape[1]
    step = lines // 2
    first = jnp.zeros((1, channels), jnp.float32)
    second = jnp.zeros((1, channels), jnp.float32)
    for at in range(0, lines, step):
        span = slice(at * half, (at + step) * half)
        normed = (coarse[span].astype(jnp.float32) - average) * inverse
        act = normed * gain[...]
        sigma = sigmoid(act)
        h = (act * sigma).reshape(step, half, channels)
        h = jnp.where(
            in_grid(h.shape, at - 1 + place[2], place[3], COARSE_RIM, rows, cols), h, 0.0
        )
        hidden[at : at + step] = h.astype(jnp.bfloat16)
        dact = pre[span] * (sigma * (1.0 + act * (1.0 - sigma)))
        dn = dact * gain[...]
        dnorm[span] = dn
        low = 1 if at == 0 else 0
        high = step - 1 if at + step == lines else step
        own = slice(low, high), slice(0, half // 2)
        first = first + over_cells(dn.reshape(step, half, channels)[own])
        second = second + over_cells((dact * normed).reshape(step, half, channels)[own])
    spread(copies, [first[:, :LANES], first[:, LANES:], second[:, :LANES], second[:, LANES:]])


def coarse_rest(center, coarse, grad, weight, out, rows_out, hidden):
    half = PITCH // 2
    height = out.shape[0]
    channels = out.shape[2]
    step = center.shape[0] // 2
    for at in range(0, center.shape[0], step):
        h = center[at : at + step].astype(jnp.float32)
        hidden[at : at + step, :, 0:channels] = pltpu.roll(h, 1, 1).astype(jnp.bfloat16)
        hidden[at : at + step, :, channels : 2 * channels] = center[at : at + step]
        hidden[at : at + step, :, 2 * channels :] = pltpu.roll(h, half - 1, 1).astype(jnp.bfloat16)
    step = height // 2
    for at in range(0, height, step):
        acc = coarse[(at + 1) * half : (at + 1 + step) * half].astype(jnp.float32)
        conv = jnp.zeros_like(acc)
        for tap in range(3):
            conv = conv + jnp.dot(
                hidden[at + tap : at + tap + step].reshape(step * half, 3 * channels),
                weight[tap],
                preferred_element_type=jnp.float32,
            )
        out[at : at + step] = (acc + conv).reshape(step, half, channels)[:, : half // 2].astype(
            jnp.bfloat16
        )
    g = grad[2 : 2 + height].astype(jnp.float32)
    own = lax.broadcasted_iota(jnp.int32, g.shape, 1) < half // 2
    g = jnp.where(own, g, 0.0).astype(jnp.bfloat16).reshape(height * half, channels)
    tall = 9 * channels
    for tap in range(3):
        k = lax.dot_general(
            hidden[tap : tap + height].reshape(height * half, 3 * channels),
            g,
            (((0,), (0,)), ((), ())),
            preferred_element_type=jnp.float32,
        ).astype(jnp.bfloat16)
        at = tap * 3 * channels
        rows_out[at : at + 3 * channels] = k[:, :LANES]
        rows_out[tall + at : tall + at + 3 * channels] = k[:, LANES:]


def fine_backward(coarse_count, rows, cols, place, sums, coarse, pooled, grad, dnorm, stats_c,
                  gain_c, projection, weight_t, x, hidden, stats_f, gain_f, rows_in,
                  keep, send, gain_c_grad, partial, rows_out, up, shifted, taps):
    rows_out[0 : rows_in.shape[0]] = rows_in[...]
    tot = jnp.sum(sums[...], axis=0)
    first = jnp.concatenate([tot[0:1], tot[1:2]], axis=1)
    second = jnp.concatenate([tot[2:3], tot[3:4]], axis=1)
    gain_c_grad[...] = second
    size = 2 * LANES // GROUPS
    a_sum = group_sum(wide(first), size)[0:1] / coarse_count
    b_sum = group_sum(wide(second * gain_c[...]), size)[0:1] / coarse_count
    average, inverse = stats_c[0, 0:1], stats_c[1, 0:1]
    half = PITCH // 2
    lines = coarse.shape[0] // half
    channels = coarse.shape[1]
    height = 2 * (lines - 2)
    step = lines // 2
    proj_grad = jnp.zeros((LANES, channels), jnp.float32)
    for at in range(0, lines, step):
        span = slice(at * half, (at + step) * half)
        normed = (coarse[span].astype(jnp.float32) - average) * inverse
        g = grad[at + 1 : at + 1 + step].astype(jnp.float32).reshape(step * half, channels)
        d = g + inverse * (dnorm[span] - a_sum - normed * b_sum)
        d = d.reshape(step, half, channels)
        d = jnp.where(
            in_grid(d.shape, at - 1 + place[2], place[3], COARSE_RIM, rows, cols), d, 0.0
        )
        line = lax.broadcasted_iota(jnp.int32, d.shape, 0) + at
        spot = lax.broadcasted_iota(jnp.int32, d.shape, 1)
        own = (line >= 1) & (line < lines - 1) & (spot < half // 2)
        own = jnp.where(own, d, 0.0).astype(jnp.bfloat16).reshape(step * half, channels)
        d = d.astype(jnp.bfloat16).reshape(step * half, channels)
        proj_grad = proj_grad + lax.dot_general(
            pooled[span], own, (((0,), (0,)), ((), ())), preferred_element_type=jnp.float32
        )
        small = lax.dot_general(
            d, projection[...], (((1,), (1,)), ((), ())), preferred_element_type=jnp.float32
        )
        small = (small * 0.25).astype(jnp.bfloat16).astype(jnp.float32)
        up[pl.ds(at * PITCH, step * half, stride=2), :] = small
        up[pl.ds(at * PITCH + 1, step * half, stride=2), :] = small
    for at in range(0, lines, step):
        u = up[at * PITCH : (at + step) * PITCH].reshape(step, PITCH, LANES)
        shifted[at : at + step, :, 0:LANES] = pltpu.roll(u, PITCH - 1, 1).astype(jnp.bfloat16)
        shifted[at : at + step, :, LANES : 2 * LANES] = u.astype(jnp.bfloat16)
        shifted[at : at + step, :, 2 * LANES :] = pltpu.roll(u, 1, 1).astype(jnp.bfloat16)
    width = PITCH // 2
    for tap in range(3):
        for at in range(0, lines, step):
            y = jnp.dot(
                shifted[at : at + step, 0:width, :].reshape(step * width, 3 * LANES),
                weight_t[tap],
                preferred_element_type=jnp.float32,
            )
            taps[tap, at : at + step] = y.reshape(step, width, LANES)
    average, inverse = stats_f[0, 0:1], stats_f[1, 0:1]
    first = jnp.zeros((1, LANES), jnp.float32)
    second = jnp.zeros((1, LANES), jnp.float32)
    step = 8
    for at in range(0, lines - 2, step):
        even = taps[0, at + 1 : at + 1 + step] + taps[1, at + 1 : at + 1 + step] + taps[
            2, at : at + step
        ]
        odd = taps[0, at + 2 : at + 2 + step] + taps[1, at + 1 : at + 1 + step] + taps[
            2, at + 1 : at + 1 + step
        ]
        both = jnp.stack([even, odd], axis=1).reshape(2 * step, width, LANES)
        begin = FINE_RIM + 2 * at
        v = x[begin : begin + 2 * step, 0:width, :].astype(jnp.float32)
        normed = (v - average) * inverse
        act = normed * gain_f[...]
        sigma = sigmoid(act)
        dact = both * (sigma * (1.0 + act * (1.0 - sigma)))
        dn = dact * gain_f[...]
        first = first + over_cells(dn)
        second = second + over_cells(dact * normed)
        u = up[(at + 1) * PITCH : (at + 1 + step) * PITCH].reshape(step, PITCH, LANES)[:, 0:width]
        u = jnp.broadcast_to(u[:, None], (step, 2, width, LANES)).reshape(2 * step, width, LANES)
        partial[2 * at : 2 * at + 2 * step] = u + inverse * dn
    for at in range(1, lines - 1, step):
        u = up[at * PITCH : (at + step) * PITCH].reshape(step, PITCH, LANES)
        own = lax.broadcasted_iota(jnp.int32, u.shape, 1) < width
        u = jnp.where(own, u, 0.0)
        shifted[at : at + step, :, 0:LANES] = pltpu.roll(u, PITCH - 1, 1).astype(jnp.bfloat16)
        shifted[at : at + step, :, LANES : 2 * LANES] = u.astype(jnp.bfloat16)
        shifted[at : at + step, :, 2 * LANES :] = pltpu.roll(u, 1, 1).astype(jnp.bfloat16)
    d = shifted[1 : lines - 1]
    d = jnp.broadcast_to(d[:, None], (lines - 2, 2) + d.shape[1:])
    d = d.reshape(height * PITCH, 3 * LANES)
    at = 18 * channels
    for tap in range(3):
        begin = FINE_RIM - 1 + tap
        k = lax.dot_general(
            hidden[begin : begin + height].reshape(height * PITCH, LANES),
            d,
            (((0,), (0,)), ((), ())),
            preferred_element_type=jnp.float32,
        ).astype(jnp.bfloat16)
        for col_tap in range(3):
            rows_out[at : at + LANES] = k[:, col_tap * LANES : (col_tap + 1) * LANES]
            at += LANES
    proj_grad = proj_grad.astype(jnp.bfloat16)
    rows_out[at : at + LANES] = proj_grad[:, :LANES]
    rows_out[at + LANES : at + 2 * LANES] = proj_grad[:, LANES:]
    at += 2 * LANES
    spare = rows_out.shape[0] - at
    small = jnp.concatenate([first, second], axis=0)
    rows_out[at:] = jnp.concatenate(
        [jnp.zeros((spare - 8, LANES), jnp.float32), split(small)], axis=0
    ).astype(jnp.bfloat16)
    half = keep.shape[0]

    def part(first, last):
        first[...] = rows_out[:half]
        last[...] = rows_out[half:]

    core = lax.axis_index(CORE)
    pl.when(core == 0)(lambda: part(keep, send))
    pl.when(core == 1)(lambda: part(send, keep))


def spread_rows(low, high, at, out, lane):
    half, count = low.shape[0], out.shape[0]
    split_at = min(max(half - at, 0), count)
    lanes = slice(lane, lane + LANES)
    if split_at > 0:
        out[:split_at, lanes] = low[at : at + split_at].astype(jnp.float32)
    if split_at < count:
        begin = at + split_at - half
        out[split_at:, lanes] = high[begin : begin + count - split_at].astype(jnp.float32)
    return at + count


def finish(fine_count, own, other, partial, x, stats, gain,
           field_grad, weight_f, gain_f, proj, weight_c):
    core = lax.axis_index(CORE)
    last = own.shape[0] - 8
    small = jnp.where(
        core == 1, own[last:].astype(jnp.float32), other[last:].astype(jnp.float32)
    )
    small = small[0:2] + small[2:4] + small[4:6]
    first, second = small[0:1], small[1:2]
    gain_f[...] = second
    size = LANES // GROUPS
    a_sum = group_sum(wide(first), size)[0:1] / fine_count
    b_sum = group_sum(wide(second * gain[...]), size)[0:1] / fine_count
    average, inverse = stats[0, 0:1], stats[1, 0:1]
    height, width, _ = partial.shape
    step = 16
    for at in range(0, height, step):
        v = x[FINE_RIM + at : FINE_RIM + at + step, 0:width, :].astype(jnp.float32)
        normed = (v - average) * inverse
        field_grad[at : at + step] = (
            partial[at : at + step] - inverse * (a_sum + normed * b_sum)
        ).astype(jnp.bfloat16)

    def weights(low, high):
        at = spread_rows(low, high, 0, weight_c, 0)
        at = spread_rows(low, high, at, weight_c, LANES)
        at = spread_rows(low, high, at, weight_f, 0)
        at = spread_rows(low, high, at, proj, 0)
        spread_rows(low, high, at, proj, LANES)

    pl.when(core == 0)(lambda: weights(own, other))
    pl.when(core == 1)(lambda: weights(other, own))


def gathered(copies, late=None):
    far = lax.axis_size(FAR)
    received = lax.all_to_all(copies, NEAR, 0, 0, tiled=True)
    (copies,) = call(relay, [((far,) + copies.shape[1:], jnp.float32, None)], received)
    if late is not None:
        copies, late = lax.optimization_barrier((copies, late))
    sums = lax.all_to_all(copies, FAR, 0, 0, tiled=True)
    return sums if late is None else (sums, late)


def split(small):
    high = small.astype(jnp.bfloat16).astype(jnp.float32)
    middle = (small - high).astype(jnp.bfloat16).astype(jnp.float32)
    low = small - high - middle
    return jnp.concatenate([high, middle, low, jnp.zeros_like(low)], axis=0)


def add_up(stage, place, *refs):
    if stage == 0:
        pieces, (out,), scratch = refs[:2], refs[2:], ()
    else:
        pieces = [refs[0].at[k] for k in range(refs[0].shape[0])]
        out, scratch = refs[1], refs[2:]
    rows = pieces[0].shape[0]
    step = 256 if rows % 256 == 0 else rows
    pitch = out.shape[-2]
    for at in range(0, rows, step):
        sums = pieces[0][at : at + step].astype(jnp.float32)
        for piece in pieces[1:]:
            sums = sums + piece[at : at + step].astype(jnp.float32)
        if at + step == rows:
            last = sums[step - 8 :]
            tail = split(last[0:2] + last[2:4] + last[4:6])
            tail = jnp.where(place[4 + stage] == 1, tail, last)
            sums = jnp.concatenate([sums[: step - 8], tail], axis=0)
        if scratch:
            scratch[0][at : at + step] = sums
        elif len(out.shape) == 3:
            for k in range(out.shape[0]):
                out[k] = sums.astype(jnp.bfloat16)
        else:
            out[at : at + step] = sums.astype(jnp.bfloat16)
    if scratch:
        for k in range(out.shape[0]):
            out[k] = scratch[0][k * pitch : (k + 1) * pitch].astype(jnp.bfloat16)


def traded(rows):
    return lax.ppermute(rows, CORE, [(0, 1), (1, 0)])


def gradient_totals(keep, send, place):
    rows = keep.shape[0]
    (part,) = call(
        functools.partial(add_up, 0), [((rows, LANES), jnp.bfloat16, None)], place, keep, traded(send)
    )
    for stage, axes in list(enumerate(STAGES))[1:]:
        count = lax.axis_size(axes)
        pieces = lax.all_to_all(part.reshape(count, -1, LANES), axes, 0, 0, tiled=True)
        rows = pieces.shape[1]
        kernel = functools.partial(add_up, stage)
        if stage == 1:
            pitch = rows // lax.axis_size(STAGES[2])
            (part,) = call(
                kernel,
                [((rows // pitch, pitch, LANES), jnp.bfloat16, None)],
                place,
                pieces,
                scratch=[((rows, LANES), jnp.float32)],
            )
        else:
            (part,) = call(kernel, [((count, rows, LANES), jnp.bfloat16, None)], place, pieces)
    part = lax.all_to_all(part, STAGES[2], 0, 0, tiled=True).reshape(-1, LANES)
    count = lax.axis_size(STAGES[1])
    copies = jnp.broadcast_to(part[None], (count,) + part.shape)
    part = lax.all_to_all(copies, STAGES[1], 0, 0, tiled=True).reshape(-1, LANES)
    return part, traded(part)


def on_device(field, cotangent, gain_fine, weight_fine, projection, gain_coarse, weight_coarse):
    height, width, chan_fine = field.shape
    chan_coarse = projection.shape[1]
    half_h, half_w = (height // 2, width // 2)
    cells_all = height * width * lax.axis_size(GY_GX)
    fine_count = cells_all * (chan_fine // GROUPS)
    coarse_count = cells_all // 4 * (chan_coarse // GROUPS)
    rows, cols = height * lax.axis_size(GY), width * lax.axis_size(GX)
    f32, bf16 = jnp.float32, jnp.bfloat16
    near = lax.axis_size(NEAR)
    row, col = lax.axis_index(GY), lax.axis_index(GX)
    holds, held = [], jnp.int32(1)
    for axes in STAGES:
        held = held * (lax.axis_index(axes) == lax.axis_size(axes) - 1)
        holds.append(held)
    place = jnp.stack([row * height, col * width, row * half_h, col * half_w] + holds)
    place = place.astype(jnp.int32)
    gain_f, gain_c = gain_fine.reshape(1, -1), gain_coarse.reshape(1, -1)

    slabs = FINE_RIM * width + COARSE_RIM * half_w * chan_coarse // LANES
    copies, inner, outer = call(
        field_sums,
        [((near, 2, LANES), f32, None), ((slabs, LANES), bf16, None), ((slabs, LANES), bf16, None)],
        field,
        cotangent,
        plain=(0, 1),
    )
    sums = gathered(copies)
    x, (tall, rims, shapes) = with_rims(field, cotangent, inner, outer)
    lines = half_h + 2
    cells = lines * PITCH // 2
    hidden_f, pooled, coarse, copies, stats_f = call(
        functools.partial(fine_forward, fine_count, rows, cols),
        [
            (x.shape, bf16, HBM),
            ((cells, chan_fine), bf16, HBM),
            ((cells, chan_coarse), bf16),
            ((near, 4, LANES), f32, None),
            ((2, 8, chan_fine), f32),
        ],
        place,
        x,
        sums,
        gain_f,
        weight_fine.reshape(3, 3 * chan_fine, chan_fine),
        projection,
        scratch=[
            (x.shape[:2] + (3 * chan_fine,), bf16),
            ((2 * lines * PITCH + 8, chan_fine), f32),
        ],
    )
    sums, (tall, rims) = gathered(copies, (tall, rims))
    grad = coarse_ring(tall, rims, shapes)
    pre, weight_t = call(
        coarse_transpose,
        [((cells, chan_coarse), f32), ((3, 3 * chan_fine, chan_fine), bf16, HBM)],
        grad,
        weight_coarse,
        weight_fine.reshape(9, chan_fine, chan_fine),
        plain=(1, 2),
        scratch=[((3,) + grad.shape, bf16)],
    )
    hidden_c, dnorm, copies, stats_c = call(
        functools.partial(coarse_middle, coarse_count, rows // 2, cols // 2),
        [
            ((lines, PITCH // 2, chan_coarse), bf16, HBM),
            ((cells, chan_coarse), f32, HBM),
            ((near, 4, LANES), f32, None),
            ((2, 8, chan_coarse), f32),
        ],
        place,
        sums,
        coarse,
        pre,
        gain_c,
    )
    sums = gathered(copies)
    used = 18 * chan_coarse + 9 * chan_fine + chan_coarse
    used += -(used + 8) % (4 * lax.axis_size(GY_GX)) + 8
    coarse_output, parts = call(
        coarse_rest,
        [((half_h, half_w, chan_coarse), bf16, None), ((18 * chan_coarse, LANES), bf16)],
        hidden_c,
        coarse,
        grad,
        weight_coarse.reshape(3, 3 * chan_coarse, chan_coarse),
        scratch=[((lines, PITCH // 2, 3 * chan_coarse), bf16)],
        plain=(0, 3),
    )
    keep, send, coarse_gain_grad, partial = call(
        functools.partial(fine_backward, coarse_count, rows // 2, cols // 2),
        [
            ((used // 2, LANES), bf16),
            ((used // 2, LANES), bf16, None),
            ((1, chan_coarse), f32, None),
            ((height, width, chan_fine), f32),
        ],
        place,
        sums,
        coarse,
        pooled,
        grad,
        dnorm,
        stats_c,
        gain_c,
        projection,
        weight_t,
        x,
        hidden_f,
        stats_f,
        gain_f,
        parts,
        scratch=[
            ((used, LANES), bf16),
            ((lines * PITCH + 8, chan_fine), f32),
            ((lines, PITCH, 3 * chan_fine), bf16),
            ((3, lines, PITCH // 2, chan_fine), f32),
        ],
        plain=(3, 5, 8, 9, 11),
    )
    own, other = gradient_totals(keep, send, place)
    field_grad, fine_weight_grad, fine_gain_grad, projection_grad, coarse_weight_grad = call(
        functools.partial(finish, fine_count),
        [
            ((height, width, chan_fine), bf16, None),
            ((9 * chan_fine, chan_fine), f32, None),
            ((1, chan_fine), f32, None),
            ((chan_fine, chan_coarse), f32, None),
            ((9 * chan_coarse, chan_coarse), f32, None),
        ],
        own,
        other,
        partial,
        x,
        stats_f,
        gain_f,
    )
    return (
        coarse_output,
        field_grad,
        fine_weight_grad.reshape(weight_fine.shape),
        fine_gain_grad.reshape(-1),
        projection_grad,
        coarse_weight_grad.reshape(weight_coarse.shape),
        coarse_gain_grad.reshape(-1),
    )


def solution(mesh):
    finer = Mesh(mesh.devices.reshape(2, 8, 2, 4, 2, 2), GY_GX)
    in_specs = (P(GY, GX, None), P(GY, GX, None), P(), P(), P(), P(), P())
    out_specs = (P(GY, GX, None), P(GY, GX, None), P(), P(), P(), P(), P())

    return jax.shard_map(
        on_device, mesh=finer, in_specs=in_specs, out_specs=out_specs, check_vma=False
    )
```

```python
import functools

import jax
import jax.numpy as jnp
from jax import lax
from jax.experimental import pallas as pl
from jax.experimental.pallas import tpu as pltpu
from jax.sharding import Mesh
from jax.sharding import PartitionSpec as P


GROUPS = 32
GY = ("gy_0", "gy_1")
CORE = "gx_3"
GX = ("gx_0", "gx_1", "gx_2", CORE)
GY_GX = GY + GX
NEAR = ("gx_1", "gx_2", CORE)
FAR = ("gx_0", "gy_0", "gy_1")
STAGES = ((CORE,), ("gx_0", "gy_0", "gx_2"), ("gx_1", "gy_1"))
LANES = 128
EPSILON = 1e-05

HBM = pltpu.HBM
PITCH = 32
FINE_RIM = 3
COARSE_RIM = 2


def is_even(axis):
    return lax.axis_index(axis) % 2 == 0


def swap(inner, outer, axis):
    count = lax.axis_size(axis)
    mate = lax.ppermute(inner, axis, [(i, i ^ 1) for i in range(count)])
    pairs = [(i, i + 1) for i in range(1, count - 1, 2)]
    other = lax.ppermute(outer, axis, pairs + [(j, i) for i, j in pairs])
    even = is_even(axis)
    return jnp.where(even, other, mate), jnp.where(even, mate, other)


def joined(fine, coarse):
    cells = coarse.reshape(-1, coarse.shape[2])
    return jnp.concatenate(
        [fine.reshape(-1, LANES)] + [cells[:, k : k + LANES] for k in range(0, cells.shape[1], LANES)]
    )


def parted(rims, fine, coarse):
    size = fine[0] * fine[1]
    cells = coarse[0] * coarse[1]
    halves = [rims[size + k * cells : size + (k + 1) * cells] for k in range(coarse[2] // LANES)]
    return rims[:size].reshape(fine), jnp.concatenate(halves, axis=1).reshape(coarse)


def ring(own, left, right, pitch):
    rows, cols, channels = own.shape
    gap = pitch - cols - left.shape[1] - right.shape[1]
    return jnp.concatenate([own, right, jnp.zeros((rows, gap, channels), own.dtype), left], axis=1)


def with_rims(fine, coarse, inner, outer):
    shapes = (FINE_RIM,) + fine.shape[1:], (COARSE_RIM,) + coarse.shape[1:]
    rims = swap(inner, outer, GY)
    (f0, c0), (f1, c1) = (parted(r, *shapes) for r in rims)
    fine = jnp.concatenate([f0, fine, f1])
    coarse = jnp.concatenate([c0, coarse, c1])
    shapes = (
        (fine.shape[0], FINE_RIM, fine.shape[2]),
        (coarse.shape[0], COARSE_RIM, coarse.shape[2]),
    )
    heads = joined(fine[:, :FINE_RIM], coarse[:, :COARSE_RIM])
    tails = joined(fine[:, -FINE_RIM:], coarse[:, -COARSE_RIM:])
    even = is_even(GX)
    inner, outer = jnp.where(even, tails, heads), jnp.where(even, heads, tails)
    rims = swap(inner, outer, GX)
    f0, f1 = (parted(r, *shapes)[0] for r in rims)
    return ring(fine, f0, f1, PITCH), (coarse, rims, shapes)


def coarse_ring(coarse, rims, shapes):
    c0, c1 = (parted(r, *shapes)[1] for r in rims)
    return ring(coarse, c0, c1, PITCH // 2)


def call(body, outs, *args, scratch=(), plain=()):
    spaces = [
        pl.BlockSpec(memory_space=pltpu.SMEM if a.dtype == jnp.int32 else pltpu.VMEM) for a in args
    ]
    args = [
        a
        if a.dtype == jnp.int32
        else pltpu.with_memory_space_constraint(a, pltpu.HBM if k in plain else pltpu.VMEM)
        for k, a in enumerate(args)
    ]
    return pl.pallas_call(
        body,
        out_shape=[
            (pltpu.VMEM if len(o) == 2 else o[2] or jax.ShapeDtypeStruct)(o[0], o[1])
            for o in outs
        ],
        in_specs=spaces,
        out_specs=[pl.BlockSpec(memory_space=pltpu.VMEM) for _ in outs],
        scratch_shapes=[pltpu.VMEM(shape, dtype) for shape, dtype in scratch],
        compiler_params=pltpu.CompilerParams(vmem_limit_bytes=24 << 20),
    )(*args)


def group_sum(values, size):
    lanes = values.shape[1]
    lane = lax.broadcasted_iota(jnp.int32, values.shape, 1)
    step = 1
    while step < size:
        after = pltpu.roll(values, lanes - step, 1)
        before = pltpu.roll(values, step, 1)
        values = values + jnp.where((lane & step) == 0, after, before)
        step *= 2
    return values


def wide(row):
    return jnp.broadcast_to(row, (8, row.shape[1]))


def moments(first, second, count, size):
    average = group_sum(wide(first), size) / count
    square = group_sum(wide(second), size) / count
    return average, lax.rsqrt(square - average * average + EPSILON)


def sigmoid(act):
    return 1.0 / (1.0 + jnp.exp(-act))


def in_grid(shape, first_row, first_col, rim, rows, cols):
    row = lax.broadcasted_iota(jnp.int32, shape, 0) + first_row
    place = lax.broadcasted_iota(jnp.int32, shape, 1)
    col = jnp.where(place < shape[1] - rim, place, place - shape[1]) + first_col
    return (row >= 0) & (row < rows) & (col >= 0) & (col < cols)


def over_cells(values):
    lanes = values.shape[-1]
    return jnp.sum(jnp.sum(values.reshape(-1, 8, lanes), axis=0), axis=0, keepdims=True)


def spread(copies, rows):
    for k, row in enumerate(rows):
        copies[:, k, :] = jnp.broadcast_to(row, (copies.shape[0], LANES))


def slab(rims, at, values):
    cells = values.reshape(-1, values.shape[-1])
    for lane in range(0, cells.shape[1], LANES):
        rims[at : at + cells.shape[0]] = cells[:, lane : lane + LANES]
        at += cells.shape[0]
    return at


def field_sums(field, grad, copies, inner, outer):
    even = is_even(GY)
    low, high = field.shape[0] - FINE_RIM, grad.shape[0] - COARSE_RIM

    def write(heads, tails):
        slab(heads, slab(heads, 0, field[:FINE_RIM]), grad[:COARSE_RIM])
        slab(tails, slab(tails, 0, field[low:]), grad[high:])

    pl.when(even)(lambda: write(outer, inner))
    pl.when(jnp.logical_not(even))(lambda: write(inner, outer))
    first = jnp.zeros((8, LANES), jnp.float32)
    second = jnp.zeros((8, LANES), jnp.float32)
    for at in range(0, field.shape[0], 8):
        v = field[at : at + 8].astype(jnp.float32).reshape(-1, 8, LANES)
        first = first + jnp.sum(v, axis=0)
        second = second + jnp.sum(v * v, axis=0)
    spread(
        copies, [jnp.sum(first, axis=0, keepdims=True), jnp.sum(second, axis=0, keepdims=True)]
    )


def relay(received, copies):
    sums = jnp.sum(received[...], axis=0)
    for k in range(copies.shape[1]):
        copies[:, k, :] = jnp.broadcast_to(sums[k : k + 1], (copies.shape[0], LANES))


def fine_forward(count, rows, cols, place, x, sums, gain, weight, projection,
                 center, pooled, coarse, copies, stats, hidden, block):
    tot = jnp.sum(sums[...], axis=0)
    average, inverse = moments(tot[0:1], tot[1:2], count, LANES // GROUPS)
    stats[0] = average
    stats[1] = inverse
    average, scale = average[0:1], inverse[0:1] * gain[...]
    lines = x.shape[0]
    step = 10
    for at in range(0, lines, step):
        v = x[at : at + step].astype(jnp.float32)
        act = (v - average) * scale
        h = act * sigmoid(act)
        keep = in_grid(
            h.shape, at - FINE_RIM + place[0], place[1], FINE_RIM, rows, cols
        )
        h = jnp.where(keep, h, 0.0)
        hidden[at : at + step, :, 0:LANES] = pltpu.roll(h, 1, 1).astype(jnp.bfloat16)
        hidden[at : at + step, :, LANES : 2 * LANES] = h.astype(jnp.bfloat16)
        center[at : at + step] = h.astype(jnp.bfloat16)
        hidden[at : at + step, :, 2 * LANES :] = pltpu.roll(h, PITCH - 1, 1).astype(jnp.bfloat16)
    step = (lines - 2) // 4
    for at in range(0, lines - 2, step):
        acc = x[at + 1 : at + 1 + step].astype(jnp.float32).reshape(step * PITCH, LANES)
        conv = jnp.zeros_like(acc)
        for tap in range(3):
            conv = conv + jnp.dot(
                hidden[at + tap : at + tap + step].reshape(step * PITCH, 3 * LANES),
                weight[tap],
                preferred_element_type=jnp.float32,
            )
        block[at * PITCH : (at + step) * PITCH] = (
            (acc + conv).astype(jnp.bfloat16).astype(jnp.float32)
        )
    half = PITCH // 2
    step = (lines - 2) // 4
    first = jnp.zeros((1, coarse.shape[1]), jnp.float32)
    second = jnp.zeros((1, coarse.shape[1]), jnp.float32)
    for at in range(0, (lines - 2) // 2, step):
        size = 2 * step * half
        pair = block[pl.ds(2 * at * PITCH, size, stride=2), :] + block[
            pl.ds(2 * at * PITCH + 1, size, stride=2), :
        ]
        mean = 0.25 * jnp.sum(pair.reshape(step, 2, half, LANES), axis=1)
        mean = mean.reshape(step * half, LANES).astype(jnp.bfloat16)
        pooled[at * half : (at + step) * half] = mean
        cells = jnp.dot(mean, projection[...], preferred_element_type=jnp.float32).astype(
            jnp.bfloat16
        )
        coarse[at * half : (at + step) * half] = cells
        own = cells.astype(jnp.float32).reshape(step, half, -1)[:, : half // 2]
        low = 1 if at == 0 else 0
        high = step - 1 if at + step == (lines - 2) // 2 else step
        own = own[low:high]
        first = first + over_cells(own)
        second = second + over_cells(own * own)
    spread(copies, [first[:, :LANES], first[:, LANES:], second[:, :LANES], second[:, LANES:]])


def coarse_transpose(grad, weight, fine_weight, out, fine_out, shifted):
    for tap in range(9):
        block = fine_weight[tap].astype(jnp.float32).T.astype(jnp.bfloat16)
        fine_out[tap // 3, tap % 3 * LANES : (tap % 3 + 1) * LANES] = block
    half = PITCH // 2
    lines = grad.shape[0]
    step = lines // 4
    for at in range(0, lines, step):
        g = grad[at : at + step].astype(jnp.float32)
        shifted[0, at : at + step] = pltpu.roll(g, half - 1, 1).astype(jnp.bfloat16)
        shifted[1, at : at + step] = grad[at : at + step]
        shifted[2, at : at + step] = pltpu.roll(g, 1, 1).astype(jnp.bfloat16)
    step = (lines - 2) // 2
    for at in range(0, lines - 2, step):
        acc = jnp.zeros((step * half, weight.shape[2]), jnp.float32)
        for row_tap in range(3):
            for col_tap in range(3):
                begin = at + 2 - row_tap
                acc = acc + lax.dot_general(
                    shifted[col_tap, begin : begin + step].reshape(step * half, -1),
                    weight[row_tap, col_tap],
                    (((1,), (1,)), ((), ())),
                    preferred_element_type=jnp.float32,
                )
        out[at * half : (at + step) * half] = acc


def coarse_middle(count, rows, cols, place, sums, coarse, pre, gain,
                  hidden, dnorm, copies, stats):
    tot = jnp.sum(sums[...], axis=0)
    average, inverse = moments(
        jnp.concatenate([tot[0:1], tot[1:2]], axis=1),
        jnp.concatenate([tot[2:3], tot[3:4]], axis=1),
        count,
        2 * LANES // GROUPS,
    )
    stats[0] = average
    stats[1] = inverse
    average, inverse = average[0:1], inverse[0:1]
    half = PITCH // 2
    lines = coarse.shape[0] // half
    channels = coarse.shape[1]
    step = lines // 2
    first = jnp.zeros((1, channels), jnp.float32)
    second = jnp.zeros((1, channels), jnp.float32)
    for at in range(0, lines, step):
        span = slice(at * half, (at + step) * half)
        normed = (coarse[span].astype(jnp.float32) - average) * inverse
        act = normed * gain[...]
        sigma = sigmoid(act)
        h = (act * sigma).reshape(step, half, channels)
        h = jnp.where(
            in_grid(h.shape, at - 1 + place[2], place[3], COARSE_RIM, rows, cols), h, 0.0
        )
        hidden[at : at + step] = h.astype(jnp.bfloat16)
        dact = pre[span] * (sigma * (1.0 + act * (1.0 - sigma)))
        dn = dact * gain[...]
        dnorm[span] = dn
        low = 1 if at == 0 else 0
        high = step - 1 if at + step == lines else step
        own = slice(low, high), slice(0, half // 2)
        first = first + over_cells(dn.reshape(step, half, channels)[own])
        second = second + over_cells((dact * normed).reshape(step, half, channels)[own])
    spread(copies, [first[:, :LANES], first[:, LANES:], second[:, :LANES], second[:, LANES:]])


def by_core(write, keep, send):
    core = lax.axis_index(CORE)
    pl.when(core == 0)(lambda: write(keep, send))
    pl.when(core == 1)(lambda: write(send, keep))


def coarse_rest(center, coarse, grad, weight, out, keep, send, hidden, halves):
    half = PITCH // 2
    height = out.shape[0]
    channels = out.shape[2]
    step = center.shape[0] // 2
    for at in range(0, center.shape[0], step):
        h = center[at : at + step].astype(jnp.float32)
        hidden[at : at + step, :, 0:channels] = pltpu.roll(h, 1, 1).astype(jnp.bfloat16)
        hidden[at : at + step, :, channels : 2 * channels] = center[at : at + step]
        hidden[at : at + step, :, 2 * channels :] = pltpu.roll(h, half - 1, 1).astype(jnp.bfloat16)
    step = height // 2
    for at in range(0, height, step):
        acc = coarse[(at + 1) * half : (at + 1 + step) * half].astype(jnp.float32)
        conv = jnp.zeros_like(acc)
        for tap in range(3):
            conv = conv + jnp.dot(
                hidden[at + tap : at + tap + step].reshape(step * half, 3 * channels),
                weight[tap],
                preferred_element_type=jnp.float32,
            )
        out[at : at + step] = (acc + conv).reshape(step, half, channels)[:, : half // 2].astype(
            jnp.bfloat16
        )
    g = grad[2 : 2 + height].astype(jnp.float32)
    own = lax.broadcasted_iota(jnp.int32, g.shape, 1) < half // 2
    g = jnp.where(own, g, 0.0).astype(jnp.bfloat16).reshape(height * half, channels)
    for tap in range(3):
        k = lax.dot_general(
            hidden[tap : tap + height].reshape(height * half, 3 * channels),
            g,
            (((0,), (0,)), ((), ())),
            preferred_element_type=jnp.float32,
        ).astype(jnp.bfloat16)
        span = slice(tap * 3 * channels, (tap + 1) * 3 * channels)
        halves[0, span] = k[:, :LANES]
        halves[1, span] = k[:, LANES:]

    def write(first, second):
        first[...] = halves[0]
        second[...] = halves[1]

    by_core(write, keep, send)


def fine_backward(coarse_count, rows, cols, place, sums, coarse, pooled, grad, dnorm, stats_c,
                  gain_c, projection, weight_t, x, hidden, stats_f, gain_f,
                  keep, send, gain_c_grad, partial, rows_out, up, shifted, taps):
    tot = jnp.sum(sums[...], axis=0)
    first = jnp.concatenate([tot[0:1], tot[1:2]], axis=1)
    second = jnp.concatenate([tot[2:3], tot[3:4]], axis=1)
    gain_c_grad[...] = second
    size = 2 * LANES // GROUPS
    a_sum = group_sum(wide(first), size)[0:1] / coarse_count
    b_sum = group_sum(wide(second * gain_c[...]), size)[0:1] / coarse_count
    average, inverse = stats_c[0, 0:1], stats_c[1, 0:1]
    half = PITCH // 2
    lines = coarse.shape[0] // half
    channels = coarse.shape[1]
    height = 2 * (lines - 2)
    step = lines // 2
    proj_grad = jnp.zeros((LANES, channels), jnp.float32)
    for at in range(0, lines, step):
        span = slice(at * half, (at + step) * half)
        normed = (coarse[span].astype(jnp.float32) - average) * inverse
        g = grad[at + 1 : at + 1 + step].astype(jnp.float32).reshape(step * half, channels)
        d = g + inverse * (dnorm[span] - a_sum - normed * b_sum)
        d = d.reshape(step, half, channels)
        d = jnp.where(
            in_grid(d.shape, at - 1 + place[2], place[3], COARSE_RIM, rows, cols), d, 0.0
        )
        line = lax.broadcasted_iota(jnp.int32, d.shape, 0) + at
        spot = lax.broadcasted_iota(jnp.int32, d.shape, 1)
        own = (line >= 1) & (line < lines - 1) & (spot < half // 2)
        own = jnp.where(own, d, 0.0).astype(jnp.bfloat16).reshape(step * half, channels)
        d = d.astype(jnp.bfloat16).reshape(step * half, channels)
        proj_grad = proj_grad + lax.dot_general(
            pooled[span], own, (((0,), (0,)), ((), ())), preferred_element_type=jnp.float32
        )
        small = lax.dot_general(
            d, projection[...], (((1,), (1,)), ((), ())), preferred_element_type=jnp.float32
        )
        small = (small * 0.25).astype(jnp.bfloat16).astype(jnp.float32)
        up[pl.ds(at * PITCH, step * half, stride=2), :] = small
        up[pl.ds(at * PITCH + 1, step * half, stride=2), :] = small
    for at in range(0, lines, step):
        u = up[at * PITCH : (at + step) * PITCH].reshape(step, PITCH, LANES)
        shifted[at : at + step, :, 0:LANES] = pltpu.roll(u, PITCH - 1, 1).astype(jnp.bfloat16)
        shifted[at : at + step, :, LANES : 2 * LANES] = u.astype(jnp.bfloat16)
        shifted[at : at + step, :, 2 * LANES :] = pltpu.roll(u, 1, 1).astype(jnp.bfloat16)
    width = PITCH // 2
    for tap in range(3):
        for at in range(0, lines, step):
            y = jnp.dot(
                shifted[at : at + step, 0:width, :].reshape(step * width, 3 * LANES),
                weight_t[tap],
                preferred_element_type=jnp.float32,
            )
            taps[tap, at : at + step] = y.reshape(step, width, LANES)
    average, inverse = stats_f[0, 0:1], stats_f[1, 0:1]
    first = jnp.zeros((1, LANES), jnp.float32)
    second = jnp.zeros((1, LANES), jnp.float32)
    step = 8
    for at in range(0, lines - 2, step):
        even = taps[0, at + 1 : at + 1 + step] + taps[1, at + 1 : at + 1 + step] + taps[
            2, at : at + step
        ]
        odd = taps[0, at + 2 : at + 2 + step] + taps[1, at + 1 : at + 1 + step] + taps[
            2, at + 1 : at + 1 + step
        ]
        both = jnp.stack([even, odd], axis=1).reshape(2 * step, width, LANES)
        begin = FINE_RIM + 2 * at
        v = x[begin : begin + 2 * step, 0:width, :].astype(jnp.float32)
        normed = (v - average) * inverse
        act = normed * gain_f[...]
        sigma = sigmoid(act)
        dact = both * (sigma * (1.0 + act * (1.0 - sigma)))
        dn = dact * gain_f[...]
        first = first + over_cells(dn)
        second = second + over_cells(dact * normed)
        u = up[(at + 1) * PITCH : (at + 1 + step) * PITCH].reshape(step, PITCH, LANES)[:, 0:width]
        u = jnp.broadcast_to(u[:, None], (step, 2, width, LANES)).reshape(2 * step, width, LANES)
        partial[2 * at : 2 * at + 2 * step] = u + inverse * dn
    for at in range(1, lines - 1, step):
        u = up[at * PITCH : (at + step) * PITCH].reshape(step, PITCH, LANES)
        own = lax.broadcasted_iota(jnp.int32, u.shape, 1) < width
        u = jnp.where(own, u, 0.0)
        shifted[at : at + step, :, 0:LANES] = pltpu.roll(u, PITCH - 1, 1).astype(jnp.bfloat16)
        shifted[at : at + step, :, LANES : 2 * LANES] = u.astype(jnp.bfloat16)
        shifted[at : at + step, :, 2 * LANES :] = pltpu.roll(u, 1, 1).astype(jnp.bfloat16)
    d = shifted[1 : lines - 1]
    d = jnp.broadcast_to(d[:, None], (lines - 2, 2) + d.shape[1:])
    d = d.reshape(height * PITCH, 3 * LANES)
    at = 0
    for tap in range(3):
        begin = FINE_RIM - 1 + tap
        k = lax.dot_general(
            hidden[begin : begin + height].reshape(height * PITCH, LANES),
            d,
            (((0,), (0,)), ((), ())),
            preferred_element_type=jnp.float32,
        ).astype(jnp.bfloat16)
        for col_tap in range(3):
            rows_out[at : at + LANES] = k[:, col_tap * LANES : (col_tap + 1) * LANES]
            at += LANES
    proj_grad = proj_grad.astype(jnp.bfloat16)
    rows_out[at : at + LANES] = proj_grad[:, :LANES]
    rows_out[at + LANES : at + 2 * LANES] = proj_grad[:, LANES:]
    at += 2 * LANES
    spare = rows_out.shape[0] - at
    small = jnp.concatenate([first, second], axis=0)
    rows_out[at:] = jnp.concatenate(
        [jnp.zeros((spare - 8, LANES), jnp.float32), split(small)], axis=0
    ).astype(jnp.bfloat16)
    half = keep.shape[0]

    def write(first, second):
        first[...] = rows_out[:half]
        second[...] = rows_out[half:]

    by_core(write, keep, send)


def spread_rows(low, high, at, out, lane):
    half, count = low.shape[0], out.shape[0]
    split_at = min(max(half - at, 0), count)
    lanes = slice(lane, lane + LANES)
    if split_at > 0:
        out[:split_at, lanes] = low[at : at + split_at].astype(jnp.float32)
    if split_at < count:
        begin = at + split_at - half
        out[split_at:, lanes] = high[begin : begin + count - split_at].astype(jnp.float32)
    return at + count


def finish(fine_count, own, other, partial, x, stats, gain,
           field_grad, weight_f, gain_f, proj, weight_c):
    core = lax.axis_index(CORE)
    last = own.shape[0] - 8
    small = jnp.where(
        core == 1, own[last:].astype(jnp.float32), other[last:].astype(jnp.float32)
    )
    small = small[0:2] + small[2:4] + small[4:6]
    first, second = small[0:1], small[1:2]
    gain_f[...] = second
    size = LANES // GROUPS
    a_sum = group_sum(wide(first), size)[0:1] / fine_count
    b_sum = group_sum(wide(second * gain[...]), size)[0:1] / fine_count
    average, inverse = stats[0, 0:1], stats[1, 0:1]
    height, width, _ = partial.shape
    step = 16
    for at in range(0, height, step):
        v = x[FINE_RIM + at : FINE_RIM + at + step, 0:width, :].astype(jnp.float32)
        normed = (v - average) * inverse
        field_grad[at : at + step] = (
            partial[at : at + step] - inverse * (a_sum + normed * b_sum)
        ).astype(jnp.bfloat16)

    def weights(low, high):
        tall = weight_c.shape[0]
        weight_c[:, :LANES] = low[:tall].astype(jnp.float32)
        weight_c[:, LANES:] = high[:tall].astype(jnp.float32)
        low, high = low.at[tall:], high.at[tall:]
        at = spread_rows(low, high, 0, weight_f, 0)
        at = spread_rows(low, high, at, proj, 0)
        spread_rows(low, high, at, proj, LANES)

    pl.when(core == 0)(lambda: weights(own, other))
    pl.when(core == 1)(lambda: weights(other, own))


def gathered(copies, late=None):
    far = lax.axis_size(FAR)
    received = lax.all_to_all(copies, NEAR, 0, 0, tiled=True)
    (copies,) = call(relay, [((far,) + copies.shape[1:], jnp.float32, None)], received)
    if late is not None:
        copies, late = lax.optimization_barrier((copies, late))
    sums = lax.all_to_all(copies, FAR, 0, 0, tiled=True)
    return sums if late is None else (sums, late)


def split(small):
    high = small.astype(jnp.bfloat16).astype(jnp.float32)
    middle = (small - high).astype(jnp.bfloat16).astype(jnp.float32)
    low = small - high - middle
    return jnp.concatenate([high, middle, low, jnp.zeros_like(low)], axis=0)


def kept_split(sums, held):
    last = sums[sums.shape[0] - 8 :]
    tail = split(last[0:2] + last[2:4] + last[4:6])
    return jnp.concatenate([sums[: sums.shape[0] - 8], jnp.where(held == 1, tail, last)], axis=0)


def add_cores(place, early, early_got, late, late_got, out):
    for k, g, base in ((early, early_got, 0), (late, late_got, early.shape[0])):
        rows = k.shape[0]
        step = rows // 3
        for at in range(0, rows, step):
            sums = k[at : at + step].astype(jnp.float32) + g[at : at + step].astype(jnp.float32)
            if base > 0 and at + step == rows:
                sums = kept_split(sums, place[4])
            out[base + at : base + at + step] = sums.astype(jnp.bfloat16)


def add_up(stage, place, *refs):
    pieces = [refs[0].at[k] for k in range(refs[0].shape[0])]
    out, scratch = refs[1], refs[2:]
    rows = pieces[0].shape[0]
    step = 256 if rows % 256 == 0 else rows
    pitch = out.shape[-2]
    for at in range(0, rows, step):
        sums = pieces[0][at : at + step].astype(jnp.float32)
        for piece in pieces[1:]:
            sums = sums + piece[at : at + step].astype(jnp.float32)
        if at + step == rows:
            sums = kept_split(sums, place[4 + stage])
        if scratch:
            scratch[0][at : at + step] = sums
        elif len(out.shape) == 3:
            for k in range(out.shape[0]):
                out[k] = sums.astype(jnp.bfloat16)
        else:
            out[at : at + step] = sums.astype(jnp.bfloat16)
    if scratch:
        for k in range(out.shape[0]):
            out[k] = scratch[0][k * pitch : (k + 1) * pitch].astype(jnp.bfloat16)


def traded(rows):
    return lax.ppermute(rows, CORE, [(0, 1), (1, 0)])


def gradient_totals(halves, place):
    rows = halves[0].shape[0] + halves[2].shape[0]
    (part,) = call(add_cores, [((rows, LANES), jnp.bfloat16, None)], place, *halves)
    for stage, axes in list(enumerate(STAGES))[1:]:
        count = lax.axis_size(axes)
        pieces = lax.all_to_all(part.reshape(count, -1, LANES), axes, 0, 0, tiled=True)
        rows = pieces.shape[1]
        kernel = functools.partial(add_up, stage)
        if stage == 1:
            pitch = rows // lax.axis_size(STAGES[2])
            (part,) = call(
                kernel,
                [((rows // pitch, pitch, LANES), jnp.bfloat16, None)],
                place,
                pieces,
                scratch=[((rows, LANES), jnp.float32)],
            )
        else:
            (part,) = call(kernel, [((count, rows, LANES), jnp.bfloat16, None)], place, pieces)
    part = lax.all_to_all(part, STAGES[2], 0, 0, tiled=True).reshape(-1, LANES)
    count = lax.axis_size(STAGES[1])
    copies = jnp.broadcast_to(part[None], (count,) + part.shape)
    part = lax.all_to_all(copies, STAGES[1], 0, 0, tiled=True).reshape(-1, LANES)
    return part, traded(part)


def on_device(field, cotangent, gain_fine, weight_fine, projection, gain_coarse, weight_coarse):
    height, width, chan_fine = field.shape
    chan_coarse = projection.shape[1]
    half_h, half_w = (height // 2, width // 2)
    cells_all = height * width * lax.axis_size(GY_GX)
    fine_count = cells_all * (chan_fine // GROUPS)
    coarse_count = cells_all // 4 * (chan_coarse // GROUPS)
    rows, cols = height * lax.axis_size(GY), width * lax.axis_size(GX)
    f32, bf16 = jnp.float32, jnp.bfloat16
    near = lax.axis_size(NEAR)
    row, col = lax.axis_index(GY), lax.axis_index(GX)
    holds, held = [], jnp.int32(1)
    for axes in STAGES:
        held = held * (lax.axis_index(axes) == lax.axis_size(axes) - 1)
        holds.append(held)
    place = jnp.stack([row * height, col * width, row * half_h, col * half_w] + holds)
    place = place.astype(jnp.int32)
    gain_f, gain_c = gain_fine.reshape(1, -1), gain_coarse.reshape(1, -1)

    slabs = FINE_RIM * width + COARSE_RIM * half_w * chan_coarse // LANES
    copies, inner, outer = call(
        field_sums,
        [((near, 2, LANES), f32, None), ((slabs, LANES), bf16, None), ((slabs, LANES), bf16, None)],
        field,
        cotangent,
        plain=(0, 1),
    )
    sums = gathered(copies)
    x, (tall, rims, shapes) = with_rims(field, cotangent, inner, outer)
    lines = half_h + 2
    cells = lines * PITCH // 2
    hidden_f, pooled, coarse, copies, stats_f = call(
        functools.partial(fine_forward, fine_count, rows, cols),
        [
            (x.shape, bf16, HBM),
            ((cells, chan_fine), bf16, HBM),
            ((cells, chan_coarse), bf16),
            ((near, 4, LANES), f32, None),
            ((2, 8, chan_fine), f32),
        ],
        place,
        x,
        sums,
        gain_f,
        weight_fine.reshape(3, 3 * chan_fine, chan_fine),
        projection,
        scratch=[
            (x.shape[:2] + (3 * chan_fine,), bf16),
            ((2 * lines * PITCH + 8, chan_fine), f32),
        ],
    )
    sums, (tall, rims) = gathered(copies, (tall, rims))
    grad = coarse_ring(tall, rims, shapes)
    pre, weight_t = call(
        coarse_transpose,
        [((cells, chan_coarse), f32), ((3, 3 * chan_fine, chan_fine), bf16, HBM)],
        grad,
        weight_coarse,
        weight_fine.reshape(9, chan_fine, chan_fine),
        plain=(1, 2),
        scratch=[((3,) + grad.shape, bf16)],
    )
    hidden_c, dnorm, copies, stats_c = call(
        functools.partial(coarse_middle, coarse_count, rows // 2, cols // 2),
        [
            ((lines, PITCH // 2, chan_coarse), bf16, HBM),
            ((cells, chan_coarse), f32, HBM),
            ((near, 4, LANES), f32, None),
            ((2, 8, chan_coarse), f32),
        ],
        place,
        sums,
        coarse,
        pre,
        gain_c,
    )
    sums, weight_late = gathered(copies, weight_coarse)
    used = 18 * chan_coarse + 9 * chan_fine + chan_coarse
    used += -(used + 8) % (4 * lax.axis_size(GY_GX)) + 8
    coarse_output, keep_c, send_c = call(
        coarse_rest,
        [((half_h, half_w, chan_coarse), bf16, None), ((9 * chan_coarse, LANES), bf16), ((9 * chan_coarse, LANES), bf16, None)],
        hidden_c,
        coarse,
        grad,
        weight_late.reshape(3, 3 * chan_coarse, chan_coarse),
        scratch=[
            ((lines, PITCH // 2, 3 * chan_coarse), bf16),
            ((2, 9 * chan_coarse, LANES), bf16),
        ],
        plain=(0, 3),
    )
    got_c = traded(send_c)
    late = used - 18 * chan_coarse
    keep_l, send_l, coarse_gain_grad, partial = call(
        functools.partial(fine_backward, coarse_count, rows // 2, cols // 2),
        [
            ((late // 2, LANES), bf16),
            ((late // 2, LANES), bf16, None),
            ((1, chan_coarse), f32, None),
            ((height, width, chan_fine), f32),
        ],
        place,
        sums,
        coarse,
        pooled,
        grad,
        dnorm,
        stats_c,
        gain_c,
        projection,
        weight_t,
        x,
        hidden_f,
        stats_f,
        gain_f,
        scratch=[
            ((late, LANES), bf16),
            ((lines * PITCH + 8, chan_fine), f32),
            ((lines, PITCH, 3 * chan_fine), bf16),
            ((3, lines, PITCH // 2, chan_fine), f32),
        ],
        plain=(3, 5, 8, 9, 11),
    )
    own, other = gradient_totals((keep_c, got_c, keep_l, traded(send_l)), place)
    field_grad, fine_weight_grad, fine_gain_grad, projection_grad, coarse_weight_grad = call(
        functools.partial(finish, fine_count),
        [
            ((height, width, chan_fine), bf16, None),
            ((9 * chan_fine, chan_fine), f32, None),
            ((1, chan_fine), f32, None),
            ((chan_fine, chan_coarse), f32, None),
            ((9 * chan_coarse, chan_coarse), f32, None),
        ],
        own,
        other,
        partial,
        x,
        stats_f,
        gain_f,
    )
    return (
        coarse_output,
        field_grad,
        fine_weight_grad.reshape(weight_fine.shape),
        fine_gain_grad.reshape(-1),
        projection_grad,
        coarse_weight_grad.reshape(weight_coarse.shape),
        coarse_gain_grad.reshape(-1),
    )


def solution(mesh):
    finer = Mesh(mesh.devices.reshape(2, 8, 2, 4, 2, 2), GY_GX)
    in_specs = (P(GY, GX, None), P(GY, GX, None), P(), P(), P(), P(), P())
    out_specs = (P(GY, GX, None), P(GY, GX, None), P(), P(), P(), P(), P())

    return jax.shard_map(
        on_device, mesh=finer, in_specs=in_specs, out_specs=out_specs, check_vma=False
    )
```
